32 devices in a mesh: dp: 4 (over y, core), lat: 8 (over z, x).
Axes of the slice: x: 2, y: 2, z: 4, core: 2. Of those that a mesh axis runs over, the one named last changes fastest.
Arguments:
- tokens: bfloat16 [2, 4, 8, 180, 768], P(None, 'dp', 'lat'), may hold values from -6 to 6
- boxes: int32 [2, 4, 2], P(None, 'dp'), may hold values from 4 to 180, as said below
- patch_mask: int32 [2, 4, 8, 180], P(None, 'dp', 'lat'), may hold values 0 or 1
- pre_gain: float32 [768], replicated, may hold values from 0.25 to 1.75
- pre_shift: float32 [768], replicated, may hold values from -3 to 3
- filter_inner: bfloat16 [2, 8, 96, 96], replicated, may hold values from -0.4375 to 0.4375
- filter_inner_bias: float32 [2, 8, 96], replicated, may hold values from -3 to 3
- filter_outer: bfloat16 [2, 8, 96, 96], replicated, may hold values from -0.4375 to 0.4375
- filter_outer_bias: float32 [2, 8, 96], replicated, may hold values from -3 to 3
- post_gain: float32 [768], replicated, may hold values from 0.25 to 1.75
- post_shift: float32 [768], replicated, may hold values from -3 to 3
- expand_weight: bfloat16 [768, 3072], replicated, may hold values from -0.21875 to 0.21875
- expand_bias: float32 [3072], replicated, may hold values from -3 to 3
- reduce_weight: bfloat16 [3072, 768], replicated, may hold values from -0.109375 to 0.109375
- reduce_bias: float32 [768], replicated, may hold values from -3 to 3
- cotangent: bfloat16 [2, 4, 8, 180, 768], P(None, 'dp', 'lat'), may hold values from -6 to 6
Outputs:
- block_out: bfloat16 [2, 4, 8, 180, 768], P(None, 'dp', 'lat')
- grad_tokens: float32 [2, 4, 8, 180, 768], P(None, 'dp', 'lat')
- grad_pre_gain: float32 [768], replicated
- grad_pre_shift: float32 [768], replicated
- grad_filter_inner: float32 [2, 8, 96, 96], replicated
- grad_filter_inner_bias: float32 [2, 8, 96], replicated
- grad_filter_outer: float32 [2, 8, 96, 96], replicated
- grad_filter_outer_bias: float32 [2, 8, 96], replicated
- grad_post_gain: float32 [768], replicated
- grad_post_shift: float32 [768], replicated
- grad_expand_weight: float32 [768, 3072], P(None, ('dp', 'lat'))
- grad_expand_bias: float32 [3072], replicated
- grad_reduce_weight: float32 [3072, 768], P(('dp', 'lat'))
- grad_reduce_bias: float32 [768], replicated
The draws below stay inside these ranges and needn't reach their ends.
Inputs may be any that keep to these rules, and one draw needn't show every extreme that they name: boxes[m,c,0] lies between 4 and 8, boxes[m,c,1] between 90 and 180. For each crop index c, at least one of the 2 micro-batches m has boxes[m,c] equal to the full box of 8 rows and 180 columns.
All inputs are finite; a program needn't handle non-finite values. No bound on the sum of `patch_mask` on one device may be relied on, other than what follows from the above.
Results may differ from the reference program's by a relative error of at most 0.013.
The reference program's roundings to bfloat16 on the way count: a program that leaves them out, or rounds other values in their place, can miss the bound.
Values may be sent and summed in bfloat16 or wider, within the bound.
No kernel may reach another device: no remote copies, remote signals or barrier semaphores. Data moves between devices by JAX's collectives and lax.ppermute only.
A program may use at most 192 MiB of HBM per device.

```python
import math
import jax
import jax.numpy as jnp
from jax import lax

D = 768
FF = 3072
NBLK = 8
BS = 96
LONS = 180
MODES = 64
LATS = 8
CROP_DEV = 1
CROPS = 4
MICRO = 2


def draw_boxes(key, part):
    key_height, key_width, key_chosen = jax.random.split(key, 3)
    heights = jax.random.randint(key_height, (MICRO, CROPS), LATS // 2, LATS + 1)
    widths = jax.random.randint(key_width, (MICRO, CROPS), LONS // 2, LONS + 1)
    groups = CROPS // CROP_DEV
    chosen = jax.random.randint(key_chosen, (groups,), 0, MICRO * CROP_DEV)
    crop_index = jnp.arange(CROPS, dtype=jnp.int32)
    slot_index = jnp.arange(MICRO, dtype=jnp.int32)[:, None] * CROP_DEV + (crop_index % CROP_DEV)[None, :]
    owner_group = crop_index // CROP_DEV
    full_box = slot_index == chosen[owner_group][None, :]
    heights = jnp.where(full_box, LATS, heights)
    widths = jnp.where(full_box, LONS, widths)
    return jnp.stack([heights, widths], axis=-1).astype(jnp.int32)


def plant(values, stream_key, smallest, high):
    index_at = [jax.random.randint(jax.random.fold_in(stream_key, axis), (), 0, length) for axis, length in enumerate(values.shape)]
    widest = values.shape.index(max(values.shape))
    next_to = index_at[:widest] + [(index_at[widest] + 1) % values.shape[widest]] + index_at[widest + 1:]
    return values.at[tuple(index_at)].set(smallest).at[tuple(next_to)].set(high)


def levels(own_key, shape, cuts, smallest, top_value):
    level, own = 1.0, jax.random.fold_in(own_key, 6)
    for axis_at, shards_of in cuts:
        draws = jnp.exp(jax.random.uniform(jax.random.fold_in(own, axis_at), (shards_of,), jnp.float32, smallest / len(cuts), top_value / len(cuts)))
        level = level * jnp.repeat(draws, shape[axis_at] // shards_of).reshape([-1 if axis == axis_at else 1 for axis in range(len(shape))])
    return level


def centred(own_key, shape, scale, limit, pieces=(), kind=jnp.bfloat16):
    array = jax.random.normal(own_key, shape, jnp.float32) * scale
    if len(pieces) > 0:
        array = levels(own_key, shape, pieces, -0.22, 0.18) * array
    return jnp.clip(array, min=-limit, max=limit).astype(kind)


def setup_inputs(seed: int = 0) -> dict:
    seeds = jax.random.split(jax.random.key(seed), 17)
    tokens = centred(seeds[0], (MICRO, CROPS, LATS, LONS, D), 1.0, 6.0, ((1, 4), (2, 8)))
    boxes = draw_boxes(jax.random.fold_in(seeds[16], 71), 0)
    patch_mask = plant((jax.random.randint(seeds[2], (MICRO, CROPS, LATS, LONS), 0, 8) < 7).astype(jnp.int32), jax.random.fold_in(seeds[2], 1), 0, 1)
    pre_gain = jnp.clip(1.0 + 0.15 * jax.random.normal(seeds[3], (D,), jnp.float32), 0.25, 1.75)
    pre_shift = centred(seeds[4], (D,), 0.3, 3.0, (), jnp.float32)
    filter_inner = centred(seeds[5], (2, NBLK, BS, BS), (2 * BS) ** -0.5, 0.4375)
    filter_inner_bias = centred(seeds[6], (2, NBLK, BS), 0.3, 3.0, (), jnp.float32)
    filter_outer = centred(seeds[7], (2, NBLK, BS, BS), (2 * BS) ** -0.5, 0.4375)
    filter_outer_bias = centred(seeds[8], (2, NBLK, BS), 0.3, 3.0, (), jnp.float32)
    post_gain = jnp.clip(1.0 + 0.15 * jax.random.normal(seeds[9], (D,), jnp.float32), 0.25, 1.75)
    post_shift = centred(seeds[10], (D,), 0.3, 3.0, (), jnp.float32)
    expand_weight = centred(seeds[11], (D, FF), D ** -0.5, 0.21875)
    expand_bias = centred(seeds[12], (FF,), 0.3, 3.0, (), jnp.float32)
    reduce_weight = centred(seeds[13], (FF, D), FF ** -0.5, 0.109375)
    reduce_bias = centred(seeds[14], (D,), 0.3, 3.0, (), jnp.float32)
    cotangent = centred(seeds[15], (MICRO, CROPS, LATS, LONS, D), 1.0, 6.0, ((1, 4), (2, 8)))
    return dict(tokens=tokens, boxes=boxes, patch_mask=patch_mask, pre_gain=pre_gain, pre_shift=pre_shift, filter_inner=filter_inner, filter_inner_bias=filter_inner_bias, filter_outer=filter_outer, filter_outer_bias=filter_outer_bias, post_gain=post_gain, post_shift=post_shift, expand_weight=expand_weight, expand_bias=expand_bias, reduce_weight=reduce_weight, reduce_bias=reduce_bias, cotangent=cotangent)


shrink_level = 0.01
epsilon = 1e-05
highest = lax.Precision.HIGHEST

@jax.custom_vjp
def low(v):
    return lax.optimization_barrier(v.astype(jnp.bfloat16)).astype(jnp.float32)

@jax.custom_vjp
def low_back(v):
    return v

def low_keep(v):
    return (low(v), None)

def low_pass(kept, grad):
    return (grad,)

def back_keep(v):
    return (v, None)

def back_low(kept, grad):
    return (low(grad),)
low.defvjp(low_keep, low_pass)
low_back.defvjp(back_keep, back_low)

def table_pair(out_index, in_index, length):
    phase = out_index[:, None] * in_index[None, :] % length
    angle = phase.astype(jnp.float32) * (2.0 * math.pi / length)
    return (jnp.cos(angle), jnp.sin(angle))

def make_tables():
    lon_index = jnp.arange(LONS, dtype=jnp.int32)
    mode_index = jnp.arange(MODES, dtype=jnp.int32)
    lat_index = jnp.arange(LATS, dtype=jnp.int32)
    lon_factor = 1.0 / math.sqrt(LONS)
    lat_factor = 1.0 / math.sqrt(LATS)
    cos_fwd, sin_fwd = table_pair(lon_index, mode_index, LONS)
    cos_lat, sin_lat = table_pair(lat_index, lat_index, LATS)
    cos_inv, sin_inv = table_pair(mode_index, lon_index, LONS)
    mode_weight = jnp.where(mode_index == 0, 1.0, 2.0).astype(jnp.float32)
    return (low(cos_fwd * lon_factor), low(sin_fwd * lon_factor), low(cos_lat * lat_factor), low(sin_lat * lat_factor), low(cos_inv * mode_weight[:, None] * lon_factor), low(sin_inv * mode_weight[:, None] * lon_factor))

def layer_norm(values, gain, shift):
    row_mean = lax.optimization_barrier(jnp.mean(values, axis=-1, keepdims=True))
    centered = values - row_mean
    variance = lax.optimization_barrier(jnp.mean(centered * centered, axis=-1, keepdims=True))
    return centered * lax.rsqrt(variance + epsilon) * gain + shift

def shrink(values):
    return values - shrink_level * values * lax.rsqrt(values * values + shrink_level * shrink_level)

def block_mix(operand, weight):
    return jnp.einsum('...bi,bio->...bo', operand, weight, precision=highest)

def complex_layer(in_real, in_imag, weight, bias):
    out_real = block_mix(in_real, weight[0]) - block_mix(in_imag, weight[1]) + bias[0]
    out_imag = block_mix(in_imag, weight[0]) + block_mix(in_real, weight[1]) + bias[1]
    return (out_real, out_imag)

def forward(crop_tokens, valid_mask, tables, pre_gain, pre_shift, filter_inner, filter_inner_bias, filter_outer, filter_outer_bias, post_gain, post_shift, expand_weight, expand_bias, reduce_weight, reduce_bias):
    fwd_cos, fwd_sin, lat_cos, lat_sin, inv_cos, inv_sin = tables
    normed = layer_norm(crop_tokens, pre_gain, pre_shift)
    masked = low(valid_mask * normed)
    lon_real = jnp.einsum('rsd,sk->rkd', masked, fwd_cos, precision=highest)
    lon_imag = -jnp.einsum('rsd,sk->rkd', masked, fwd_sin, precision=highest)
    lon_real = low_back(low(lon_real))
    lon_imag = low_back(low(lon_imag))
    lat_real = jnp.einsum('pr,rkd->pkd', lat_cos, lon_real, precision=highest) + jnp.einsum('pr,rkd->pkd', lat_sin, lon_imag, precision=highest)
    lat_imag = jnp.einsum('pr,rkd->pkd', lat_cos, lon_imag, precision=highest) - jnp.einsum('pr,rkd->pkd', lat_sin, lon_real, precision=highest)
    lat_real = low_back(low(lat_real)).reshape(LATS, MODES, NBLK, BS)
    lat_imag = low_back(low(lat_imag)).reshape(LATS, MODES, NBLK, BS)
    pre_real, pre_imag = complex_layer(lat_real, lat_imag, filter_inner, filter_inner_bias)
    pre_real = low_back(pre_real)
    pre_imag = low_back(pre_imag)
    hid_real = low(jax.nn.gelu(pre_real, approximate=False))
    hid_imag = low(jax.nn.gelu(pre_imag, approximate=False))
    mid_real, mid_imag = complex_layer(hid_real, hid_imag, filter_outer, filter_outer_bias)
    mid_real = low_back(mid_real)
    mid_imag = low_back(mid_imag)
    filt_real = low_back(low(shrink(mid_real))).reshape(LATS, MODES, D)
    filt_imag = low_back(low(shrink(mid_imag))).reshape(LATS, MODES, D)
    back_real = jnp.einsum('pr,pkd->rkd', lat_cos, filt_real, precision=highest) - jnp.einsum('pr,pkd->rkd', lat_sin, filt_imag, precision=highest)
    back_imag = jnp.einsum('pr,pkd->rkd', lat_cos, filt_imag, precision=highest) + jnp.einsum('pr,pkd->rkd', lat_sin, filt_real, precision=highest)
    back_real = low_back(low(back_real))
    back_imag = low_back(low(back_imag))
    filtered = jnp.einsum('rkd,ks->rsd', back_real, inv_cos, precision=highest) - jnp.einsum('rkd,ks->rsd', back_imag, inv_sin, precision=highest)
    filtered = low_back(filtered)
    mixed = crop_tokens + normed + valid_mask * filtered
    normed_post = low(layer_norm(mixed, post_gain, post_shift))
    pre_hidden = jnp.einsum('rsd,df->rsf', normed_post, expand_weight, precision=highest) + expand_bias
    pre_hidden = low_back(pre_hidden)
    hidden = low(jax.nn.gelu(pre_hidden, approximate=False))
    return mixed + (jnp.einsum('rsf,fd->rsd', hidden, reduce_weight, precision=highest) + reduce_bias)

def reference(tokens, boxes, patch_mask, pre_gain, pre_shift, filter_inner, filter_inner_bias, filter_outer, filter_outer_bias, post_gain, post_shift, expand_weight, expand_bias, reduce_weight, reduce_bias, cotangent):
    tables = make_tables()
    params = tuple((param.astype(jnp.float32) for param in (pre_gain, pre_shift, filter_inner, filter_inner_bias, filter_outer, filter_outer_bias, post_gain, post_shift, expand_weight, expand_bias, reduce_weight, reduce_bias)))
    crop_total = MICRO * CROPS
    all_tokens = tokens.reshape(crop_total, LATS, LONS, D)
    all_boxes = boxes.reshape(crop_total, 2)
    all_holes = patch_mask.reshape(crop_total, LATS, LONS)
    all_cot = cotangent.reshape(crop_total, LATS, LONS, D)
    row_index = lax.broadcasted_iota(jnp.int32, (LATS, LONS), 0)
    col_index = lax.broadcasted_iota(jnp.int32, (LATS, LONS), 1)

    def one_crop(totals, item):
        crop_tokens, crop_box, crop_holes, crop_cot = item
        valid_mask = (row_index < crop_box[0]) & (col_index < crop_box[1]) & (crop_holes > 0)
        valid_mask = valid_mask.astype(jnp.float32)[..., None]

        def crop_forward(*values):
            return forward(values[0], valid_mask, tables, *values[1:])
        result, pullback = jax.vjp(crop_forward, crop_tokens.astype(jnp.float32), *params)
        grads = pullback(crop_cot.astype(jnp.float32))
        totals = tuple((total + grad for total, grad in zip(totals, grads[1:])))
        return (totals, (result.astype(jnp.bfloat16), grads[0]))
    zeros = tuple((jnp.zeros(param.shape, jnp.float32) for param in params))
    totals, (results, input_grads) = lax.scan(one_crop, zeros, (all_tokens, all_boxes, all_holes, all_cot))
    block_out = results.reshape(MICRO, CROPS, LATS, LONS, D)
    grad_tokens = input_grads.reshape(MICRO, CROPS, LATS, LONS, D)
    return (block_out, grad_tokens, totals[0], totals[1], totals[2], totals[3], totals[4], totals[5], totals[6], totals[7], totals[8], totals[9], totals[10], totals[11])
```

```python
import math

import jax
import jax.numpy as jnp
from jax import lax
from jax.sharding import PartitionSpec as P

MODES = 64
shrink_level = 0.01
epsilon = 1e-05
inv_root_two = 1.0 / math.sqrt(2.0)
inv_root_tau = 1.0 / math.sqrt(2.0 * math.pi)
f32 = jnp.float32
bf16 = jnp.bfloat16


def table_pair(out_index, in_index, length):
    phase = out_index[:, None] * in_index[None, :] % length
    angle = phase.astype(f32) * (2.0 * math.pi / length)
    return (jnp.cos(angle), jnp.sin(angle))


def norm_parts(values):
    row_mean = jnp.mean(values, axis=-1, keepdims=True)
    centered = values - row_mean
    inv_scale = lax.rsqrt(jnp.mean(centered * centered, axis=-1, keepdims=True) + epsilon)
    return (centered * inv_scale, inv_scale)


def norm_back(grad_normed, unit_values, inv_scale, gain):
    grad_unit = grad_normed * gain
    plain_mean = jnp.mean(grad_unit, axis=-1, keepdims=True)
    cross_mean = jnp.mean(grad_unit * unit_values, axis=-1, keepdims=True)
    grad_input = inv_scale * (grad_unit - plain_mean - unit_values * cross_mean)
    width = grad_normed.shape[-1]
    flat_grad = grad_normed.reshape(-1, width)
    flat_unit = unit_values.reshape(-1, width)
    return (grad_input, jnp.sum(flat_grad * flat_unit, axis=0), jnp.sum(flat_grad, axis=0))


def gelu_pair(values):
    half = 0.5 * (1.0 + lax.erf(values * inv_root_two))
    return values * half, half + values * jnp.exp(-0.5 * values * values) * inv_root_tau


def shrink(values):
    return values - shrink_level * values * lax.rsqrt(values * values + shrink_level * shrink_level)


def shrink_slope(values):
    inverse = lax.rsqrt(values * values + shrink_level * shrink_level)
    return 1.0 - shrink_level * shrink_level * shrink_level * inverse * inverse * inverse


def dot(a, b, ca, cb):
    return lax.dot_general(a, b, (((ca,), (cb,)), ((), ())), preferred_element_type=f32)


def pair_swap(operand, axis_name, bit):
    size = lax.axis_size(axis_name)
    return lax.ppermute(operand, axis_name, [(i, i ^ bit) for i in range(size)])


def axis_bits(axis_name):
    size = lax.axis_size(axis_name)
    return [1 << i for i in range(size.bit_length() - 1)]


def all_sum(vector):
    for axis_name in ("dp", "lat"):
        for bit in axis_bits(axis_name):
            vector = vector + pair_swap(vector, axis_name, bit)
    return vector


def halving_scatter(part, order):
    names = [("dp", b) for b in reversed(axis_bits("dp"))]
    names += [("lat", b) for b in reversed(axis_bits("lat"))]
    for step in order:
        dim = names.index(step)
        axis_name, bit = step
        own = (lax.axis_index(axis_name) // bit) % 2
        keep = lax.dynamic_slice_in_dim(part, own, 1, dim).astype(f32)
        away = lax.dynamic_slice_in_dim(part, 1 - own, 1, dim).astype(bf16)
        shape = away.shape
        away = pair_swap(away.reshape(-1, shape[-1]), axis_name, bit).reshape(shape)
        part = keep + away.astype(f32)
        if step != order[-1]:
            part = part.astype(bf16)
    return part.reshape(part.shape[-2:])


def scatter_orders():
    dp_bits = [("dp", b) for b in axis_bits("dp")]
    lat_bits = [("lat", b) for b in axis_bits("lat")]
    first, rest = dp_bits[:1], dp_bits[1:]
    return (
        first + rest + lat_bits,
        first + lat_bits[:1] + lat_bits[1:] + rest,
        first + lat_bits[1:2] + rest + lat_bits[:1] + lat_bits[2:],
    )


def body(
    tokens,
    boxes,
    patch_mask,
    pre_gain,
    pre_shift,
    filter_inner,
    filter_inner_bias,
    filter_outer,
    filter_outer_bias,
    post_gain,
    post_shift,
    expand_weight,
    expand_bias,
    reduce_weight,
    reduce_bias,
    cotangent,
):
    micro_count, crop_count, lat_rows, lon_cells, width = tokens.shape
    groups = lax.axis_size("lat")
    lat_count = lat_rows * groups
    block_count, block_size = filter_inner.shape[1:3]
    sub = groups // block_count
    modes_own = MODES // sub
    crops = micro_count * crop_count
    hidden_width = expand_weight.shape[1]
    lat_index = lax.axis_index("lat")
    own_block = lat_index // sub
    own_index = lat_index * lat_rows + jnp.arange(lat_rows, dtype=jnp.int32)
    lon_index = jnp.arange(lon_cells, dtype=jnp.int32)
    mode_index = jnp.arange(MODES, dtype=jnp.int32)
    lat_range = jnp.arange(lat_count, dtype=jnp.int32)

    lon_factor = 1.0 / math.sqrt(lon_cells)
    cos_fwd, sin_fwd = table_pair(lon_index, mode_index, lon_cells)
    fwd_cos = (cos_fwd * lon_factor).astype(bf16)
    fwd_sin = (sin_fwd * lon_factor).astype(bf16)
    cos_inv, sin_inv = table_pair(mode_index, lon_index, lon_cells)
    mode_weight = jnp.where(mode_index == 0, 1.0, 2.0).astype(f32)
    inv_cos = (cos_inv * mode_weight[:, None] * lon_factor).astype(bf16)
    inv_sin = (sin_inv * mode_weight[:, None] * lon_factor).astype(bf16)
    cos_lat, sin_lat = table_pair(lat_range, lat_range, lat_count)
    lat_factor = 1.0 / math.sqrt(lat_count)
    lat_cos = (cos_lat * lat_factor).astype(bf16)
    lat_sin = (sin_lat * lat_factor).astype(bf16)

    def to_modes(real, imag):
        both = jnp.stack([real, imag], axis=3)
        both = both.reshape(
            crops, lat_rows, sub, modes_own, 2, block_count, block_size
        ).transpose(5, 2, 1, 0, 3, 4, 6)
        both = both.reshape(groups, lat_rows, crops * modes_own, 2 * block_size)
        both = lax.all_to_all(both, "lat", 0, 0, tiled=True)
        return both.reshape(lat_count, crops * modes_own, 2 * block_size)

    def to_rows(both):
        both = both.reshape(groups, lat_rows, crops * modes_own, 2 * block_size)
        both = lax.all_to_all(both, "lat", 0, 0, tiled=True)
        both = both.reshape(
            block_count, sub, lat_rows, crops, modes_own, 2, block_size
        ).transpose(5, 3, 2, 1, 4, 0, 6)
        both = both.reshape(2, crops, lat_rows, MODES, width)
        return both[0], both[1]

    def turn(both, sign):
        flat = both.reshape(lat_count, crops * modes_own, 2, block_size)
        real, imag = flat[:, :, 0], flat[:, :, 1]

        def table(t, v):
            return jnp.einsum("pr,rnd->pnd", t, v, preferred_element_type=f32)

        out_real = table(lat_cos, real) + sign * table(lat_sin, imag)
        out_imag = table(lat_cos, imag) - sign * table(lat_sin, real)
        return jnp.stack([out_real, out_imag], axis=2).astype(bf16).reshape(both.shape)

    def own_matrix(matrix):
        pair = lax.dynamic_index_in_dim(matrix, own_block, 1, keepdims=False)
        top = jnp.concatenate([pair[0], pair[1]], axis=1)
        low = jnp.concatenate([-pair[1], pair[0]], axis=1)
        return jnp.concatenate([top, low], axis=0)

    def own_bias(bias):
        return lax.dynamic_index_in_dim(bias, own_block, 1, keepdims=False).reshape(-1)

    def pair_grad(grad):
        b = block_size
        return jnp.stack(
            [grad[:b, :b] + grad[b:, b:], grad[:b, b:] - grad[b:, :b]]
        )

    inner, outer = own_matrix(filter_inner), own_matrix(filter_outer)
    inner_bias, outer_bias = own_bias(filter_inner_bias), own_bias(filter_outer_bias)

    crop_input = tokens.astype(f32).reshape(crops, lat_rows, lon_cells, width)
    box = boxes.reshape(crops, 2)
    live_rows = own_index[None, :, None] < box[:, 0][:, None, None]
    live_cols = lon_index[None, None, :] < box[:, 1][:, None, None]
    holes = patch_mask.reshape(crops, lat_rows, lon_cells) > 0
    valid = (live_rows & live_cols & holes).astype(f32)[..., None]

    unit_pre, scale_pre = norm_parts(crop_input)
    normed = unit_pre * pre_gain + pre_shift
    masked = (valid * normed).astype(bf16)
    lon_real = jnp.einsum("crsd,sk->crkd", masked, fwd_cos, preferred_element_type=f32)
    lon_imag = -jnp.einsum("crsd,sk->crkd", masked, fwd_sin, preferred_element_type=f32)
    spec = turn(to_modes(lon_real.astype(bf16), lon_imag.astype(bf16)), 1.0)
    spec = spec.reshape(-1, 2 * block_size)
    pre = dot(spec, inner, 1, 0) + inner_bias
    hid, slope = gelu_pair(pre)
    hid = hid.astype(bf16)
    mid = dot(hid, outer, 1, 0) + outer_bias
    filt = shrink(mid).astype(bf16).reshape(lat_count, -1, 2 * block_size)
    back_real, back_imag = to_rows(turn(filt, -1.0))
    filtered = jnp.einsum(
        "crkd,ks->crsd", back_real, inv_cos, preferred_element_type=f32
    ) - jnp.einsum("crkd,ks->crsd", back_imag, inv_sin, preferred_element_type=f32)
    mixed = crop_input + normed + valid * filtered
    unit_post, scale_post = norm_parts(mixed)
    normed_post = (unit_post * post_gain + post_shift).astype(bf16).reshape(-1, width)

    grad_out = cotangent.reshape(-1, width)
    pre_hidden = dot(normed_post, expand_weight, 1, 0) + expand_bias
    hidden, hidden_slope = gelu_pair(pre_hidden)
    hidden = hidden.astype(bf16)
    result = mixed + (dot(hidden, reduce_weight, 1, 0) + reduce_bias).reshape(mixed.shape)
    grad_flat = grad_out.astype(f32)
    grad_pre_hidden = (dot(grad_out, reduce_weight, 1, 1) * hidden_slope).astype(bf16)
    grad_reduce_w = dot(hidden, grad_out, 0, 0)
    grad_expand_t = dot(grad_pre_hidden, normed_post, 0, 0)
    grad_reduce_b = jnp.sum(grad_flat, axis=0)
    grad_expand_b = jnp.sum(grad_pre_hidden.astype(f32), axis=0)
    grad_normed_post = dot(grad_pre_hidden, expand_weight, 1, 1).reshape(mixed.shape)

    shards = lax.axis_size("dp") * groups
    bits = [2] * (shards.bit_length() - 1)
    lanes = width // 3
    pieces = []
    for part in (grad_expand_t, grad_reduce_w):
        part = part.astype(bf16).reshape(bits + [hidden_width // shards, width])
        pieces.append(part)
    summed = []
    for turn_at, order in enumerate(scatter_orders()):
        cut = [lax.slice_in_dim(p, turn_at * lanes, (turn_at + 1) * lanes, axis=-1) for p in pieces]
        summed.append(halving_scatter(jnp.concatenate(cut, axis=-1), order))
    expand_part = jnp.concatenate([s[:, :lanes] for s in summed], axis=1).T
    reduce_part = jnp.concatenate([s[:, lanes:] for s in summed], axis=1)

    grad_mixed, grad_post_g, grad_post_s = norm_back(
        grad_normed_post, unit_post, scale_post, post_gain
    )
    grad_mixed = grad_flat.reshape(mixed.shape) + grad_mixed
    grad_filtered = (valid * grad_mixed).astype(bf16)
    grad_back_real = jnp.einsum(
        "crsd,ks->crkd", grad_filtered, inv_cos, preferred_element_type=f32
    )
    grad_back_imag = -jnp.einsum(
        "crsd,ks->crkd", grad_filtered, inv_sin, preferred_element_type=f32
    )
    grad_filt = turn(to_modes(grad_back_real.astype(bf16), grad_back_imag.astype(bf16)), 1.0)
    grad_filt = lax.optimization_barrier(grad_filt).astype(f32).reshape(-1, 2 * block_size)
    grad_mid = (grad_filt * shrink_slope(mid)).astype(bf16)
    grad_outer = pair_grad(dot(hid, grad_mid, 0, 0))
    grad_outer_b = jnp.sum(grad_mid.astype(f32), axis=0)
    grad_pre = (dot(grad_mid, outer, 1, 1) * slope).astype(bf16)
    grad_inner = pair_grad(dot(spec, grad_pre, 0, 0))
    grad_inner_b = jnp.sum(grad_pre.astype(f32), axis=0)
    grad_lat = dot(grad_pre, inner, 1, 1).astype(bf16).reshape(lat_count, -1, 2 * block_size)
    grad_lon_real, grad_lon_imag = to_rows(turn(grad_lat, -1.0))
    grad_masked = jnp.einsum(
        "crkd,sk->crsd", grad_lon_real, fwd_cos, preferred_element_type=f32
    ) - jnp.einsum("crkd,sk->crsd", grad_lon_imag, fwd_sin, preferred_element_type=f32)
    grad_normed = grad_mixed + valid * grad_masked
    grad_input, grad_pre_g, grad_pre_s = norm_back(grad_normed, unit_pre, scale_pre, pre_gain)
    grad_tokens = (grad_mixed + grad_input).reshape(tokens.shape)

    filters = jnp.stack([grad_inner, grad_outer]).reshape(-1, 2 * block_size)
    for bit in axis_bits("dp"):
        filters = filters + pair_swap(filters, "dp", bit)
    for bit in [b for b in axis_bits("lat") if b < sub]:
        filters = filters + pair_swap(filters, "lat", bit)
    filters = jnp.broadcast_to(filters.astype(bf16), (groups,) + filters.shape)
    filters = lax.all_to_all(filters, "lat", 0, 0, tiled=True)[::sub].astype(f32)
    filters = filters.reshape(block_count, 2, 2, block_size, block_size).transpose(1, 2, 0, 3, 4)

    def place(bias):
        whole = jnp.zeros((2, block_count, block_size), f32)
        return lax.dynamic_update_slice_in_dim(
            whole, bias.reshape(2, 1, block_size), own_block, 1
        ).reshape(-1)

    small = [
        grad_pre_g,
        grad_pre_s,
        place(grad_inner_b),
        place(grad_outer_b),
        grad_post_g,
        grad_post_s,
        grad_expand_b,
        grad_reduce_b,
    ]
    lengths = [v.shape[0] for v in small]
    total = all_sum(jnp.concatenate(small).reshape(-1, 128)).reshape(-1)
    split, at = [], 0
    for length in lengths:
        split.append(total[at : at + length])
        at += length
    return (
        result.astype(bf16).reshape(tokens.shape),
        grad_tokens,
        split[0],
        split[1],
        filters[0],
        split[2].reshape(2, block_count, block_size),
        filters[1],
        split[3].reshape(2, block_count, block_size),
        split[4],
        split[5],
        expand_part,
        split[6],
        reduce_part,
        split[7],
    )


def solution(mesh):
    rows = P(None, "dp", "lat", None, None)
    in_specs = (rows, P(None, "dp", None), P(None, "dp", "lat", None)) + (P(),) * 12 + (rows,)
    out_specs = (
        (rows, rows)
        + (P(),) * 8
        + (P(None, ("dp", "lat")), P(), P(("dp", "lat"), None), P())
    )
    return jax.shard_map(body, mesh=mesh, in_specs=in_specs, out_specs=out_specs, check_vma=False)
```

```python
import functools
import math

import jax
import jax.numpy as jnp
import ml_dtypes
import numpy as np
from jax import lax
from jax.experimental import pallas as pl
from jax.experimental.pallas import tpu as pltpu
from jax.sharding import PartitionSpec as P

MODES = 64
shrink_level = 0.01
epsilon = 1e-05
inv_root_two = 1.0 / math.sqrt(2.0)
inv_root_tau = 1.0 / math.sqrt(2.0 * math.pi)
f32 = jnp.float32
bf16 = jnp.bfloat16


def table_pair(out_count, in_count, length):
    phase = np.arange(out_count)[:, None] * np.arange(in_count)[None, :] % length
    angle = phase.astype(np.float32) * np.float32(2.0 * math.pi / length)
    return np.cos(angle).astype(np.float32), np.sin(angle).astype(np.float32)


def low(values):
    return values.astype(np.float32).astype(ml_dtypes.bfloat16)


def make_tables(lon_cells, lat_count, block_size, chunk):
    lon_factor = np.float32(1.0 / math.sqrt(lon_cells))
    cosine, sine = table_pair(MODES, lon_cells, lon_cells)
    weight = np.where(np.arange(MODES) == 0, 1.0, 2.0).astype(np.float32)[:, None]
    forward = low(np.concatenate([cosine, -sine]) * lon_factor)
    inverse = low(np.concatenate([cosine * weight, -sine * weight]) * lon_factor)
    cosine, sine = table_pair(lat_count, lat_count, lat_count)
    lat_factor = np.float32(1.0 / math.sqrt(lat_count))
    same = np.eye(chunk, dtype=np.float32)
    cosine = np.kron(low(cosine * lat_factor).astype(np.float32), same)
    sine = np.kron(low(sine * lat_factor).astype(np.float32), same)
    turn_fwd = low(np.concatenate([cosine, sine], axis=1))
    turn_inv = low(np.concatenate([cosine, -sine], axis=1))
    eye, none = np.eye(block_size), np.zeros((block_size, block_size))
    swap = low(np.block([[none, -eye], [eye, none]]))
    return dict(
        fwd=forward, fwd_t=forward.T.copy(), inv=inverse, inv_t=inverse.T.copy(),
        turn_fwd=turn_fwd, turn_inv=turn_inv, swap=swap,
    )


def dot(a, b, ca, cb):
    return lax.dot_general(a, b, (((ca,), (cb,)), ((), ())), preferred_element_type=f32)


def row_mean(values):
    return jnp.sum(values, axis=-1, keepdims=True) * (1.0 / values.shape[-1])


def norm_parts(values):
    centered = values - row_mean(values)
    inv_scale = lax.rsqrt(row_mean(centered * centered) + epsilon)
    return centered * inv_scale, inv_scale


def norm_back(grad_normed, unit_values, inv_scale, gain):
    grad_unit = grad_normed * gain
    plain, cross = row_mean(grad_unit), row_mean(grad_unit * unit_values)
    return inv_scale * (grad_unit - plain - unit_values * cross)


def gelu_pair(values):
    half = 0.5 * (1.0 + lax.erf(values * inv_root_two))
    return values * half, half + values * jnp.exp(-0.5 * values * values) * inv_root_tau


def shrink_pair(values):
    inverse = lax.rsqrt(values * values + shrink_level * shrink_level)
    slope = 1.0 - shrink_level * shrink_level * shrink_level * inverse * inverse * inverse
    return values - shrink_level * values * inverse, slope


def valid_row(box_ref, row_ref, hole_ref, lat_rows, cells):
    item = pl.program_id(0)
    crop, row = item // lat_rows, row_ref[0] + item % lat_rows
    limit = jnp.where(row < box_ref[2 * crop], box_ref[2 * crop + 1], 0)
    column = lax.broadcasted_iota(jnp.int32, (1, cells), 1)
    return jnp.where((column < limit) & (hole_ref[0] > 0), 1.0, 0.0)


def as_column(row):
    cells = row.shape[1]
    down = lax.broadcasted_iota(jnp.int32, (cells, cells), 0)
    along = lax.broadcasted_iota(jnp.int32, (cells, cells), 1)
    return jnp.sum(jnp.where(down == along, row, 0.0), axis=1, keepdims=True)


def put_modes(send_ref, spectrum, block_size, sub):
    spectrum = spectrum.astype(bf16)
    own = MODES // sub
    for block in range(spectrum.shape[1] // block_size):
        cut = spectrum[:, block * block_size : (block + 1) * block_size]
        both = jnp.concatenate([cut[:MODES], cut[MODES:]], axis=1)
        for j in range(sub):
            send_ref[block * sub + j, 0] = both[j * own : (j + 1) * own]


def get_modes(recv_ref, block_size, sub):
    groups = recv_ref.shape[0]
    real, imag = [], []
    for block in range(groups // sub):
        parts = [recv_ref[block * sub + j, 0] for j in range(sub)]
        both = parts[0] if sub == 1 else jnp.concatenate(parts, axis=0)
        real.append(both[:, :block_size])
        imag.append(both[:, block_size:])
    real, imag = jnp.concatenate(real, axis=1), jnp.concatenate(imag, axis=1)
    return jnp.concatenate([real, imag], axis=0)


def turn_rows(src_ref, dst_ref, table, swap, chunk):
    lat_count, points, wide = src_ref.shape
    for at in range(0, points, chunk):
        piece = src_ref[:, at : at + chunk, :].reshape(lat_count * chunk, wide)
        other = dot(piece, swap, 1, 0).astype(bf16)
        out = dot(table, jnp.concatenate([piece, other], axis=0), 1, 0)
        dst_ref[:, at : at + chunk, :] = out.astype(bf16).reshape(lat_count, chunk, wide)


def pre_kernel(
    lat_rows, block_size, sub,
    box_ref, row_ref, token_ref, cot_ref, hole_ref, gain_ref, shift_ref, table_ref,
    send_ref, cot_pad_ref,
):
    cells = token_ref.shape[1]
    valid = valid_row(box_ref, row_ref, hole_ref, lat_rows, cells)
    unit, _ = norm_parts(token_ref[0].astype(f32))
    normed = (unit * gain_ref[...] + shift_ref[...]).astype(bf16)
    table = (table_ref[...].astype(f32) * valid).astype(bf16)
    put_modes(send_ref, dot(table, normed, 1, 0), block_size, sub)
    pad = cot_pad_ref.shape[1] - cells
    cot_pad_ref[0, :cells] = cot_ref[0]
    if pad:
        cot_pad_ref[0, cells:] = jnp.zeros((pad, cot_ref.shape[2]), bf16)


def filter_kernel(
    chunk,
    recv_ref, inner_ref, inner_bias_ref, outer_ref, outer_bias_ref, turn_fwd_ref, turn_inv_ref, swap_ref,
    send_ref, spec_ref, hid_ref, slope_ref, shrunk_ref, filt_ref,
):
    turn_rows(recv_ref, spec_ref, turn_fwd_ref[...], swap_ref[...], chunk)
    for p in range(spec_ref.shape[0]):
        pre = dot(spec_ref[p], inner_ref[...], 1, 0) + inner_bias_ref[...]
        hid, slope = gelu_pair(pre)
        hid = hid.astype(bf16)
        hid_ref[p] = hid
        slope_ref[p] = slope
        mid = dot(hid, outer_ref[...], 1, 0) + outer_bias_ref[...]
        filt, shrunk = shrink_pair(mid)
        filt_ref[p] = filt.astype(bf16)
        shrunk_ref[p] = shrunk
    turn_rows(filt_ref, send_ref, turn_inv_ref[...], swap_ref[...], chunk)


def mix_kernel(
    lat_rows, block_size, sub,
    box_ref, row_ref, recv_ref, token_ref, hole_ref, gain_ref, shift_ref,
    post_gain_ref, post_shift_ref, table_ref,
    mixed_ref, post_ref,
):
    cells = token_ref.shape[1]
    valid = as_column(valid_row(box_ref, row_ref, hole_ref, lat_rows, cells))
    tokens = token_ref[0].astype(f32)
    unit, _ = norm_parts(tokens)
    normed = unit * gain_ref[...] + shift_ref[...]
    filtered = dot(table_ref[...], get_modes(recv_ref, block_size, sub), 1, 0)
    mixed = tokens + normed + valid * filtered
    mixed_ref[0] = mixed
    unit, _ = norm_parts(mixed)
    post_ref[0, :cells] = (unit * post_gain_ref[...] + post_shift_ref[...]).astype(bf16)
    pad = post_ref.shape[1] - cells
    if pad:
        post_ref[0, cells:] = jnp.zeros((pad, token_ref.shape[2]), bf16)


def feed_kernel(
    core_ref, post_own_ref, post_other_ref, cot_own_ref, cot_other_ref,
    expand_ref, expand_bias_ref, reduce_ref,
    group_a_ref, group_b_ref, group_c_ref, bias_grad_ref,
    out_own_ref, out_other_ref, grad_own_ref, grad_other_ref,
    post_ref, cot_ref, out_ref, grad_ref,
):
    step = pl.program_id(0)
    rows = post_own_ref.shape[0]

    @pl.when(step == 0)
    def _():
        post_ref[:rows] = post_own_ref[...]
        post_ref[rows:] = post_other_ref[...]
        cot_ref[:rows] = cot_own_ref[...]
        cot_ref[rows:] = cot_other_ref[...]
        out_ref[...] = jnp.zeros_like(out_ref)
        grad_ref[...] = jnp.zeros_like(grad_ref)

    expand, reduce = expand_ref[...], reduce_ref[...]
    post, cot = post_ref[...], cot_ref[...]
    hidden, slope = gelu_pair(dot(post, expand, 1, 0) + expand_bias_ref[...])
    hidden = hidden.astype(bf16)
    grad = (dot(cot, reduce, 1, 1) * slope).astype(bf16)
    bias_grad_ref[...] = jnp.sum(grad.astype(f32), axis=0, keepdims=True)
    out_ref[...] += dot(hidden, reduce, 1, 0)
    grad_ref[...] += dot(grad, expand, 1, 1)
    grad_expand = dot(grad, post, 0, 0).astype(bf16)
    grad_reduce = dot(hidden, cot, 0, 0).astype(bf16)
    lanes = group_a_ref.shape[1] // 2
    for at, group_ref in enumerate((group_a_ref, group_b_ref, group_c_ref)):
        group_ref[:, :lanes] = grad_expand[:, at * lanes : (at + 1) * lanes]
        group_ref[:, lanes:] = grad_reduce[:, at * lanes : (at + 1) * lanes]

    @pl.when(step == pl.num_programs(0) - 1)
    def _():
        out_own_ref[...] = out_ref[:rows]
        out_other_ref[...] = out_ref[rows:].astype(bf16)
        grad_own_ref[...] = grad_ref[:rows]
        grad_other_ref[...] = grad_ref[rows:].astype(bf16)


def add_sum(ref, value):
    value = jnp.sum(value, axis=0, keepdims=True)

    @pl.when(pl.program_id(0) == 0)
    def _():
        ref[...] = value

    @pl.when(pl.program_id(0) > 0)
    def _():
        ref[...] += value


def post_kernel(
    lat_rows, block_size, sub,
    box_ref, row_ref, mixed_ref, out_own_ref, out_other_ref, grad_own_ref, grad_other_ref,
    cot_ref, hole_ref, gain_ref, bias_ref, table_ref,
    result_ref, grad_mixed_ref, send_ref, gain_grad_ref, shift_grad_ref, bias_grad_ref,
):
    cells = mixed_ref.shape[1]
    valid = valid_row(box_ref, row_ref, hole_ref, lat_rows, cells)
    mixed = mixed_ref[0]
    out = out_own_ref[0, :cells] + out_other_ref[0, :cells].astype(f32)
    result_ref[0] = (mixed + (out + bias_ref[...])).astype(bf16)
    grad = grad_own_ref[0, :cells] + grad_other_ref[0, :cells].astype(f32)
    unit, inv_scale = norm_parts(mixed)
    add_sum(gain_grad_ref, grad * unit)
    add_sum(shift_grad_ref, grad)
    cot = cot_ref[0].astype(f32)
    add_sum(bias_grad_ref, cot)
    grad_mixed = cot + norm_back(grad, unit, inv_scale, gain_ref[...])
    grad_mixed_ref[0] = grad_mixed
    table = (table_ref[...].astype(f32) * valid).astype(bf16)
    put_modes(send_ref, dot(table, grad_mixed.astype(bf16), 1, 0), block_size, sub)


def filter_back_kernel(
    chunk,
    recv_ref, spec_ref, hid_ref, slope_ref, shrunk_ref, inner_ref, outer_ref,
    turn_fwd_ref, turn_inv_ref, swap_ref,
    send_ref, weight_grad_ref, bias_grad_ref,
    turned_ref, grad_mid_ref, grad_pre_ref,
):
    lat_count, points, wide = recv_ref.shape
    turn_rows(recv_ref, turned_ref, turn_fwd_ref[...], swap_ref[...], chunk)
    inner_bias = jnp.zeros((1, wide), f32)
    outer_bias = jnp.zeros((1, wide), f32)
    for p in range(lat_count):
        grad_mid = (turned_ref[p].astype(f32) * shrunk_ref[p]).astype(bf16)
        grad_mid_ref[p] = grad_mid
        outer_bias += jnp.sum(grad_mid.astype(f32), axis=0, keepdims=True)
        grad_pre = (dot(grad_mid, outer_ref[...], 1, 1) * slope_ref[p]).astype(bf16)
        grad_pre_ref[p] = grad_pre
        inner_bias += jnp.sum(grad_pre.astype(f32), axis=0, keepdims=True)
        turned_ref[p] = dot(grad_pre, inner_ref[...], 1, 1).astype(bf16)
    turn_rows(turned_ref, send_ref, turn_inv_ref[...], swap_ref[...], chunk)
    bias_grad_ref[0:1] = inner_bias
    bias_grad_ref[1:2] = outer_bias
    flat = (lat_count * points, wide)
    half = wide // 2
    pairs = ((spec_ref, grad_pre_ref), (hid_ref, grad_mid_ref))
    for at, (left, right) in enumerate(pairs):
        grad = dot(left[...].reshape(flat), right[...].reshape(flat), 0, 0)
        weight_grad_ref[at, 0] = grad[:half, :half] + grad[half:, half:]
        weight_grad_ref[at, 1] = grad[:half, half:] - grad[half:, :half]


def last_kernel(
    lat_rows, block_size, sub,
    box_ref, row_ref, recv_ref, token_ref, grad_mixed_ref, hole_ref, gain_ref, table_ref,
    result_ref, gain_grad_ref, shift_grad_ref,
):
    cells = token_ref.shape[1]
    valid = as_column(valid_row(box_ref, row_ref, hole_ref, lat_rows, cells))
    grad_masked = dot(table_ref[...], get_modes(recv_ref, block_size, sub), 1, 0)
    grad_mixed = grad_mixed_ref[0]
    grad = grad_mixed + valid * grad_masked
    unit, inv_scale = norm_parts(token_ref[0].astype(f32))
    add_sum(gain_grad_ref, grad * unit)
    add_sum(shift_grad_ref, grad)
    result_ref[0] = grad_mixed + norm_back(grad, unit, inv_scale, gain_ref[...])


def call(kernel, grid, in_specs, out_specs, out_shape, args, prefetch=0, scratch=(), flops=0):
    moved = sum(a.size * a.dtype.itemsize for a in args)
    moved += sum(math.prod(s.shape) * np.dtype(s.dtype).itemsize for s in out_shape)
    return pl.pallas_call(
        kernel,
        out_shape=out_shape,
        grid_spec=pltpu.PrefetchScalarGridSpec(
            num_scalar_prefetch=prefetch,
            grid=grid,
            in_specs=in_specs,
            out_specs=out_specs,
            scratch_shapes=scratch,
        ),
        compiler_params=pltpu.CompilerParams(
            dimension_semantics=("arbitrary",), vmem_limit_bytes=48 << 20
        ),
        cost_estimate=pl.CostEstimate(flops=int(flops), bytes_accessed=int(moved), transcendentals=0),
    )(*args)


def shape(dims, dtype):
    return jax.ShapeDtypeStruct(tuple(dims), dtype)


def item_spec(dims):
    rest = (0,) * (len(dims) - 1)
    return pl.BlockSpec((1,) + tuple(dims[1:]), lambda i, *_: (i,) + rest)


def mode_spec(dims):
    return pl.BlockSpec((dims[0], 1) + tuple(dims[2:]), lambda i, *_: (0, i, 0, 0))


def whole_spec(dims):
    rest = (0,) * len(dims)
    return pl.BlockSpec(tuple(dims), lambda *_: rest)


def pair_swap(operand, axis_name, bit):
    size = lax.axis_size(axis_name)
    return lax.ppermute(operand, axis_name, [(i, i ^ bit) for i in range(size)])


def axis_bits(axis_name):
    size = lax.axis_size(axis_name)
    return [1 << i for i in range(size.bit_length() - 1)]


def all_sum(vector):
    for axis_name in ("dp", "lat"):
        for bit in axis_bits(axis_name):
            vector = vector + pair_swap(vector, axis_name, bit)
    return vector


def halving_scatter(part, names, order):
    for step in order:
        dim = names.index(step)
        axis_name, bit = step
        own = (lax.axis_index(axis_name) // bit) % 2
        keep = lax.dynamic_slice_in_dim(part, own, 1, dim).astype(f32)
        away = lax.dynamic_slice_in_dim(part, 1 - own, 1, dim).astype(bf16)
        dims = away.shape
        away = pair_swap(away.reshape(-1, dims[-1]), axis_name, bit).reshape(dims)
        part = keep + away.astype(f32)
        if step != order[-1]:
            part = part.astype(bf16)
    return part.reshape(part.shape[-2:])


def body(
    tokens,
    boxes,
    patch_mask,
    pre_gain,
    pre_shift,
    filter_inner,
    filter_inner_bias,
    filter_outer,
    filter_outer_bias,
    post_gain,
    post_shift,
    expand_weight,
    expand_bias,
    reduce_weight,
    reduce_bias,
    cotangent,
):
    micro_count, crop_count, lat_rows, cells, width = tokens.shape
    groups = lax.axis_size("lat")
    lat_count = lat_rows * groups
    block_count, block_size = filter_inner.shape[1:3]
    sub = groups // block_count
    modes_own = MODES // sub
    crops = micro_count * crop_count
    items = crops * lat_rows
    points = crops * modes_own
    wide = 2 * block_size
    padded = -(-cells // 16) * 16
    rows = items * padded
    chunk = 16
    hidden_width = expand_weight.shape[1]
    dp_size = lax.axis_size("dp")
    lat_index, dp_index = lax.axis_index("lat"), lax.axis_index("dp")
    own_block = lat_index // sub
    tables = {k: jnp.asarray(v) for k, v in make_tables(cells, lat_count, block_size, chunk).items()}

    box = boxes.reshape(-1)
    own_row = (lat_index * lat_rows).astype(jnp.int32).reshape(1)
    core = (dp_index % 2).astype(jnp.int32).reshape(1)
    token_items = tokens.reshape(items, cells, width)
    cot_items = cotangent.reshape(items, cells, width)
    holes = patch_mask.reshape(items, 1, cells)
    gain_pre, shift_pre = pre_gain.reshape(1, width), pre_shift.reshape(1, width)
    gain_post, shift_post = post_gain.reshape(1, width), post_shift.reshape(1, width)
    row_item, hole_item = (items, cells, width), (items, 1, cells)
    pad_item = (items, padded, width)
    mode_dims = (groups, items, modes_own, wide)
    vector = (1, width)
    names = (lat_rows, block_size, sub)
    lon_flops = 2 * items * 2 * MODES * cells * width

    def exchange(both, by_rows):
        if by_rows:
            both = both.reshape(groups, crops, lat_rows, modes_own, wide).swapaxes(1, 2)
            both = both.reshape(groups, lat_rows * points, wide)
            both = lax.all_to_all(both, "lat", 0, 0, tiled=True)
            return both.reshape(lat_count, points, wide)
        both = lax.all_to_all(both.reshape(groups, lat_rows * points, wide), "lat", 0, 0, tiled=True)
        both = both.reshape(groups, lat_rows, crops, modes_own, wide).swapaxes(1, 2)
        return both.reshape(mode_dims)

    def own_matrix(matrix):
        pair = lax.dynamic_index_in_dim(matrix, own_block, 1, keepdims=False)
        top = jnp.concatenate([pair[0], pair[1]], axis=1)
        under = jnp.concatenate([-pair[1], pair[0]], axis=1)
        return jnp.concatenate([top, under], axis=0)

    def own_bias(bias):
        return lax.dynamic_index_in_dim(bias, own_block, 1, keepdims=False).reshape(1, wide)

    args = (box, own_row, token_items, cot_items, holes, gain_pre, shift_pre, tables["fwd"])
    send, cot_pad = call(
        functools.partial(pre_kernel, *names),
        (items,),
        [item_spec(row_item), item_spec(row_item), item_spec(hole_item)]
        + [whole_spec(a.shape) for a in args[5:]],
        [mode_spec(mode_dims), item_spec(pad_item)],
        [shape(mode_dims, bf16), shape(pad_item, bf16)],
        args,
        prefetch=2,
        flops=lon_flops,
    )
    cot_pad = cot_pad.reshape(rows, width)
    cot_other = pair_swap(cot_pad, "dp", 1)
    recv = exchange(send, True)

    spectrum = (lat_count, points, wide)
    filter_flops = 4 * lat_count * points * wide * wide
    inner, outer = own_matrix(filter_inner), own_matrix(filter_outer)
    args = (
        recv, inner, own_bias(filter_inner_bias), outer, own_bias(filter_outer_bias),
        tables["turn_fwd"], tables["turn_inv"], tables["swap"],
    )
    send, spec, hid, slope, shrunk = call(
        functools.partial(filter_kernel, chunk),
        (1,),
        [whole_spec(a.shape) for a in args],
        [whole_spec(spectrum)] * 5,
        [shape(spectrum, t) for t in (bf16, bf16, bf16, f32, f32)],
        args,
        scratch=[pltpu.VMEM(spectrum, bf16)],
        flops=filter_flops,
    )
    recv = exchange(send, False)

    args = (
        box, own_row, recv, token_items, holes, gain_pre, shift_pre, gain_post, shift_post,
        tables["inv_t"],
    )
    mixed, post = call(
        functools.partial(mix_kernel, *names),
        (items,),
        [mode_spec(mode_dims), item_spec(row_item), item_spec(hole_item)]
        + [whole_spec(a.shape) for a in args[5:]],
        [item_spec(row_item), item_spec(pad_item)],
        [shape(row_item, f32), shape(pad_item, bf16)],
        args,
        prefetch=2,
        flops=lon_flops,
    )
    post = post.reshape(rows, width)
    post_other = pair_swap(post, "dp", 1)

    run = hidden_width // dp_size
    tile = next(t for t in (256, 384, 128, run) if run % t == 0)
    per_run = run // tile
    hidden_own = hidden_width // 2
    lanes = width // 3

    def column(j, core_ref):
        return ((j // per_run) * 2 + core_ref[0]) * per_run + j % per_run

    args = (
        core, post, post_other, cot_pad, cot_other,
        expand_weight, expand_bias.reshape(1, hidden_width), reduce_weight,
    )
    group_spec = pl.BlockSpec((tile, 2 * lanes), lambda j, _: (j, 0))
    flat = (rows, width)
    *parts, grad_expand_b, out_own, out_other, grad_own, grad_other = call(
        feed_kernel,
        (hidden_own // tile,),
        [whole_spec(flat)] * 4
        + [
            pl.BlockSpec((width, tile), lambda j, c: (0, column(j, c))),
            pl.BlockSpec((1, tile), lambda j, c: (0, column(j, c))),
            pl.BlockSpec((tile, width), lambda j, c: (column(j, c), 0)),
        ],
        [group_spec] * 3
        + [pl.BlockSpec((1, tile), lambda j, _: (0, j))]
        + [whole_spec(flat)] * 4,
        [shape((hidden_own, 2 * lanes), bf16)] * 3
        + [shape((1, hidden_own), f32)]
        + [shape(flat, t) for t in (f32, bf16, f32, bf16)],
        args,
        prefetch=1,
        scratch=[pltpu.VMEM((2 * rows, width), t) for t in (bf16, bf16, f32, f32)],
        flops=6 * 2 * 2 * rows * width * hidden_own,
    )
    grad_other = pair_swap(grad_other, "dp", 1).reshape(pad_item)
    out_other = pair_swap(out_other, "dp", 1).reshape(pad_item)

    args = (
        box, own_row, mixed, out_own.reshape(pad_item), out_other, grad_own.reshape(pad_item),
        grad_other, cot_items, holes, gain_post, reduce_bias.reshape(1, width), tables["inv"],
    )
    result, grad_mixed, send, grad_post_g, grad_post_s, grad_reduce_b = call(
        functools.partial(post_kernel, *names),
        (items,),
        [item_spec(row_item)] + [item_spec(pad_item)] * 4
        + [item_spec(row_item), item_spec(hole_item)]
        + [whole_spec(a.shape) for a in args[9:]],
        [item_spec(row_item), item_spec(row_item), mode_spec(mode_dims)] + [whole_spec(vector)] * 3,
        [shape(row_item, bf16), shape(row_item, f32), shape(mode_dims, bf16)] + [shape(vector, f32)] * 3,
        args,
        prefetch=2,
        flops=lon_flops,
    )
    recv = exchange(send, True)

    lat_bits = [("lat", b) for b in axis_bits("lat")]
    dp_bits = [("dp", b) for b in axis_bits("dp")[1:]]
    orders = (
        dp_bits + lat_bits,
        lat_bits + dp_bits,
        lat_bits[1:2] + dp_bits + lat_bits[:1] + lat_bits[2:],
    )
    bit_names = dp_bits[::-1] + lat_bits[::-1]
    own_rows = hidden_width // (dp_size * groups)
    summed = []
    for part, order in zip(parts, orders):
        part = part.reshape([2] * len(bit_names) + [own_rows, 2 * lanes])
        summed.append(halving_scatter(part, bit_names, order))
    expand_part = jnp.concatenate([s[:, :lanes] for s in summed], axis=1).T
    reduce_part = jnp.concatenate([s[:, lanes:] for s in summed], axis=1)

    args = (
        recv, spec, hid, slope, shrunk, inner, outer,
        tables["turn_fwd"], tables["turn_inv"], tables["swap"],
    )
    weight_dims = (2, 2, block_size, block_size)
    send, filters, filter_bias = call(
        functools.partial(filter_back_kernel, chunk),
        (1,),
        [whole_spec(a.shape) for a in args],
        [whole_spec(spectrum), whole_spec(weight_dims), whole_spec((2, wide))],
        [shape(spectrum, bf16), shape(weight_dims, f32), shape((2, wide), f32)],
        args,
        scratch=[pltpu.VMEM(spectrum, bf16)] * 3,
        flops=2 * filter_flops,
    )
    recv = exchange(send, False)

    args = (
        box, own_row, recv, token_items, grad_mixed, holes, gain_pre, tables["fwd_t"],
    )
    grad_tokens, grad_pre_g, grad_pre_s = call(
        functools.partial(last_kernel, *names),
        (items,),
        [mode_spec(mode_dims), item_spec(row_item), item_spec(row_item), item_spec(hole_item)]
        + [whole_spec(a.shape) for a in args[6:]],
        [item_spec(row_item)] + [whole_spec(vector)] * 2,
        [shape(row_item, f32)] + [shape(vector, f32)] * 2,
        args,
        prefetch=2,
        flops=lon_flops,
    )

    filters = filters.reshape(-1, block_size)
    for bit in axis_bits("dp"):
        filters = filters + pair_swap(filters, "dp", bit)
    for bit in [b for b in axis_bits("lat") if b < sub]:
        filters = filters + pair_swap(filters, "lat", bit)
    filters = jnp.broadcast_to(filters.astype(bf16), (groups,) + filters.shape)
    filters = lax.all_to_all(filters, "lat", 0, 0, tiled=True)[::sub].astype(f32)
    filters = filters.reshape((block_count,) + weight_dims).transpose(1, 2, 0, 3, 4)

    def place(bias):
        spread = jnp.zeros((2, block_count, block_size), f32)
        return lax.dynamic_update_slice_in_dim(
            spread, bias.reshape(2, 1, block_size), own_block, 1
        ).reshape(-1)

    spread = jnp.zeros((dp_size // 2, 2, run), f32)
    spread = lax.dynamic_update_slice_in_dim(
        spread, grad_expand_b.reshape(dp_size // 2, 1, run), core[0], 1
    )
    small = [
        grad_pre_g.reshape(-1),
        grad_pre_s.reshape(-1),
        place(filter_bias[0]),
        place(filter_bias[1]),
        grad_post_g.reshape(-1),
        grad_post_s.reshape(-1),
        spread.reshape(-1),
        grad_reduce_b.reshape(-1),
    ]
    lengths = [v.shape[0] for v in small]
    total = all_sum(jnp.concatenate(small).reshape(-1, 128)).reshape(-1)
    split, at = [], 0
    for length in lengths:
        split.append(total[at : at + length])
        at += length
    return (
        result.reshape(tokens.shape),
        grad_tokens.reshape(tokens.shape),
        split[0],
        split[1],
        filters[0],
        split[2].reshape(2, block_count, block_size),
        filters[1],
        split[3].reshape(2, block_count, block_size),
        split[4],
        split[5],
        expand_part,
        split[6],
        reduce_part,
        split[7],
    )


def solution(mesh):
    rows = P(None, "dp", "lat", None, None)
    in_specs = (rows, P(None, "dp", None), P(None, "dp", "lat", None)) + (P(),) * 12 + (rows,)
    out_specs = (
        (rows, rows)
        + (P(),) * 8
        + (P(None, ("dp", "lat")), P(), P(("dp", "lat"), None), P())
    )
    return jax.shard_map(body, mesh=mesh, in_specs=in_specs, out_specs=out_specs, check_vma=False)
```

```python
import functools
import math

import jax
import jax.numpy as jnp
import ml_dtypes
import numpy as np
from jax import lax
from jax.experimental import pallas as pl
from jax.experimental.pallas import tpu as pltpu
from jax.sharding import PartitionSpec as P

MODES = 64
shrink_level = 0.01
epsilon = 1e-05
inv_root_two = 1.0 / math.sqrt(2.0)
inv_root_tau = 1.0 / math.sqrt(2.0 * math.pi)
f32 = jnp.float32
bf16 = jnp.bfloat16


def table_pair(out_count, in_count, length):
    phase = np.arange(out_count)[:, None] * np.arange(in_count)[None, :] % length
    angle = phase.astype(np.float32) * np.float32(2.0 * math.pi / length)
    return np.cos(angle).astype(np.float32), np.sin(angle).astype(np.float32)


def low(values):
    return values.astype(np.float32).astype(ml_dtypes.bfloat16)


def make_tables(lon_cells, lat_count, block_size, chunk):
    lon_factor = np.float32(1.0 / math.sqrt(lon_cells))
    cosine, sine = table_pair(MODES, lon_cells, lon_cells)
    weight = np.where(np.arange(MODES) == 0, 1.0, 2.0).astype(np.float32)[:, None]
    forward = low(np.concatenate([cosine, -sine]) * lon_factor)
    inverse = low(np.concatenate([cosine * weight, -sine * weight]) * lon_factor)
    cosine, sine = table_pair(lat_count, lat_count, lat_count)
    lat_factor = np.float32(1.0 / math.sqrt(lat_count))
    same = np.eye(chunk, dtype=np.float32)
    cosine = np.kron(low(cosine * lat_factor).astype(np.float32), same)
    sine = np.kron(low(sine * lat_factor).astype(np.float32), same)
    turn_fwd = low(np.concatenate([cosine, sine], axis=1))
    turn_inv = low(np.concatenate([cosine, -sine], axis=1))
    eye, none = np.eye(block_size), np.zeros((block_size, block_size))
    swap = low(np.block([[none, -eye], [eye, none]]))
    return dict(
        fwd=forward, fwd_t=forward.T.copy(), inv=inverse, inv_t=inverse.T.copy(),
        turn_fwd=turn_fwd, turn_inv=turn_inv, swap=swap,
    )


def dot(a, b, ca, cb):
    return lax.dot_general(a, b, (((ca,), (cb,)), ((), ())), preferred_element_type=f32)


def line(ref):
    return ref[...].reshape(1, -1)


def row_mean(values):
    return jnp.sum(values, axis=-1, keepdims=True) * (1.0 / values.shape[-1])


def norm_parts(values):
    centered = values - row_mean(values)
    inv_scale = lax.rsqrt(row_mean(centered * centered) + epsilon)
    return centered * inv_scale, inv_scale


def norm_back(grad_normed, unit_values, inv_scale, gain):
    grad_unit = grad_normed * gain
    plain, cross = row_mean(grad_unit), row_mean(grad_unit * unit_values)
    return inv_scale * (grad_unit - plain - unit_values * cross)


def gelu_pair(values):
    half = 0.5 * (1.0 + lax.erf(values * inv_root_two))
    return values * half, half + values * jnp.exp(-0.5 * values * values) * inv_root_tau


def shrink_pair(values):
    inverse = lax.rsqrt(values * values + shrink_level * shrink_level)
    slope = 1.0 - shrink_level * shrink_level * shrink_level * inverse * inverse * inverse
    return values - shrink_level * values * inverse, slope


def valid_row(item, box_ref, row_ref, hole_ref, lat_rows, cells):
    crop, row = item // lat_rows, row_ref[0] + item % lat_rows
    crop_count = box_ref.shape[1]
    micro, crop = crop // crop_count, crop % crop_count
    limit = jnp.where(row < box_ref[micro, crop, 0], box_ref[micro, crop, 1], 0)
    column = lax.broadcasted_iota(jnp.int32, (1, cells), 1)
    return jnp.where((column < limit) & (hole_ref[item] > 0), 1.0, 0.0)


def as_column(row):
    cells = row.shape[1]
    down = lax.broadcasted_iota(jnp.int32, (cells, cells), 0)
    along = lax.broadcasted_iota(jnp.int32, (cells, cells), 1)
    return jnp.sum(jnp.where(down == along, row, 0.0), axis=1, keepdims=True)


def pack(both):
    half = both.shape[0] // 2
    rest = both[:, 128:]
    return both[:, :128], jnp.concatenate([rest[:half], rest[half:]], axis=1)


def unpack(packed):
    points = packed.shape[0] * 2 // 3
    rest = packed[points:]
    rest = jnp.concatenate([rest[:, :64], rest[:, 64:]], axis=0)
    return jnp.concatenate([packed[:points], rest], axis=1)


def put_modes(send_ref, item, spectrum, block_size, sub):
    spectrum = spectrum.astype(bf16)
    own = MODES // sub
    for block in range(spectrum.shape[1] // block_size):
        cut = spectrum[:, block * block_size : (block + 1) * block_size]
        both = jnp.concatenate([cut[:MODES], cut[MODES:]], axis=1)
        for j in range(sub):
            top, rest = pack(both[j * own : (j + 1) * own])
            send_ref[block * sub + j, item, :own] = top
            send_ref[block * sub + j, item, own:] = rest


def get_modes(recv_ref, item, block_size, sub):
    groups = recv_ref.shape[0]
    real, imag = [], []
    for block in range(groups // sub):
        parts = [unpack(recv_ref[block * sub + j, item]) for j in range(sub)]
        both = parts[0] if sub == 1 else jnp.concatenate(parts, axis=0)
        real.append(both[:, :block_size])
        imag.append(both[:, block_size:])
    real, imag = jnp.concatenate(real, axis=1), jnp.concatenate(imag, axis=1)
    return jnp.concatenate([real, imag], axis=0)


def unpack_all(recv_ref, points_ref):
    lat_count, crops, packed, _ = recv_ref.shape
    own = packed * 2 // 3
    for p in range(lat_count):
        for crop in range(crops):
            points_ref[p, crop * own : (crop + 1) * own] = unpack(recv_ref[p, crop])


def pack_all(points_ref, send_ref):
    lat_count, crops, packed, _ = send_ref.shape
    own = packed * 2 // 3
    for p in range(lat_count):
        for crop in range(crops):
            top, rest = pack(points_ref[p, crop * own : (crop + 1) * own])
            send_ref[p, crop, :own] = top
            send_ref[p, crop, own:] = rest


def turn_rows(src_ref, dst_ref, table, swap, chunk):
    lat_count, points, wide = src_ref.shape
    for at in range(0, points, chunk):
        piece = src_ref[:, at : at + chunk, :].reshape(lat_count * chunk, wide)
        other = dot(piece, swap, 1, 0).astype(bf16)
        out = dot(table, jnp.concatenate([piece, other], axis=0), 1, 0)
        dst_ref[:, at : at + chunk, :] = out.astype(bf16).reshape(lat_count, chunk, wide)


def pre_kernel(
    lat_rows, block_size, sub,
    box_ref, row_ref, token_ref, hole_ref, gain_ref, shift_ref, table_ref,
    send_ref,
):
    items, cells, _ = token_ref.shape
    units = [norm_parts(token_ref[item].astype(f32))[0] for item in range(items)]
    for item in range(items):
        valid = valid_row(item, box_ref, row_ref, hole_ref, lat_rows, cells)
        normed = (units[item] * line(gain_ref) + line(shift_ref)).astype(bf16)
        table = (table_ref[...].astype(f32) * valid).astype(bf16)
        put_modes(send_ref, item, dot(table, normed, 1, 0), block_size, sub)


def filter_kernel(
    chunk,
    recv_ref, inner_ref, inner_bias_ref, outer_ref, outer_bias_ref, turn_fwd_ref, turn_inv_ref, swap_ref,
    send_ref, spec, hid_out, slope_out, shrunk_out,
    hid_ref, slope_ref, shrunk_ref, filt_ref, points_ref, sems,
):
    unpack_all(recv_ref, points_ref)
    spec_ref = spec.here
    turn_rows(points_ref, spec_ref, turn_fwd_ref[...], swap_ref[...], chunk)
    spec.start()
    copies = []
    for p in range(spec_ref.shape[0]):
        pre = dot(spec_ref[p], inner_ref[...], 1, 0) + inner_bias_ref[...]
        hid, slope = gelu_pair(pre)
        hid = hid.astype(bf16)
        hid_ref[p] = hid
        slope_ref[p] = slope
        mid = dot(hid, outer_ref[...], 1, 0) + outer_bias_ref[...]
        filt, shrunk = shrink_pair(mid)
        filt_ref[p] = filt.astype(bf16)
        shrunk_ref[p] = shrunk
        for at, (kept, out) in enumerate(((hid_ref, hid_out), (slope_ref, slope_out), (shrunk_ref, shrunk_out))):
            copies.append(pltpu.make_async_copy(kept.at[p], out.at[p], sems.at[p, at]))
            copies[-1].start()
    turn_rows(filt_ref, points_ref, turn_inv_ref[...], swap_ref[...], chunk)
    pack_all(points_ref, send_ref)
    for copy in copies:
        copy.wait()


def mix_kernel(
    lat_rows, block_size, sub,
    box_ref, row_ref, recv_ref, token_ref, hole_ref, gain_ref, shift_ref,
    post_gain_ref, post_shift_ref, table_ref,
    mixed, post_ref,
):
    items, cells, width = token_ref.shape
    pad = post_ref.shape[1] - cells
    backs = [get_modes(recv_ref, item, block_size, sub) for item in range(items)]
    units = [norm_parts(token_ref[item].astype(f32))[0] for item in range(items)]
    for item in range(items):
        valid = as_column(valid_row(item, box_ref, row_ref, hole_ref, lat_rows, cells))
        normed = units[item] * line(gain_ref) + line(shift_ref)
        filtered = dot(table_ref[...], backs[item], 1, 0)
        value = token_ref[item].astype(f32) + normed + valid * filtered
        mixed[item] = value
        unit, _ = norm_parts(value)
        post_ref[item, :cells] = (unit * line(post_gain_ref) + line(post_shift_ref)).astype(bf16)
        if pad:
            post_ref[item, cells:] = jnp.zeros((pad, width), bf16)


def feed_kernel(
    cuts, runs, run,
    bit_ref, core_ref, post_own, post_other, cot_own, cot_other, expand_far, reduce_far, bias_ref,
    *refs,
):
    far_refs, refs = refs[:6], refs[6:]
    bias_grad, out_own, grad_own_ref, out_other_ref, grad_0_ref, grad_1_ref, *refs = refs
    post_ref, cot_ref, expand_ref, reduce_ref, hidden_ref, grad_ref, *refs = refs
    expand_grad_ref, reduce_grad_ref, row_sems, weight_sems, far_sems = refs
    rows = post_own.shape[0]
    arrivals = []
    for at, (source, to) in enumerate(((post_own, post_ref), (post_other, post_ref), (cot_own, cot_ref), (cot_other, cot_ref))):
        here = slice(at % 2 * rows, (at % 2 + 1) * rows)
        arrivals.append(pltpu.make_async_copy(source, to.at[here], row_sems.at[at]))
    fetches = []
    for r in range(runs):
        start = pl.multiple_of((2 * r + core_ref[0]) * run, 128)
        here, there = slice(r * run, (r + 1) * run), pl.ds(start, run)
        fetches.append(pltpu.make_async_copy(expand_far.at[:, there], expand_ref.at[:, here], weight_sems.at[0, r]))
        fetches.append(pltpu.make_async_copy(reduce_far.at[there], reduce_ref.at[here], weight_sems.at[1, r]))
    waves = [arrivals[:2] + fetches[:1], arrivals[2:] + fetches[1:2]] + [fetches[2 * r : 2 * r + 2] for r in range(1, runs)]

    def turn_over(at):
        for copy in waves[at]:
            copy.wait()
        for copy in waves[at + 1] if at + 1 < len(waves) else ():
            copy.start()

    for copy in waves[0]:
        copy.start()
    turn_over(0)
    post = post_ref[...]
    for r in range(runs):
        here = slice(r * run, (r + 1) * run)
        if r:
            turn_over(r + 1)
        start = pl.multiple_of((2 * r + core_ref[0]) * run, 128)
        pre = dot(post, expand_ref[:, here], 1, 0) + bias_ref[:, pl.ds(start, run)]
        hidden, slope = gelu_pair(pre)
        hidden_ref[:, here] = hidden.astype(bf16)
        if not r:
            turn_over(1)
        cot = cot_ref[...]
        grad = (dot(cot, reduce_ref[here], 1, 1) * slope).astype(bf16)
        grad_ref[:, here] = grad
        bias_grad.here[:, here] = jnp.sum(grad.astype(f32), axis=0, keepdims=True)
    bias_grad.start()

    for r in range(runs):
        here = slice(r * run, (r + 1) * run)
        expand_grad_ref[here] = dot(grad_ref[:, here], post, 0, 0).astype(bf16)
        reduce_grad_ref[here] = dot(hidden_ref[:, here], cot, 0, 0).astype(bf16)
    lanes = post.shape[1] // 3
    copies = []
    for group, (at, outer) in enumerate(cuts):
        inner = runs * run // (2 * outer)
        own = bit_ref[at]
        for side, source in enumerate((expand_grad_ref, reduce_grad_ref)):
            for o in range(outer):
                for target, half in enumerate((1 - own, own)):
                    start = pl.multiple_of((2 * o + half) * inner, 16)
                    part = source.at[pl.ds(start, inner), group * lanes : (group + 1) * lanes]
                    to = far_refs[2 * group + target].at[
                        o * inner : (o + 1) * inner, side * lanes : (side + 1) * lanes
                    ]
                    copies.append(pltpu.make_async_copy(part, to, far_sems.at[len(copies)]))
                    copies[-1].start()

    out = dot(hidden_ref[...], reduce_ref[...], 1, 0)
    out_own.here[...] = out[:rows]
    out_own.start()
    out_other_ref[...] = out[rows:].astype(bf16)
    back = dot(grad_ref[...], expand_ref[...], 1, 1)
    half = back.shape[1] // 2
    grad_own_ref[...] = back[:rows]
    grad_0_ref[...] = back[rows:, :half].astype(bf16)
    grad_1_ref[...] = back[rows:, half:].astype(bf16)
    for copy in copies:
        copy.wait()


def combine_kernel(places, bit_ref, *refs):
    groups = len(places)
    ins, outs = refs[: 2 * groups], refs[2 * groups :]
    for at, place in enumerate(places):
        keep, recv = ins[2 * at], ins[2 * at + 1]
        low_own = bit_ref[place] == 0
        first, second = keep[:, 0] + recv[:, 0], keep[:, 1] + recv[:, 1]
        outs[2 * at].here[...] = jnp.where(low_own, second, first)
        outs[2 * at].start()
        outs[2 * at + 1].here[...] = jnp.where(low_own, first, second)
        outs[2 * at + 1].start()


def shard_kernel(*refs):
    *ins, expand_ref, reduce_ref = refs
    lanes = ins[0].here.shape[1] // 2
    for at in range(len(ins) // 2):
        total = ins[2 * at][...].astype(f32) + ins[2 * at + 1][...].astype(f32)
        expand_ref[:, at * lanes : (at + 1) * lanes] = total[:, :lanes]
        reduce_ref[:, at * lanes : (at + 1) * lanes] = total[:, lanes:]


def both_halves(first_ref, second_ref, item, cells):
    return jnp.concatenate([first_ref[item, :cells], second_ref[item, :cells]], axis=1).astype(f32)


def result_kernel(mixed_ref, out_own_ref, out_other_ref, bias_ref, result_ref):
    items, cells, _ = result_ref.shape
    for item in range(items):
        out = out_own_ref[item, :cells] + out_other_ref[item, :cells].astype(f32)
        result_ref[item] = (mixed_ref[item] + (out + line(bias_ref))).astype(bf16)


def post_kernel(
    lat_rows, block_size, sub,
    box_ref, row_ref, mixed_ref, grad_own_ref, grad_0_ref, grad_1_ref, cot_ref, hole_ref, gain_ref, table_ref,
    grad_mixed, send_ref, sum_ref,
):
    items, cells, _ = grad_mixed.shape
    sums = 0.0
    for item in range(items):
        valid = valid_row(item, box_ref, row_ref, hole_ref, lat_rows, cells)
        grad = grad_own_ref[item, :cells] + both_halves(grad_0_ref, grad_1_ref, item, cells)
        unit, inv_scale = norm_parts(mixed_ref[item])
        cot = cot_ref[item, :cells].astype(f32)
        sums += jnp.concatenate([jnp.sum(v, axis=0, keepdims=True) for v in (grad * unit, grad, cot)], axis=0)
        value = cot + norm_back(grad, unit, inv_scale, line(gain_ref))
        grad_mixed[item] = value
        table = (table_ref[...].astype(f32) * valid).astype(bf16)
        put_modes(send_ref, item, dot(table, value.astype(bf16), 1, 0), block_size, sub)
    sum_ref[...] = sums


def small_kernel(layout, core_ref, post_sum_ref, expand_bias_ref, small_ref):
    per_run, runs, _ = layout
    small_ref[...] = jnp.zeros_like(small_ref)
    per_line = post_sum_ref.shape[1] // 128
    for line_at in range(3):
        for at in range(per_line):
            row = line_at * per_line + at
            small_ref[row : row + 1] = post_sum_ref[line_at : line_at + 1, at * 128 : (at + 1) * 128]
    for at in range(runs * per_run):
        row = (at // per_run * 2 + core_ref[0]) * per_run + at % per_run
        small_ref[pl.ds(3 * per_line + row, 1)] = expand_bias_ref[:, at * 128 : (at + 1) * 128]


def filter_back_kernel(
    chunk, bias_row, blocks, place_ref,
    recv_ref, spec_ref, hid_ref, slope_ref, shrunk_ref, inner_ref, outer_ref,
    turn_fwd_ref, turn_inv_ref, swap_ref, small_ref,
    send_ref, weight_send_ref, weight_keep_ref,
    turned_ref, grad_mid_ref, grad_pre_ref, points_ref,
):
    lat_count, points, wide = turned_ref.shape
    unpack_all(recv_ref, grad_mid_ref)
    turn_rows(grad_mid_ref, turned_ref, turn_fwd_ref[...], swap_ref[...], chunk)
    inner_bias = jnp.zeros((1, wide), f32)
    outer_bias = jnp.zeros((1, wide), f32)
    for p in range(lat_count):
        grad_mid = (turned_ref[p].astype(f32) * shrunk_ref[p]).astype(bf16)
        grad_mid_ref[p] = grad_mid
        outer_bias += jnp.sum(grad_mid.astype(f32), axis=0, keepdims=True)
        grad_pre = (dot(grad_mid, outer_ref[...], 1, 1) * slope_ref[p]).astype(bf16)
        grad_pre_ref[p] = grad_pre
        inner_bias += jnp.sum(grad_pre.astype(f32), axis=0, keepdims=True)
        turned_ref[p] = dot(grad_pre, inner_ref[...], 1, 1).astype(bf16)
    turn_rows(turned_ref, points_ref, turn_inv_ref[...], swap_ref[...], chunk)
    pack_all(points_ref, send_ref)
    flat = (lat_count * points, wide)
    half = wide // 2
    base = weight_keep_ref.shape[0] - small_ref.shape[0]
    own = place_ref[0]
    for at, (left, right) in enumerate(((spec_ref, grad_pre_ref), (hid_ref, grad_mid_ref))):
        grad = dot(left[...].reshape(flat), right[...].reshape(flat), 0, 0)
        first = grad[:half, :half] + grad[half:, half:]
        second = grad[:half, half:] - grad[half:, :half]
        top, rest = pack(jnp.concatenate([first, second], axis=1))

        @pl.when(own == at)
        def _():
            weight_keep_ref[:half] = top
            weight_keep_ref[half:base] = rest

        @pl.when(own != at)
        def _():
            weight_send_ref[:half] = top
            weight_send_ref[half:base] = rest

    weight_keep_ref[base:] = small_ref[...]
    for at, bias in enumerate((inner_bias, outer_bias)):
        for side in range(2):
            row = bias_row + (2 * at + side) * blocks + place_ref[1]
            weight_keep_ref[pl.ds(base + row, 1), :half] = bias[:, side * half : (side + 1) * half]
    weight_send_ref[base:] = weight_keep_ref[base:]


def last_kernel(
    lat_rows, block_size, sub,
    box_ref, row_ref, recv_ref, token_ref, grad_mixed_ref, hole_ref, gain_ref, table_ref,
    result_ref, tail,
):
    items, cells, width = token_ref.shape
    backs = [get_modes(recv_ref, item, block_size, sub) for item in range(items)]
    parts = [norm_parts(token_ref[item].astype(f32)) for item in range(items)]
    sums = 0.0
    grads = []
    for item in range(items):
        valid = as_column(valid_row(item, box_ref, row_ref, hole_ref, lat_rows, cells))
        grad = grad_mixed_ref[item] + valid * dot(table_ref[...], backs[item], 1, 0)
        grads.append(grad)
        sums += jnp.concatenate([jnp.sum(v, axis=0, keepdims=True) for v in (grad * parts[item][0], grad)], axis=0)

    per_line = width // 128
    pieces = [sums[i : i + 1, j * 128 : (j + 1) * 128] for i in range(2) for j in range(per_line)]
    pad = tail.shape[1] - 2 * per_line
    if pad:
        pieces.append(jnp.zeros((pad, 128), f32))
    value = jnp.concatenate(pieces, axis=0).astype(bf16)
    for device in range(tail.shape[0]):
        tail.here[device] = value
    tail.start()
    for item in range(items):
        unit, inv_scale = parts[item]
        result_ref[item] = grad_mixed_ref[item] + norm_back(grads[item], unit, inv_scale, line(gain_ref))


def put_split(ref, at, value):
    high = value.astype(bf16)
    rows = value.shape[0]
    ref[at : at + rows] = high
    ref[at + rows : at + 2 * rows] = (value - high.astype(f32)).astype(bf16)


def get_split(ref, rows):
    at = ref.shape[0] - 2 * rows
    return ref[at : at + rows].astype(f32) + ref[at + rows :].astype(f32)


def first_kernel(own_ref, recv_ref, send_ref, small_ref):
    rows = small_ref.shape[0]
    base = own_ref.shape[0] - rows
    send_ref[:base] = (own_ref[:base] + recv_ref[:base]).astype(bf16)
    total = own_ref[base:] + recv_ref[base:]
    small_ref[...] = total
    put_split(send_ref, base, total)


def second_kernel(own_ref, recv_ref, small_in_ref, send_ref, small_ref):
    rows = small_ref.shape[0]
    base = own_ref.shape[0] - 2 * rows
    send_ref[:base] = own_ref[:base]
    send_ref[base : 2 * base] = recv_ref[:base]
    total = small_in_ref[...] + get_split(recv_ref, rows)
    small_ref[...] = total
    put_split(send_ref, 2 * base, total)


def third_kernel(*refs):
    *parts, small_in_ref, weight_ref, small_ref = refs
    rows = small_ref.shape[0]
    both = parts[0].shape[0] - 2 * rows
    total = small_in_ref[...]
    for at, ref in enumerate(parts):
        weight_ref[at * both : (at + 1) * both] = ref[:both]
        if at:
            total += get_split(ref, rows)
    small_ref[...] = total


def tail_kernel(
    place_ref, tail_ref, small_ref, weight_ref, weight_other_ref,
    pre_gain_ref, pre_shift_ref, inner_ref, inner_bias_ref, outer_ref, outer_bias_ref,
    post_gain_ref, post_shift_ref, expand_bias_ref, reduce_bias_ref,
):
    per_line = pre_gain_ref.shape[0] // 128
    sums = jnp.sum(tail_ref[:, : 2 * per_line].astype(f32), axis=0)

    def put(ref, at, value):
        ref[pl.ds(at * 128, 128)] = value.reshape(128)

    for i, ref in enumerate((pre_gain_ref, pre_shift_ref)):
        for j in range(per_line):
            put(ref, j, sums[i * per_line + j : i * per_line + j + 1])

    def row(at):
        return small_ref[at : at + 1]

    at = 0
    for ref in (post_gain_ref, post_shift_ref, reduce_bias_ref, expand_bias_ref):
        for j in range(ref.shape[0] // 128):
            put(ref, j, row(at))
            at += 1
    _, blocks, size = inner_bias_ref.shape
    for ref in (inner_bias_ref, outer_bias_ref):
        for side in range(2):
            for block in range(blocks):
                ref[side, block : block + 1] = row(at)[:, :size]
                at += 1
    own = place_ref[0]
    for at in range(blocks):
        mine = unpack(weight_ref[at].astype(f32))
        theirs = unpack(weight_other_ref[at].astype(f32))
        inner, outer = jnp.where(own == 0, mine, theirs), jnp.where(own == 0, theirs, mine)
        block = at ^ place_ref[1]
        for side in range(2):
            inner_ref[side, block] = inner[:, side * size : (side + 1) * size]
            outer_ref[side, block] = outer[:, side * size : (side + 1) * size]


class Far:
    def __init__(self, far_ref, here_ref, sem, incoming):
        pair = (far_ref, here_ref) if incoming else (here_ref, far_ref)
        self.here, self.copy, self.pending = here_ref, pltpu.make_async_copy(*pair, sem), False
        if incoming:
            self.start()

    def start(self):
        self.copy.start()
        self.pending = True

    def wait(self):
        if self.pending:
            self.copy.wait()
            self.pending = False

    @property
    def shape(self):
        return self.here.shape

    def __getitem__(self, index):
        self.wait()
        return self.here[index]


def call(kernel, out_shape, args, prefetch=0, scratch=(), flops=0, vmem=16, after=(), far_in=(), far_out=(), raw=()):
    args, after = tuple(args), tuple(after)
    far_out = [len(args) + i for i in far_out]
    raw = set(i if i >= 0 else len(args) - 1 - i for i in raw)
    far = list(far_in) + far_out
    count = len(args) + len(out_shape)
    every = list(args) + list(out_shape)
    anywhere = pl.BlockSpec(memory_space=pl.ANY)

    def spec(i):
        if i in far or i in raw:
            return anywhere
        dims = every[i].shape
        rest = (0,) * len(dims)
        return pl.BlockSpec(tuple(dims), lambda *_: rest)

    def whole_kernel(*refs):
        refs = list(refs[: len(args)]) + list(refs[len(args) + len(after) :])
        sems = refs.pop() if far else None
        buffers = [refs.pop() for _ in far][::-1]
        fars = {}
        for at, i in enumerate(far):
            fars[i] = refs[i] = Far(refs[i], buffers[at], sems.at[at], i < len(args))
        kernel(*refs)
        for value in fars.values():
            value.wait()

    moved = sum(math.prod(a.shape) * np.dtype(a.dtype).itemsize for a in every)
    fixed = [pltpu.with_memory_space_constraint(a, pltpu.HBM) if i in far else a for i, a in enumerate(args)]
    shapes = [
        pltpu.HBM(a.shape, a.dtype) if i in far_out or i in raw else a for i, a in enumerate(out_shape, len(args))
    ]
    scratch = list(scratch) + [pltpu.VMEM(every[i].shape, every[i].dtype) for i in far]
    if far:
        scratch.append(pltpu.SemaphoreType.DMA((len(far),)))
    return pl.pallas_call(
        whole_kernel,
        out_shape=shapes,
        grid_spec=pltpu.PrefetchScalarGridSpec(
            num_scalar_prefetch=prefetch,
            grid=(1,),
            in_specs=[spec(i) for i in range(prefetch, len(args))] + [anywhere] * len(after),
            out_specs=[spec(i) for i in range(len(args), count)],
            scratch_shapes=scratch,
        ),
        compiler_params=pltpu.CompilerParams(
            dimension_semantics=("arbitrary",), vmem_limit_bytes=vmem << 20
        ),
        cost_estimate=pl.CostEstimate(flops=int(flops), bytes_accessed=int(moved), transcendentals=0),
    )(*fixed, *after)


def shape(dims, dtype):
    return jax.ShapeDtypeStruct(tuple(dims), dtype)


def stay(operand):
    return pltpu.with_memory_space_constraint(operand, pltpu.HBM)


def pair_swap(operand, axis_name, bit):
    size = lax.axis_size(axis_name)
    return lax.ppermute(operand, axis_name, [(i, i ^ bit) for i in range(size)])


def axis_bits(axis_name):
    size = lax.axis_size(axis_name)
    return [1 << i for i in range(size.bit_length() - 1)]


def body(
    tokens,
    boxes,
    patch_mask,
    pre_gain,
    pre_shift,
    filter_inner,
    filter_inner_bias,
    filter_outer,
    filter_outer_bias,
    post_gain,
    post_shift,
    expand_weight,
    expand_bias,
    reduce_weight,
    reduce_bias,
    cotangent,
):
    micro_count, crop_count, lat_rows, cells, width = tokens.shape
    groups = lax.axis_size("lat")
    lat_count = lat_rows * groups
    block_count, block_size = filter_inner.shape[1:3]
    sub = groups // block_count
    modes_own = MODES // sub
    crops = micro_count * crop_count
    items = crops * lat_rows
    points = crops * modes_own
    wide = 2 * block_size
    padded = -(-cells // 16) * 16
    rows = items * padded
    chunk = 16
    hidden_width = expand_weight.shape[1]
    dp_size = lax.axis_size("dp")
    lat_index, dp_index = lax.axis_index("lat"), lax.axis_index("dp")
    own_block = lat_index // sub
    tables = {k: jnp.asarray(v) for k, v in make_tables(cells, lat_count, block_size, chunk).items()}

    box = boxes
    own_row = (lat_index * lat_rows).astype(jnp.int32).reshape(1)
    core = dp_index % 2
    token_items = tokens.reshape(items, cells, width)
    cot_pad = jnp.pad(cotangent.reshape(items, cells, width), ((0, 0), (0, padded - cells), (0, 0)))
    holes = patch_mask.reshape(items, 1, cells)
    row_item = (items, cells, width)
    pad_item = (items, padded, width)
    packed = modes_own * 3 // 2
    mode_dims = (groups, items, packed, 128)
    names = (lat_rows, block_size, sub)
    lon_flops = 2 * items * 2 * MODES * cells * width

    def exchange(both, by_rows):
        if by_rows:
            both = both.reshape(groups, crops, lat_rows, packed, 128).swapaxes(1, 2)
            both = both.reshape(groups, items * packed, 128)
            both = lax.all_to_all(both, "lat", 0, 0, tiled=True)
            return both.reshape(lat_count, crops, packed, 128)
        both = both.reshape(groups, items * packed, 128)
        both = lax.all_to_all(both, "lat", 0, 0, tiled=True)
        both = both.reshape(groups, lat_rows, crops, packed, 128).swapaxes(1, 2)
        return both.reshape(mode_dims)

    def own_matrix(matrix):
        pair = lax.dynamic_index_in_dim(matrix, own_block, 1, keepdims=False)
        top = jnp.concatenate([pair[0], pair[1]], axis=1)
        under = jnp.concatenate([-pair[1], pair[0]], axis=1)
        return jnp.concatenate([top, under], axis=0)

    def own_bias(bias):
        return lax.dynamic_index_in_dim(bias, own_block, 1, keepdims=False).reshape(1, wide)

    args = (box, own_row, token_items, holes, pre_gain, pre_shift, tables["fwd"])
    (send,) = call(
        functools.partial(pre_kernel, *names),
        [shape(mode_dims, bf16)],
        args,
        prefetch=2,
        far_in=range(3, 7),
        flops=lon_flops,
    )
    recv = exchange(send, True)
    cot_other = pair_swap(cot_pad.reshape(rows, width), "dp", 1)

    spectrum = (lat_count, points, wide)
    grid_dims = (lat_count, crops, packed, 128)
    filter_flops = 4 * lat_count * points * wide * wide
    inner, outer = own_matrix(filter_inner), own_matrix(filter_outer)
    turns = (tables["turn_fwd"], tables["turn_inv"], tables["swap"])
    args = (recv, inner, own_bias(filter_inner_bias), outer, own_bias(filter_outer_bias), *turns)
    send, spec, hid, slope, shrunk = call(
        functools.partial(filter_kernel, chunk),
        [shape(grid_dims, bf16)] + [shape(spectrum, t) for t in (bf16, bf16, f32, f32)],
        args,
        far_in=(5, 6, 7),
        far_out=(1,),
        raw=(-3, -4, -5),
        scratch=[pltpu.VMEM(spectrum, t) for t in (bf16, f32, f32, bf16, bf16)]
        + [pltpu.SemaphoreType.DMA((lat_count, 3))],
        flops=filter_flops,
    )
    recv = exchange(send, False)

    args = (
        box, own_row, recv, token_items, holes, pre_gain, pre_shift, post_gain, post_shift, tables["inv_t"],
    )
    mixed, post = call(
        functools.partial(mix_kernel, *names),
        [shape(row_item, f32), shape(pad_item, bf16)],
        args,
        prefetch=2,
        far_in=range(4, 10),
        flops=lon_flops,
    )
    post = post.reshape(rows, width)
    post_other = pair_swap(post, "dp", 1)

    dp_bits = [("dp", b) for b in axis_bits("dp")[1:]]
    lat_bits = [("lat", b) for b in axis_bits("lat")]
    bit_names = dp_bits[::-1] + lat_bits[::-1]
    own_bits = jnp.stack([(lax.axis_index(n) // b) % 2 for n, b in bit_names]).astype(jnp.int32)
    own_rows = hidden_width // (dp_size * groups)
    half = hidden_width // 2
    run = hidden_width // dp_size
    runs = dp_size // 2
    core_bit = core.astype(jnp.int32).reshape(1)

    whole_rows = [n for n in lat_bits if own_rows * n[1] % 16 == 0]
    orders = [
        dp_bits + lat_bits,
        whole_rows[:1] + [n for n in lat_bits[:-1] if n != whole_rows[0]] + dp_bits + lat_bits[-1:],
        whole_rows[1:2] + dp_bits + [n for n in lat_bits if n != whole_rows[1]],
    ]
    lefts = [list(bit_names) for _ in orders]

    def place_of(step, left):
        return bit_names.index(step), 2 ** left.index(step)

    lanes = 2 * width // 3
    flat, double = (rows, width), (2 * rows, width)
    cuts = [place_of(order[0], left) for order, left in zip(orders, lefts)]
    copy_count = sum(4 * outer for _, outer in cuts)
    args = (
        own_bits, core_bit, post, post_other, cot_pad.reshape(rows, width), cot_other,
        stay(expand_weight), stay(reduce_weight), expand_bias.reshape(1, hidden_width),
    )
    *parts, grad_b, out_own, grad_own, out_other, grad_0, grad_1 = call(
        functools.partial(feed_kernel, cuts, runs, run),
        [shape((half // 2, lanes), bf16)] * 6
        + [shape((1, half), f32), shape(flat, f32), shape(flat, f32), shape(flat, bf16)]
        + [shape((rows, width // 2), bf16)] * 2,
        args,
        prefetch=2,
        far_in=(8,),
        far_out=(6, 7),
        raw=tuple(range(2, 8)) + tuple(range(-1, -7, -1)),
        scratch=[pltpu.VMEM(double, bf16)] * 2
        + [pltpu.VMEM((width, half), bf16), pltpu.VMEM((half, width), bf16)]
        + [pltpu.VMEM((2 * rows, half), bf16)] * 2
        + [pltpu.VMEM((half, width), bf16)] * 2
        + [pltpu.SemaphoreType.DMA((4,)), pltpu.SemaphoreType.DMA((2, runs))]
        + [pltpu.SemaphoreType.DMA((copy_count,))],
        flops=6 * 2 * 2 * rows * width * half,
        vmem=52,
    )
    others = [pair_swap(v, "dp", 1).reshape(items, padded, width // 2) for v in (grad_0, grad_1)]
    out_other = pair_swap(out_other, "dp", 1).reshape(pad_item)

    class Scatter:
        def __init__(self):
            self.at, self.sends, self.keeps = 0, list(parts[0::2]), list(parts[1::2])

        def swap(self):
            self.recvs = []
            for send, order, left in zip(self.sends, orders, lefts):
                left.remove(order[self.at])
                self.recvs.append(pair_swap(send, *order[self.at]))
            self.at += 1
            return list(self.recvs)

        def add(self, after=()):
            cuts = [place_of(order[self.at], left) for order, left in zip(orders, lefts)]
            left_rows = self.keeps[0].shape[0]
            dims = [(outer, 2, left_rows // (2 * outer), lanes) for _, outer in cuts]
            ins = [v.reshape(d) for keep, recv, d in zip(self.keeps, self.recvs, dims) for v in (keep, recv)]
            outs = call(
                functools.partial(combine_kernel, [place for place, _ in cuts]),
                [shape((d[0], d[2], lanes), bf16) for d in dims for _ in range(2)],
                (own_bits, *ins),
                prefetch=1,
                far_in=range(1, 7),
                far_out=range(6),
                after=after,
            )
            outs = [v.reshape(left_rows // 2, lanes) for v in outs]
            self.sends, self.keeps = outs[0::2], outs[1::2]
            return outs

    scatter = Scatter()
    scatter.swap()

    args = (
        box, own_row, mixed, grad_own.reshape(pad_item), *others, cot_pad, holes, post_gain, tables["inv"],
    )
    grad_mixed, send, post_sums = call(
        functools.partial(post_kernel, *names),
        [shape(row_item, f32), shape(mode_dims, bf16), shape((3, width), f32)],
        args,
        prefetch=2,
        far_in=(6, 7, 8, 9),
        flops=lon_flops,
    )
    (result,) = call(
        result_kernel,
        [shape(row_item, bf16)],
        (mixed, out_own.reshape(pad_item), out_other, reduce_bias),
        far_in=(1, 3),
        after=(send,),
    )
    recv = exchange(send, True)

    bias_row = 3 * width // 128 + hidden_width // 128
    small_rows = -(-(bias_row + 4 * block_count) // 16) * 16
    small_dims = (small_rows, 128)
    (small,) = call(
        functools.partial(small_kernel, (run // 128, runs, block_count)),
        [shape(small_dims, f32)],
        (core_bit, post_sums, grad_b),
        prefetch=1,
    )
    base = block_size * 3 // 2
    places = jnp.stack([core, own_block]).astype(jnp.int32)
    packed_weight = (base + small_rows, 128)
    args = (places, recv, spec, hid, slope, shrunk, inner, outer, *turns, small)
    send, weight_send, weight_keep = call(
        functools.partial(filter_back_kernel, chunk, bias_row, block_count),
        [shape(grid_dims, bf16)] + [shape(packed_weight, f32)] * 2,
        args,
        prefetch=1,
        far_in=(8, 9, 10, 5, 4, 2, 3),
        scratch=[pltpu.VMEM(spectrum, bf16)] * 4,
        flops=2 * filter_flops,
    )
    recv = exchange(send, False)

    weight = [weight_keep, pair_swap(weight_send, "dp", 1)]
    for step in dp_bits + [n for n in lat_bits if n[1] < sub]:
        weight = [weight[0] + weight[1]]
        weight.append(pair_swap(weight[0], *step))

    args = (box, own_row, recv, token_items, grad_mixed, holes, pre_gain, tables["fwd_t"])
    tail_dims = (dp_size * groups, -(-2 * width // 2048) * 16, 128)
    grad_tokens, tail = call(
        functools.partial(last_kernel, *names),
        [shape(row_item, f32), shape(tail_dims, bf16)],
        args,
        prefetch=2,
        far_in=(7, 5, 6),
        far_out=(1,),
        flops=lon_flops,
    )

    tail = lax.all_to_all(tail, ("dp", "lat"), 0, 0, tiled=True)
    gather_bits = [b for _, b in lat_bits if b >= sub]
    first_dims, second_dims = (base + 2 * small_rows, 128), (2 * base + 2 * small_rows, 128)
    while scatter.at < len(bit_names):
        stage = scatter.at
        if stage == 2:
            first, small = call(
                first_kernel, [shape(first_dims, bf16), shape(small_dims, f32)], weight, after=sums[:1]
            )
            first_recv = pair_swap(first, "lat", gather_bits[0])
        if stage == 3:
            second, small = call(
                second_kernel, [shape(second_dims, bf16), shape(small_dims, f32)], (first, first_recv, small),
                after=(grad_tokens,),
            )
            far_masks = [m * gather_bits[1] for m in range(1, block_count // 2)]
            second_recvs = [pair_swap(second, "lat", m) for m in far_masks]
            weight, small = call(
                third_kernel,
                [shape((block_count * base, 128), bf16), shape(small_dims, f32)],
                (second, *second_recvs, small),
            )
        ahead = {1: (send, weight[-1], result), 2: (grad_tokens,), 3: (tail, weight)}
        sums = scatter.add(ahead.get(stage, ()))
        scatter.swap()
    weight_other = pair_swap(weight, "dp", 1)
    merged = [v for pair in zip(scatter.keeps, scatter.recvs) for v in pair]
    expand_part, reduce_part = call(
        shard_kernel,
        [shape((own_rows, width), f32)] * 2,
        merged,
        far_in=range(6),
    )
    expand_part = expand_part.T

    rows_of = (block_size * 3 // 2, 128)
    args = (places, tail, small, weight.reshape(-1, *rows_of), weight_other.reshape(-1, *rows_of))
    line_dims = (width,)
    filter_dims, bias_dims = filter_inner.shape, filter_inner_bias.shape
    out_dims = [line_dims, line_dims, filter_dims, bias_dims, filter_dims, bias_dims]
    out_dims += [line_dims, line_dims, (hidden_width,), line_dims]
    sums = call(tail_kernel, [shape(d, f32) for d in out_dims], args, prefetch=1)
    return (
        result.reshape(tokens.shape),
        grad_tokens.reshape(tokens.shape),
        *sums[:8],
        expand_part,
        sums[8],
        reduce_part,
        sums[9],
    )


def solution(mesh):
    rows = P(None, "dp", "lat", None, None)
    in_specs = (rows, P(None, "dp", None), P(None, "dp", "lat", None)) + (P(),) * 12 + (rows,)
    out_specs = (
        (rows, rows)
        + (P(),) * 8
        + (P(None, ("dp", "lat")), P(), P(("dp", "lat"), None), P())
    )
    return jax.shard_map(body, mesh=mesh, in_specs=in_specs, out_specs=out_specs, check_vma=False)
```

```python
import functools
import math

import jax
import jax.numpy as jnp
import ml_dtypes
import numpy as np
from jax import lax
from jax.experimental import pallas as pl
from jax.experimental.pallas import tpu as pltpu
from jax.sharding import PartitionSpec as P

MODES = 64
GROUP = 2
COMBINE_FLOPS = 2 * 10**10
shrink_level = 0.01
epsilon = 1e-05
inv_root_two = 1.0 / math.sqrt(2.0)
inv_root_tau = 1.0 / math.sqrt(2.0 * math.pi)
f32 = jnp.float32
bf16 = jnp.bfloat16


def table_pair(out_count, in_count, length):
    phase = np.arange(out_count)[:, None] * np.arange(in_count)[None, :] % length
    angle = phase.astype(np.float32) * np.float32(2.0 * math.pi / length)
    return np.cos(angle).astype(np.float32), np.sin(angle).astype(np.float32)


def low(values):
    return values.astype(np.float32).astype(ml_dtypes.bfloat16)


def make_tables(lon_cells, lat_count, block_size, chunk):
    lon_factor = np.float32(1.0 / math.sqrt(lon_cells))
    cosine, sine = table_pair(MODES, lon_cells, lon_cells)
    weight = np.where(np.arange(MODES) == 0, 1.0, 2.0).astype(np.float32)[:, None]
    forward = low(np.concatenate([cosine, -sine]) * lon_factor)
    inverse = low(np.concatenate([cosine * weight, -sine * weight]) * lon_factor)
    cosine, sine = table_pair(lat_count, lat_count, lat_count)
    lat_factor = np.float32(1.0 / math.sqrt(lat_count))
    same = np.eye(chunk, dtype=np.float32)
    cosine = np.kron(low(cosine * lat_factor).astype(np.float32), same)
    sine = np.kron(low(sine * lat_factor).astype(np.float32), same)
    turn_fwd = low(np.concatenate([cosine, sine], axis=1))
    turn_inv = low(np.concatenate([cosine, -sine], axis=1))
    eye, none = np.eye(block_size), np.zeros((block_size, block_size))
    swap = low(np.block([[none, -eye], [eye, none]]))
    return dict(
        fwd=forward, fwd_t=forward.T.copy(), inv=inverse, inv_t=inverse.T.copy(),
        turn_fwd=turn_fwd, turn_inv=turn_inv, swap=swap,
    )


def dot(a, b, ca, cb):
    return lax.dot_general(a, b, (((ca,), (cb,)), ((), ())), preferred_element_type=f32)


def line(ref):
    return ref[...].reshape(1, -1)


def row_mean(values):
    return jnp.sum(values, axis=-1, keepdims=True) * (1.0 / values.shape[-1])


def norm_parts(values):
    centered = values - row_mean(values)
    inv_scale = lax.rsqrt(row_mean(centered * centered) + epsilon)
    return centered * inv_scale, inv_scale


def norm_back(grad_normed, unit_values, inv_scale, gain):
    grad_unit = grad_normed * gain
    plain, cross = row_mean(grad_unit), row_mean(grad_unit * unit_values)
    return inv_scale * (grad_unit - plain - unit_values * cross)


def gelu_pair(values):
    half = 0.5 * (1.0 + lax.erf(values * inv_root_two))
    return values * half, half + values * jnp.exp(-0.5 * values * values) * inv_root_tau


def shrink_pair(values):
    inverse = lax.rsqrt(values * values + shrink_level * shrink_level)
    slope = 1.0 - shrink_level * shrink_level * shrink_level * inverse * inverse * inverse
    return values - shrink_level * values * inverse, slope


def valid_row(item, box_ref, row_ref, hole_ref, lat_rows, cells):
    crop, row = item // lat_rows, row_ref[0] + item % lat_rows
    crop_count = box_ref.shape[1]
    micro, crop = crop // crop_count, crop % crop_count
    limit = jnp.where(row < box_ref[micro, crop, 0], box_ref[micro, crop, 1], 0)
    column = lax.broadcasted_iota(jnp.int32, (1, cells), 1)
    return jnp.where((column < limit) & (hole_ref[item] > 0), 1.0, 0.0)


def as_column(row):
    cells = row.shape[1]
    down = lax.broadcasted_iota(jnp.int32, (cells, cells), 0)
    along = lax.broadcasted_iota(jnp.int32, (cells, cells), 1)
    return jnp.sum(jnp.where(down == along, row, 0.0), axis=1, keepdims=True)


def pack(both):
    half = both.shape[0] // 2
    rest = both[:, 128:]
    return both[:, :128], jnp.concatenate([rest[:half], rest[half:]], axis=1)


def unpack(packed):
    points = packed.shape[0] * 2 // 3
    rest = packed[points:]
    rest = jnp.concatenate([rest[:, :64], rest[:, 64:]], axis=0)
    return jnp.concatenate([packed[:points], rest], axis=1)


def put_modes(send_ref, item, spectrum, block_size, sub):
    spectrum = spectrum.astype(bf16)
    own = MODES // sub
    for block in range(spectrum.shape[1] // block_size):
        cut = spectrum[:, block * block_size : (block + 1) * block_size]
        both = jnp.concatenate([cut[:MODES], cut[MODES:]], axis=1)
        for j in range(sub):
            top, rest = pack(both[j * own : (j + 1) * own])
            send_ref[block * sub + j, item, :own] = top
            send_ref[block * sub + j, item, own:] = rest


def get_modes(recv_ref, item, block_size, sub):
    groups = recv_ref.shape[0]
    real, imag = [], []
    for block in range(groups // sub):
        parts = [unpack(recv_ref[block * sub + j, item]) for j in range(sub)]
        both = parts[0] if sub == 1 else jnp.concatenate(parts, axis=0)
        real.append(both[:, :block_size])
        imag.append(both[:, block_size:])
    real, imag = jnp.concatenate(real, axis=1), jnp.concatenate(imag, axis=1)
    return jnp.concatenate([real, imag], axis=0)


def unpack_all(recv_ref, points_ref):
    lat_count, crops, packed, _ = recv_ref.shape
    own = packed * 2 // 3
    for p in range(lat_count):
        for crop in range(crops):
            points_ref[p, crop * own : (crop + 1) * own] = unpack(recv_ref[p, crop])


def pack_all(points_ref, send_ref):
    lat_count, crops, packed, _ = send_ref.shape
    own = packed * 2 // 3
    for p in range(lat_count):
        for crop in range(crops):
            top, rest = pack(points_ref[p, crop * own : (crop + 1) * own])
            send_ref[p, crop, :own] = top
            send_ref[p, crop, own:] = rest


def turn_rows(src_ref, dst_ref, table, swap, chunk):
    lat_count, points, wide = src_ref.shape
    for at in range(0, points, chunk):
        piece = src_ref[:, at : at + chunk, :].reshape(lat_count * chunk, wide)
        other = dot(piece, swap, 1, 0).astype(bf16)
        out = dot(table, jnp.concatenate([piece, other], axis=0), 1, 0)
        dst_ref[:, at : at + chunk, :] = out.astype(bf16).reshape(lat_count, chunk, wide)


def pre_kernel(
    lat_rows, block_size, sub,
    box_ref, row_ref, token_ref, hole_ref, gain_ref, shift_ref, table_ref,
    send_ref,
):
    items, cells, _ = token_ref.shape
    units = [norm_parts(token_ref[item].astype(f32))[0] for item in range(items)]
    for item in range(items):
        valid = valid_row(item, box_ref, row_ref, hole_ref, lat_rows, cells)
        normed = (units[item] * line(gain_ref) + line(shift_ref)).astype(bf16)
        table = (table_ref[...].astype(f32) * valid).astype(bf16)
        put_modes(send_ref, item, dot(table, normed, 1, 0), block_size, sub)


def filter_kernel(
    chunk,
    recv_ref, inner_ref, inner_bias_ref, outer_ref, outer_bias_ref, turn_fwd_ref, turn_inv_ref, swap_ref,
    send_ref, spec, hid_out, slope_out, shrunk_out,
    hid_ref, slope_ref, shrunk_ref, filt_ref, points_ref, sems,
):
    unpack_all(recv_ref, points_ref)
    spec_ref = spec.here
    turn_rows(points_ref, spec_ref, turn_fwd_ref[...], swap_ref[...], chunk)
    spec.start()
    copies = []
    lat_count, points, wide = spec_ref.shape
    for p in range(0, lat_count, GROUP):
        rows, dims = slice(p, p + GROUP), (GROUP, points, wide)
        pre = dot(spec_ref[rows].reshape(GROUP * points, wide), inner_ref[...], 1, 0) + inner_bias_ref[...]
        hid, slope = gelu_pair(pre)
        hid = hid.astype(bf16)
        hid_ref[rows] = hid.reshape(dims)
        slope_ref[rows] = slope.reshape(dims)
        mid = dot(hid, outer_ref[...], 1, 0) + outer_bias_ref[...]
        filt, shrunk = shrink_pair(mid)
        filt_ref[rows] = filt.astype(bf16).reshape(dims)
        shrunk_ref[rows] = shrunk.reshape(dims)
        for at, (kept, out) in enumerate(((hid_ref, hid_out), (slope_ref, slope_out), (shrunk_ref, shrunk_out))):
            copies.append(pltpu.make_async_copy(kept.at[rows], out.at[rows], sems.at[p, at]))
            copies[-1].start()
    turn_rows(filt_ref, points_ref, turn_inv_ref[...], swap_ref[...], chunk)
    pack_all(points_ref, send_ref)
    for copy in copies:
        copy.wait()


def mix_kernel(
    lat_rows, block_size, sub,
    box_ref, row_ref, recv_ref, token_ref, hole_ref, gain_ref, shift_ref,
    post_gain_ref, post_shift_ref, table_ref,
    mixed, post_ref,
):
    items, cells, width = token_ref.shape
    pad = post_ref.shape[1] - cells
    backs = [get_modes(recv_ref, item, block_size, sub) for item in range(items)]
    units = [norm_parts(token_ref[item].astype(f32))[0] for item in range(items)]
    for item in range(items):
        valid = as_column(valid_row(item, box_ref, row_ref, hole_ref, lat_rows, cells))
        normed = units[item] * line(gain_ref) + line(shift_ref)
        filtered = dot(table_ref[...], backs[item], 1, 0)
        value = token_ref[item].astype(f32) + normed + valid * filtered
        mixed[item] = value
        unit, _ = norm_parts(value)
        post_ref[item, :cells] = (unit * line(post_gain_ref) + line(post_shift_ref)).astype(bf16)
        if pad:
            post_ref[item, cells:] = jnp.zeros((pad, width), bf16)


def feed_kernel(
    cuts, shares, runs, run,
    bit_ref, core_ref, post_own, post_other, cot_own, cot_other, expand_far, reduce_far, bias_ref,
    *refs,
):
    far_refs, refs = refs[:6], refs[6:]
    bias_grad, out_own, grad_own, out_other_ref, grad_0_ref, grad_1_ref, *refs = refs
    post_ref, cot_ref, expand_ref, reduce_ref, hidden_ref, grad_ref, *refs = refs
    expand_grad_ref, reduce_grad_ref, row_sems, weight_sems, far_sems = refs
    rows = post_own.shape[0]
    arrivals = []
    for at, (source, to) in enumerate(((post_own, post_ref), (post_other, post_ref), (cot_own, cot_ref), (cot_other, cot_ref))):
        here = slice(at % 2 * rows, (at % 2 + 1) * rows)
        arrivals.append(pltpu.make_async_copy(source, to.at[here], row_sems.at[at]))
    fetches = []
    for r in range(runs):
        start = pl.multiple_of((2 * r + core_ref[0]) * run, 128)
        here, there = slice(r * run, (r + 1) * run), pl.ds(start, run)
        fetches.append(pltpu.make_async_copy(expand_far.at[:, there], expand_ref.at[:, here], weight_sems.at[0, r]))
        fetches.append(pltpu.make_async_copy(reduce_far.at[there], reduce_ref.at[here], weight_sems.at[1, r]))
    waves = [arrivals[:2] + fetches[:1], arrivals[2:] + fetches[1:2]] + [fetches[2 * r : 2 * r + 2] for r in range(1, runs)]

    def turn_over(at):
        for copy in waves[at]:
            copy.wait()
        for copy in waves[at + 1] if at + 1 < len(waves) else ():
            copy.start()

    for copy in waves[0]:
        copy.start()
    turn_over(0)
    post = post_ref[...]
    for r in range(runs):
        here = slice(r * run, (r + 1) * run)
        if r:
            turn_over(r + 1)
        start = pl.multiple_of((2 * r + core_ref[0]) * run, 128)
        pre = dot(post, expand_ref[:, here], 1, 0) + bias_ref[:, pl.ds(start, run)]
        hidden, slope = gelu_pair(pre)
        hidden_ref[:, here] = hidden.astype(bf16)
        if not r:
            turn_over(1)
        cot = cot_ref[...]
        grad = (dot(cot, reduce_ref[here], 1, 1) * slope).astype(bf16)
        grad_ref[:, here] = grad
        bias_grad.here[:, here] = jnp.sum(grad.astype(f32), axis=0, keepdims=True)
    bias_grad.start()

    for r in range(runs):
        here = slice(r * run, (r + 1) * run)
        expand_grad_ref[here] = dot(grad_ref[:, here], post, 0, 0).astype(bf16)
        reduce_grad_ref[here] = dot(hidden_ref[:, here], cot, 0, 0).astype(bf16)
    copies = []
    for group, (at, outer) in enumerate(cuts):
        inner = runs * run // (2 * outer)
        own = bit_ref[at]
        to_lanes = 0
        for side, source in enumerate((expand_grad_ref, reduce_grad_ref)):
            lanes = shares[side][group]
            from_lanes = sum(shares[side][:group])
            for o in range(outer):
                for target, half in enumerate((1 - own, own)):
                    start = pl.multiple_of((2 * o + half) * inner, 16)
                    part = source.at[pl.ds(start, inner), from_lanes : from_lanes + lanes]
                    to = far_refs[2 * group + target].at[o * inner : (o + 1) * inner, to_lanes : to_lanes + lanes]
                    copies.append(pltpu.make_async_copy(part, to, far_sems.at[len(copies)]))
                    copies[-1].start()
            to_lanes += lanes

    out = dot(hidden_ref[...], reduce_ref[...], 1, 0)
    out_own.here[...] = out[:rows]
    out_own.start()
    out_other_ref[...] = out[rows:].astype(bf16)
    back = dot(grad_ref[...], expand_ref[...], 1, 1)
    half = back.shape[1] // 2
    grad_own.here[...] = back[:rows]
    grad_own.start()
    grad_0_ref[...] = back[rows:, :half].astype(bf16)
    grad_1_ref[...] = back[rows:, half:].astype(bf16)
    for copy in copies:
        copy.wait()


def combine_kernel(places, bit_ref, *refs):
    groups = len(places)
    ins, outs = refs[: 2 * groups], refs[2 * groups :]
    for at, place in enumerate(places):
        keep, recv = ins[2 * at], ins[2 * at + 1]
        low_own = bit_ref[place] == 0
        first, second = keep[:, 0] + recv[:, 0], keep[:, 1] + recv[:, 1]
        outs[2 * at].here[...] = jnp.where(low_own, second, first)
        outs[2 * at].start()
        outs[2 * at + 1].here[...] = jnp.where(low_own, first, second)
        outs[2 * at + 1].start()


def shard_kernel(shares, *refs):
    *ins, expand_ref, reduce_ref = refs
    starts = [0, 0]
    for at in range(len(ins) // 2):
        total = ins[2 * at][...].astype(f32) + ins[2 * at + 1][...].astype(f32)
        begin = 0
        for side, ref in enumerate((expand_ref, reduce_ref)):
            lanes = shares[side][at]
            ref[:, starts[side] : starts[side] + lanes] = total[:, begin : begin + lanes]
            starts[side] += lanes
            begin += lanes


def both_halves(first_ref, second_ref, item, cells):
    return jnp.concatenate([first_ref[item, :cells], second_ref[item, :cells]], axis=1).astype(f32)


def result_kernel(mixed_ref, out_own_ref, out_other_ref, bias_ref, result_ref):
    cells, items, _ = result_ref.shape
    for item in range(items):
        out = out_own_ref[item, :cells] + out_other_ref[item, :cells].astype(f32)
        value = (mixed_ref[item] + (out + line(bias_ref))).astype(bf16)
        result_ref[:, item, :] = value


def post_kernel(
    lat_rows, block_size, sub,
    box_ref, row_ref, mixed_ref, grad_own_ref, grad_0_ref, grad_1_ref, cot_ref, hole_ref, gain_ref, table_ref,
    grad_mixed, send_ref, sum_ref, mixed_grad_ref, sems,
):
    items, cells, _ = mixed_grad_ref.shape
    sums = 0.0
    copies = []
    parts = [norm_parts(mixed_ref[item]) for item in range(items)]
    for item in range(items):
        unit, inv_scale = parts[item]
        grad = grad_own_ref[item, :cells] + both_halves(grad_0_ref, grad_1_ref, item, cells)
        cot = cot_ref[item, :cells].astype(f32)
        sums += jnp.concatenate([jnp.sum(v, axis=0, keepdims=True) for v in (grad * unit, grad, cot)], axis=0)
        value = cot + norm_back(grad, unit, inv_scale, line(gain_ref))
        mixed_grad_ref[item] = value
        copies.append(pltpu.make_async_copy(mixed_grad_ref.at[item], grad_mixed.at[item], sems.at[item]))
        copies[-1].start()
        valid = valid_row(item, box_ref, row_ref, hole_ref, lat_rows, cells)
        table = (table_ref[...].astype(f32) * valid).astype(bf16)
        put_modes(send_ref, item, dot(table, value.astype(bf16), 1, 0), block_size, sub)
    sum_ref[...] = sums
    for copy in copies:
        copy.wait()


def small_kernel(layout, core_ref, post_sum_ref, expand_bias_ref, small_ref):
    per_run, runs, _ = layout
    small_ref[...] = jnp.zeros_like(small_ref)
    per_line = post_sum_ref.shape[1] // 128
    for line_at in range(3):
        for at in range(per_line):
            row = line_at * per_line + at
            small_ref[row : row + 1] = post_sum_ref[line_at : line_at + 1, at * 128 : (at + 1) * 128]
    for at in range(runs * per_run):
        row = (at // per_run * 2 + core_ref[0]) * per_run + at % per_run
        small_ref[pl.ds(3 * per_line + row, 1)] = expand_bias_ref[:, at * 128 : (at + 1) * 128]


def filter_back_kernel(
    chunk,
    recv_ref, slope_ref, shrunk_ref, inner_ref, outer_ref, turn_fwd_ref, turn_inv_ref, swap_ref,
    send_ref, grad_mid, grad_pre, bias_ref,
    turned_ref, points_ref,
):
    lat_count, points, wide = turned_ref.shape
    grad_mid_ref, grad_pre_ref = grad_mid.here, grad_pre.here
    unpack_all(recv_ref, points_ref)
    turn_rows(points_ref, turned_ref, turn_fwd_ref[...], swap_ref[...], chunk)
    inner_bias = jnp.zeros((1, wide), f32)
    outer_bias = jnp.zeros((1, wide), f32)
    for p in range(0, lat_count, GROUP):
        rows, dims, flat = slice(p, p + GROUP), (GROUP, points, wide), (GROUP * points, wide)
        mid = (turned_ref[rows].astype(f32) * shrunk_ref[rows]).astype(bf16).reshape(flat)
        grad_mid_ref[rows] = mid.reshape(dims)
        outer_bias += jnp.sum(mid.astype(f32), axis=0, keepdims=True)
        pre = (dot(mid, outer_ref[...], 1, 1) * slope_ref[rows].reshape(flat)).astype(bf16)
        grad_pre_ref[rows] = pre.reshape(dims)
        inner_bias += jnp.sum(pre.astype(f32), axis=0, keepdims=True)
        turned_ref[rows] = dot(pre, inner_ref[...], 1, 1).astype(bf16).reshape(dims)
    grad_mid.start()
    grad_pre.start()
    turn_rows(turned_ref, points_ref, turn_inv_ref[...], swap_ref[...], chunk)
    pack_all(points_ref, send_ref)
    bias_ref[0:1] = inner_bias
    bias_ref[1:2] = outer_bias


def filter_weight_kernel(
    bias_row, blocks, place_ref, spec_ref, hid_ref, grad_mid_ref, grad_pre_ref, bias_ref, small_in_ref,
    send_ref, keep_ref, small_ref,
):
    lat_count, points, wide = spec_ref.shape
    flat, half = (lat_count * points, wide), wide // 2
    own = place_ref[0]
    count = small_ref.shape[0] // 2
    base = keep_ref.shape[0] - count
    small_ref[...] = small_in_ref[...]
    for at in range(2):
        for side in range(2):
            row = bias_row + (2 * at + side) * blocks + place_ref[1]
            small_ref[pl.ds(row, 1), :half] = bias_ref[at : at + 1, side * half : (side + 1) * half]
    for at, (left, right) in enumerate(((spec_ref, grad_pre_ref), (hid_ref, grad_mid_ref))):
        grad = dot(left[...].reshape(flat), right[...].reshape(flat), 0, 0)
        first = grad[:half, :half] + grad[half:, half:]
        second = grad[:half, half:] - grad[half:, :half]
        top, rest = pack(jnp.concatenate([first, second], axis=1))
        share = small_ref[at * count : (at + 1) * count]

        @pl.when(own == at)
        def _():
            keep_ref[:half] = top
            keep_ref[half:base] = rest
            keep_ref[base:] = share

        @pl.when(own != at)
        def _():
            send_ref[:half] = top
            send_ref[half:base] = rest
            send_ref[base:] = share


def halve_kernel(base, place_ref, own_ref, recv_ref, send_ref, keep_ref):
    low_own = place_ref[2] == 0
    total = own_ref[...] + recv_ref[...]
    at = 0
    for begin, end in ((0, base), (base, total.shape[0])):
        count = (end - begin) // 2
        first, second = total[begin : begin + count], total[begin + count : end]
        send_ref[at : at + count] = jnp.where(low_own, second, first)
        keep_ref[at : at + count] = jnp.where(low_own, first, second)
        at += count


def last_sums_kernel(
    lat_rows, block_size, sub, base,
    box_ref, row_ref, recv_ref, token_ref, grad_mixed_ref, hole_ref, table_ref, own_ref, other_ref,
    tail,
):
    items, cells, width = token_ref.shape
    backs = [get_modes(recv_ref, item, block_size, sub) for item in range(items)]
    units = [norm_parts(token_ref[item].astype(f32))[0] for item in range(items)]
    sums = 0.0
    for item in range(items):
        valid = as_column(valid_row(item, box_ref, row_ref, hole_ref, lat_rows, cells))
        grad = grad_mixed_ref[item] + valid * dot(table_ref[...], backs[item], 1, 0)
        sums += jnp.concatenate([jnp.sum(v, axis=0, keepdims=True) for v in (grad * units[item], grad)], axis=0)

    rows = own_ref.shape[0] - base
    total = own_ref[...] + other_ref[...]
    value_ref = tail.here.at[0]
    value_ref[:base] = total[:base].astype(bf16)
    put_split(value_ref, base, total[base:])
    per_line, at = width // 128, base + 2 * rows
    value_ref[at:] = jnp.zeros((value_ref.shape[0] - at, 128), bf16)
    for i in range(2):
        for j in range(per_line):
            row = at + i * per_line + j
            value_ref[row : row + 1] = sums[i : i + 1, j * 128 : (j + 1) * 128].astype(bf16)
    value = value_ref[...]
    for group in range(1, tail.shape[0]):
        tail.here[group] = value
    tail.start()


def last_kernel(
    lat_rows, block_size, sub,
    box_ref, row_ref, recv_ref, token_ref, grad_mixed_ref, hole_ref, gain_ref, table_ref,
    result, result_ref, sems,
):
    items, cells, width = token_ref.shape
    copies = []
    for item in range(items):
        back = get_modes(recv_ref, item, block_size, sub)
        unit, inv_scale = norm_parts(token_ref[item].astype(f32))
        valid = as_column(valid_row(item, box_ref, row_ref, hole_ref, lat_rows, cells))
        grad = grad_mixed_ref[item] + valid * dot(table_ref[...], back, 1, 0)
        value = grad_mixed_ref[item] + norm_back(grad, unit, inv_scale, line(gain_ref))
        result_ref[item] = value[:, None, :]
        copies.append(pltpu.make_async_copy(result_ref.at[item], result.at[item], sems.at[item]))
        copies[-1].start()
    for copy in copies:
        copy.wait()


def put_split(ref, at, value):
    high = value.astype(bf16)
    rows = value.shape[0]
    ref[at : at + rows] = high
    ref[at + rows : at + 2 * rows] = (value - high.astype(f32)).astype(bf16)


def get_split(ref, at, rows):
    return ref[at : at + rows].astype(f32) + ref[at + rows : at + 2 * rows].astype(f32)


def third_kernel(sub, rows, pre_rows, recv_ref, *refs):
    *other_refs, out_ref = refs
    groups, total_rows, _ = recv_ref.shape
    base = total_rows - 2 * rows - pre_rows
    blocks = groups // sub
    total = 0.0
    for block in range(blocks):
        part = recv_ref[block * sub]
        out_ref[block * base : (block + 1) * base] = part[:base]
        total += part[base : base + rows].astype(f32) + part[base + rows : base + 2 * rows].astype(f32)
    put_split(out_ref, blocks * base, total)
    total = jnp.sum(recv_ref[:, base + 2 * rows :].astype(f32), axis=0)
    for ref in other_refs:
        total += jnp.sum(ref[...].astype(f32), axis=0)
    put_split(out_ref, blocks * base + 2 * rows, total)


def join_kernel(*refs):
    *parts, out_ref = refs
    rows = parts[0].shape[0]
    for at, ref in enumerate(parts):
        out_ref[at * rows : (at + 1) * rows] = ref[...]


def tail_kernel(
    count, rows, pre_rows, place_ref, *refs,
):
    parts, refs = list(refs[:count]), refs[count:]
    joined = parts.pop()
    size = parts[0].shape[0]
    parts += [joined.at[at * size : (at + 1) * size] for at in range(len(parts))]
    count = len(parts)
    (
        pre_gain_ref, pre_shift_ref, inner_ref, inner_bias_ref, outer_ref, outer_bias_ref,
        post_gain_ref, post_shift_ref, expand_bias_ref, reduce_bias_ref, small_ref,
    ) = refs
    own, y_own = place_ref[0], place_ref[2]

    def in_order(values):
        if count == 4:
            pairs = [values[0:2], values[2:4]]
            sides = [
                [jnp.where(y_own == 0, a, b), jnp.where(y_own == 0, b, a)] for a, b in pairs
            ]
        else:
            sides = [values[0:1], values[1:2]]
        joined = [jnp.concatenate(side, axis=0) if len(side) > 1 else side[0] for side in sides]
        return jnp.where(own == 0, joined[0], joined[1]), jnp.where(own == 0, joined[1], joined[0])

    pre_at = parts[0].shape[0] - 2 * pre_rows
    small_at = pre_at - 2 * rows
    for at, value in enumerate(in_order([get_split(ref, small_at, rows) for ref in parts])):
        small_ref[at * value.shape[0] : (at + 1) * value.shape[0]] = value
    per_line = pre_gain_ref.shape[0] // 128
    sums = sum(get_split(ref, pre_at, pre_rows) for ref in parts)

    def put(ref, at, value):
        ref[pl.ds(at * 128, 128)] = value.reshape(128)

    for i, ref in enumerate((pre_gain_ref, pre_shift_ref)):
        for j in range(per_line):
            put(ref, j, sums[i * per_line + j : i * per_line + j + 1])

    def row(at):
        return small_ref[at : at + 1]

    at = 0
    for ref in (post_gain_ref, post_shift_ref, reduce_bias_ref, expand_bias_ref):
        for j in range(ref.shape[0] // 128):
            put(ref, j, row(at))
            at += 1
    _, blocks, size = inner_bias_ref.shape
    for ref in (inner_bias_ref, outer_bias_ref):
        for side in range(2):
            for block in range(blocks):
                ref[side, block : block + 1] = row(at)[:, :size]
                at += 1
    base = small_at // blocks
    for at in range(blocks):
        cuts = [ref[at * base : (at + 1) * base].astype(f32) for ref in parts]
        for ref, value in zip((inner_ref, outer_ref), in_order(cuts)):
            value = unpack(value)
            for side in range(2):
                ref[side, at] = value[:, side * size : (side + 1) * size]


class Far:
    def __init__(self, far_ref, here_ref, sem, incoming):
        pair = (far_ref, here_ref) if incoming else (here_ref, far_ref)
        self.here, self.copy, self.pending = here_ref, pltpu.make_async_copy(*pair, sem), False
        if incoming:
            self.start()

    def start(self):
        self.copy.start()
        self.pending = True

    def wait(self):
        if self.pending:
            self.copy.wait()
            self.pending = False

    @property
    def shape(self):
        return self.here.shape

    def __getitem__(self, index):
        self.wait()
        return self.here[index]


def call(kernel, out_shape, args, prefetch=0, scratch=(), flops=0, vmem=16, after=(), far_in=(), far_out=(), raw=()):
    args, after = tuple(args), tuple(after)
    far_out = [len(args) + i for i in far_out]
    raw = set(i if i >= 0 else len(args) - 1 - i for i in raw)
    far = list(far_in) + far_out
    count = len(args) + len(out_shape)
    every = list(args) + list(out_shape)
    anywhere = pl.BlockSpec(memory_space=pl.ANY)

    def spec(i):
        if i in far or i in raw:
            return anywhere
        dims = every[i].shape
        rest = (0,) * len(dims)
        return pl.BlockSpec(tuple(dims), lambda *_: rest)

    def whole_kernel(*refs):
        refs = list(refs[: len(args)]) + list(refs[len(args) + len(after) :])
        sems = refs.pop() if far else None
        buffers = [refs.pop() for _ in far][::-1]
        fars = {}
        for at, i in enumerate(far):
            fars[i] = refs[i] = Far(refs[i], buffers[at], sems.at[at], i < len(args))
        kernel(*refs)
        for value in fars.values():
            value.wait()

    moved = sum(math.prod(a.shape) * np.dtype(a.dtype).itemsize for a in every)
    fixed = [pltpu.with_memory_space_constraint(a, pltpu.HBM) if i in far else a for i, a in enumerate(args)]
    shapes = [
        pltpu.HBM(a.shape, a.dtype) if i in far_out or i in raw else a for i, a in enumerate(out_shape, len(args))
    ]
    scratch = list(scratch) + [pltpu.VMEM(every[i].shape, every[i].dtype) for i in far]
    if far:
        scratch.append(pltpu.SemaphoreType.DMA((len(far),)))
    return pl.pallas_call(
        whole_kernel,
        out_shape=shapes,
        grid_spec=pltpu.PrefetchScalarGridSpec(
            num_scalar_prefetch=prefetch,
            grid=(1,),
            in_specs=[spec(i) for i in range(prefetch, len(args))] + [anywhere] * len(after),
            out_specs=[spec(i) for i in range(len(args), count)],
            scratch_shapes=scratch,
        ),
        compiler_params=pltpu.CompilerParams(
            dimension_semantics=("arbitrary",), vmem_limit_bytes=vmem << 20
        ),
        cost_estimate=pl.CostEstimate(flops=int(flops), bytes_accessed=int(moved), transcendentals=0),
    )(*fixed, *after)


def shape(dims, dtype):
    return jax.ShapeDtypeStruct(tuple(dims), dtype)


def stay(operand):
    return pltpu.with_memory_space_constraint(operand, pltpu.HBM)


def pair_swap(operand, axis_name, bit):
    size = lax.axis_size(axis_name)
    return lax.ppermute(operand, axis_name, [(i, i ^ bit) for i in range(size)])


def axis_bits(axis_name):
    size = lax.axis_size(axis_name)
    return [1 << i for i in range(size.bit_length() - 1)]


def body(
    tokens,
    boxes,
    patch_mask,
    pre_gain,
    pre_shift,
    filter_inner,
    filter_inner_bias,
    filter_outer,
    filter_outer_bias,
    post_gain,
    post_shift,
    expand_weight,
    expand_bias,
    reduce_weight,
    reduce_bias,
    cotangent,
):
    micro_count, crop_count, lat_rows, cells, width = tokens.shape
    groups = lax.axis_size("lat")
    lat_count = lat_rows * groups
    block_count, block_size = filter_inner.shape[1:3]
    sub = groups // block_count
    modes_own = MODES // sub
    crops = micro_count * crop_count
    items = crops * lat_rows
    points = crops * modes_own
    wide = 2 * block_size
    padded = -(-cells // 16) * 16
    rows = items * padded
    chunk = 16
    hidden_width = expand_weight.shape[1]
    dp_size = lax.axis_size("dp")
    lat_index, dp_index = lax.axis_index("lat"), lax.axis_index("dp")
    own_block = lat_index // sub
    tables = {k: jnp.asarray(v) for k, v in make_tables(cells, lat_count, block_size, chunk).items()}

    box = boxes
    own_row = (lat_index * lat_rows).astype(jnp.int32).reshape(1)
    core = dp_index % 2
    token_items = tokens.reshape(items, cells, width)
    cot_pad = jnp.pad(cotangent.reshape(items, cells, width), ((0, 0), (0, padded - cells), (0, 0)))
    holes = patch_mask.reshape(items, 1, cells)
    row_item = (items, cells, width)
    pad_item = (items, padded, width)
    packed = modes_own * 3 // 2
    mode_dims = (groups, items, packed, 128)
    names = (lat_rows, block_size, sub)
    lon_flops = 2 * items * 2 * MODES * cells * width

    def exchange(both, by_rows):
        if by_rows:
            both = both.reshape(groups, crops, lat_rows, packed, 128).swapaxes(1, 2)
            both = both.reshape(groups, items * packed, 128)
            both = lax.all_to_all(both, "lat", 0, 0, tiled=True)
            return both.reshape(lat_count, crops, packed, 128)
        both = both.reshape(groups, items * packed, 128)
        both = lax.all_to_all(both, "lat", 0, 0, tiled=True)
        both = both.reshape(groups, lat_rows, crops, packed, 128).swapaxes(1, 2)
        return both.reshape(mode_dims)

    def own_matrix(matrix):
        pair = lax.dynamic_index_in_dim(matrix, own_block, 1, keepdims=False)
        top = jnp.concatenate([pair[0], pair[1]], axis=1)
        under = jnp.concatenate([-pair[1], pair[0]], axis=1)
        return jnp.concatenate([top, under], axis=0)

    def own_bias(bias):
        return lax.dynamic_index_in_dim(bias, own_block, 1, keepdims=False).reshape(1, wide)

    args = (box, own_row, token_items, holes, pre_gain, pre_shift, tables["fwd"])
    (send,) = call(
        functools.partial(pre_kernel, *names),
        [shape(mode_dims, bf16)],
        args,
        prefetch=2,
        far_in=range(3, 7),
        flops=lon_flops,
    )
    recv = exchange(send, True)
    cot_other = pair_swap(cot_pad.reshape(rows, width), "dp", 1)

    spectrum = (lat_count, points, wide)
    grid_dims = (lat_count, crops, packed, 128)
    filter_flops = 4 * lat_count * points * wide * wide
    inner, outer = own_matrix(filter_inner), own_matrix(filter_outer)
    turns = (tables["turn_fwd"], tables["turn_inv"], tables["swap"])
    args = (recv, inner, own_bias(filter_inner_bias), outer, own_bias(filter_outer_bias), *turns)
    send, spec, hid, slope, shrunk = call(
        functools.partial(filter_kernel, chunk),
        [shape(grid_dims, bf16)] + [shape(spectrum, t) for t in (bf16, bf16, f32, f32)],
        args,
        far_in=(5, 6, 7),
        far_out=(1,),
        raw=(-3, -4, -5),
        scratch=[pltpu.VMEM(spectrum, t) for t in (bf16, f32, f32, bf16, bf16)]
        + [pltpu.SemaphoreType.DMA((lat_count, 3))],
        flops=filter_flops,
    )
    recv = exchange(send, False)

    args = (
        box, own_row, recv, token_items, holes, pre_gain, pre_shift, post_gain, post_shift, tables["inv_t"],
    )
    mixed, post = call(
        functools.partial(mix_kernel, *names),
        [shape(row_item, f32), shape(pad_item, bf16)],
        args,
        prefetch=2,
        far_in=range(4, 10),
        flops=lon_flops,
    )
    post = post.reshape(rows, width)
    post_other = pair_swap(post, "dp", 1)

    dp_bits = [("dp", b) for b in axis_bits("dp")[1:]]
    lat_bits = [("lat", b) for b in axis_bits("lat")]
    bit_names = dp_bits[::-1] + lat_bits[::-1]
    own_bits = jnp.stack([(lax.axis_index(n) // b) % 2 for n, b in bit_names]).astype(jnp.int32)
    own_rows = hidden_width // (dp_size * groups)
    half = hidden_width // 2
    run = hidden_width // dp_size
    runs = dp_size // 2
    core_bit = core.astype(jnp.int32).reshape(1)

    whole_rows = [n for n in lat_bits if own_rows * n[1] % 16 == 0]
    orders = [
        dp_bits + lat_bits,
        whole_rows[:1] + [n for n in lat_bits[:-1] if n != whole_rows[0]] + dp_bits + lat_bits[-1:],
        whole_rows[1:2] + dp_bits + [n for n in lat_bits if n != whole_rows[1]],
    ]
    lefts = [list(bit_names) for _ in orders]

    def place_of(step, left):
        return bit_names.index(step), 2 ** left.index(step)

    third = width // 3
    shares = ((third * 3 // 2, third, third // 2), (third,) * 3)
    lanes = [a + b for a, b in zip(*shares)]
    flat, double = (rows, width), (2 * rows, width)
    cuts = [place_of(order[0], left) for order, left in zip(orders, lefts)]
    copy_count = sum(4 * outer for _, outer in cuts)
    args = (
        own_bits, core_bit, post, post_other, cot_pad.reshape(rows, width), cot_other,
        stay(expand_weight), stay(reduce_weight), expand_bias.reshape(1, hidden_width),
    )
    *parts, grad_b, out_own, grad_own, out_other, grad_0, grad_1 = call(
        functools.partial(feed_kernel, cuts, shares, runs, run),
        [shape((half // 2, n), bf16) for n in lanes for _ in range(2)]
        + [shape((1, half), f32), shape(flat, f32), shape(flat, f32), shape(flat, bf16)]
        + [shape((rows, width // 2), bf16)] * 2,
        args,
        prefetch=2,
        far_in=(8,),
        far_out=(6, 7, 8),
        raw=tuple(range(2, 8)) + tuple(range(-1, -7, -1)),
        scratch=[pltpu.VMEM(double, bf16)] * 2
        + [pltpu.VMEM((width, half), bf16), pltpu.VMEM((half, width), bf16)]
        + [pltpu.VMEM((2 * rows, half), bf16)] * 2
        + [pltpu.VMEM((half, width), bf16)] * 2
        + [pltpu.SemaphoreType.DMA((4,)), pltpu.SemaphoreType.DMA((2, runs))]
        + [pltpu.SemaphoreType.DMA((copy_count,))],
        flops=6 * 2 * 2 * rows * width * half,
        vmem=52,
    )
    others = [pair_swap(v, "dp", 1).reshape(items, padded, width // 2) for v in (grad_0, grad_1)]
    out_other = pair_swap(out_other, "dp", 1).reshape(pad_item)

    class Scatter:
        def __init__(self):
            self.at, self.sends, self.keeps = 0, list(parts[0::2]), list(parts[1::2])

        def swap(self):
            self.recvs = []
            for send, order, left in zip(self.sends, orders, lefts):
                left.remove(order[self.at])
                self.recvs.append(pair_swap(send, *order[self.at]))
            self.at += 1
            return list(self.recvs)

        def add(self, after=(), flops=0):
            cuts = [place_of(order[self.at], left) for order, left in zip(orders, lefts)]
            left_rows = self.keeps[0].shape[0]
            dims = [(outer, 2, left_rows // (2 * outer), n) for (_, outer), n in zip(cuts, lanes)]
            ins = [v.reshape(d) for keep, recv, d in zip(self.keeps, self.recvs, dims) for v in (keep, recv)]
            outs = call(
                functools.partial(combine_kernel, [place for place, _ in cuts]),
                [shape((d[0], d[2], d[3]), bf16) for d in dims for _ in range(2)],
                (own_bits, *ins),
                prefetch=1,
                far_in=range(1, 7),
                far_out=range(6),
                after=after,
                flops=flops,
            )
            outs = [v.reshape(left_rows // 2, v.shape[-1]) for v in outs]
            self.sends, self.keeps = outs[0::2], outs[1::2]
            return outs

    scatter = Scatter()
    scatter.swap()

    args = (
        box, own_row, mixed, grad_own.reshape(pad_item), *others, cot_pad, holes, post_gain, tables["inv"],
    )
    grad_mixed, send, post_sums = call(
        functools.partial(post_kernel, *names),
        [shape(row_item, f32), shape(mode_dims, bf16), shape((3, width), f32)],
        args,
        prefetch=2,
        far_in=(3, 6, 8, 9, 7),
        raw=(-1,),
        scratch=[pltpu.VMEM(row_item, f32), pltpu.SemaphoreType.DMA((items,))],
        flops=lon_flops,
    )
    (result,) = call(
        result_kernel,
        [shape((cells, items, width), bf16)],
        (mixed, out_own.reshape(pad_item), out_other, reduce_bias),
        far_in=(1, 3),
        after=(send,),
    )
    recv = exchange(send, True)

    sums = scatter.add((send,), flops=COMBINE_FLOPS)
    scatter.swap()

    bias_row = 3 * width // 128 + hidden_width // 128
    small_rows = -(-(bias_row + 4 * block_count) // 32) * 32
    small_dims = (small_rows, 128)
    (small,) = call(
        functools.partial(small_kernel, (run // 128, runs, block_count)),
        [shape(small_dims, f32)],
        (core_bit, post_sums, grad_b),
        prefetch=1,
    )
    base = block_size * 3 // 2
    y_index = (dp_index // 2) % 2
    places = jnp.stack([core, own_block, y_index]).astype(jnp.int32)
    args = (recv, slope, shrunk, inner, outer, *turns)
    send, grad_mid, grad_pre, filter_bias = call(
        functools.partial(filter_back_kernel, chunk),
        [shape(grid_dims, bf16), shape(spectrum, bf16), shape(spectrum, bf16), shape((2, wide), f32)],
        args,
        far_in=(5, 7, 2, 1, 6),
        far_out=(1, 2),
        scratch=[pltpu.VMEM(spectrum, bf16)] * 2,
        flops=2 * filter_flops,
        after=[stay(v) for v in sums[:1]],
    )
    recv = exchange(send, False)

    halves = len(dp_bits) > 0
    packed_weight = (base + small_rows // 2, 128)
    send_core, keep_core = call(
        functools.partial(filter_weight_kernel, bias_row, block_count),
        [shape(packed_weight, f32)] * 2,
        (places, spec, hid, grad_mid, grad_pre, filter_bias, small),
        prefetch=1,
        far_in=(1, 4, 2, 3),
        scratch=[pltpu.VMEM(small_dims, f32)],
        after=[stay(scatter.recvs[2])],
    )
    weight = [keep_core, pair_swap(send_core, "dp", 1)]
    sums = scatter.add((send, keep_core), flops=COMBINE_FLOPS)
    ahead = scatter.swap()
    own_base, own_small = base, small_rows // 2
    if halves:
        own_base, own_small = base // 2, small_rows // 4
        send_y, keep_y = call(
            functools.partial(halve_kernel, base),
            [shape((own_base + own_small, 128), f32)] * 2,
            (places, *weight),
            prefetch=1,
            after=[stay(sums[0])],
        )
        weight = [keep_y, pair_swap(send_y, *dp_bits[0])]
    for step in dp_bits[1:] + [n for n in lat_bits if n[1] < sub]:
        weight = [weight[0] + weight[1]]
        weight.append(pair_swap(weight[0], *step))
    pre_rows = -(-2 * width // 2048) * 16
    tail_dims = (groups, own_base + 2 * own_small + pre_rows, 128)
    (tail_send,) = call(
        functools.partial(last_sums_kernel, *names, own_base),
        [shape(tail_dims, bf16)],
        (box, own_row, recv, token_items, grad_mixed, holes, tables["fwd_t"], *weight),
        prefetch=2,
        far_in=(6, 5, 4),
        far_out=(0,),
        flops=lon_flops,
        after=[stay(v) for v in ahead],
    )
    result_dims = (items, cells, 1, width)
    (grad_tokens,) = call(
        functools.partial(last_kernel, *names),
        [shape(result_dims, f32)],
        (box, own_row, recv, token_items, grad_mixed, holes, pre_gain, tables["fwd_t"]),
        prefetch=2,
        far_in=(7, 5, 4, 6),
        raw=(-1,),
        scratch=[pltpu.VMEM(result_dims, f32), pltpu.SemaphoreType.DMA((items,))],
        flops=lon_flops,
        after=(stay(tail_send),),
    )
    tail = tail_send
    tail = lax.all_to_all(tail, "lat", 0, 0, tiled=True)

    while scatter.at < len(bit_names):
        sums = scatter.add((stay(tail_send),), flops=COMBINE_FLOPS)
        scatter.swap()
    merged = [v for pair in zip(scatter.keeps, scatter.recvs) for v in pair]
    expand_part, reduce_part = call(
        functools.partial(shard_kernel, shares),
        [shape((own_rows, width), f32)] * 2,
        merged,
        far_in=range(6),
                flops=COMBINE_FLOPS,
        after=(result, stay(grad_tokens), tail),
    )
    expand_part = expand_part.T
    extra = [n[1] for n in dp_bits[1:]]
    masks = [sum(b for i, b in enumerate(extra) if m >> i & 1) for m in range(1, 2 ** len(extra))]
    others = [pair_swap(tail[:, own_base + 2 * own_small :], "dp", m) for m in masks]
    third_dims = (block_count * own_base + 2 * own_small + 2 * pre_rows, 128)
    (third,) = call(
        functools.partial(third_kernel, sub, own_small, pre_rows),
        [shape(third_dims, bf16)],
        (tail, *others),
        after=(stay(sums[0]),),
    )
    thirds = [third]
    if halves:
        thirds.append(pair_swap(third, *dp_bits[0]))
    (joined,) = call(
        join_kernel,
        [shape((len(thirds) * third_dims[0], 128), bf16)],
        thirds,
        after=(stay(reduce_part),),
    )
    thirds += [pair_swap(joined, "dp", 1)]

    args = (places, *thirds)
    line_dims = (width,)
    filter_dims, bias_dims = filter_inner.shape, filter_inner_bias.shape
    out_dims = [line_dims, line_dims, filter_dims, bias_dims, filter_dims, bias_dims]
    out_dims += [line_dims, line_dims, (hidden_width,), line_dims]
    sums = call(
        functools.partial(tail_kernel, len(thirds), own_small, pre_rows),
        [shape(d, f32) for d in out_dims],
        args,
        prefetch=1,
        scratch=[pltpu.VMEM(small_dims, f32)],
    )
    return (
        result.swapaxes(0, 1).reshape(tokens.shape),
        grad_tokens.reshape(tokens.shape),
        *sums[:8],
        expand_part,
        sums[8],
        reduce_part,
        sums[9],
    )


def solution(mesh):
    rows = P(None, "dp", "lat", None, None)
    in_specs = (rows, P(None, "dp", None), P(None, "dp", "lat", None)) + (P(),) * 12 + (rows,)
    out_specs = (
        (rows, rows)
        + (P(),) * 8
        + (P(None, ("dp", "lat")), P(), P(("dp", "lat"), None), P())
    )
    return jax.shard_map(body, mesh=mesh, in_specs=in_specs, out_specs=out_specs, check_vma=False)
```

```python
import functools
import math

import jax
import jax.numpy as jnp
import ml_dtypes
import numpy as np
from jax import lax
from jax.experimental import pallas as pl
from jax.experimental.pallas import tpu as pltpu
from jax.sharding import PartitionSpec as P

MODES = 64
GROUP = 2
COMBINE_FLOPS = 2 * 10**10
shrink_level = 0.01
epsilon = 1e-05
inv_root_two = 1.0 / math.sqrt(2.0)
inv_root_tau = 1.0 / math.sqrt(2.0 * math.pi)
f32 = jnp.float32
bf16 = jnp.bfloat16


def table_pair(out_count, in_count, length):
    phase = np.arange(out_count)[:, None] * np.arange(in_count)[None, :] % length
    angle = phase.astype(np.float32) * np.float32(2.0 * math.pi / length)
    return np.cos(angle).astype(np.float32), np.sin(angle).astype(np.float32)


def low(values):
    return values.astype(np.float32).astype(ml_dtypes.bfloat16)


def make_tables(lon_cells, lat_count, block_size, chunk):
    lon_factor = np.float32(1.0 / math.sqrt(lon_cells))
    cosine, sine = table_pair(MODES, lon_cells, lon_cells)
    weight = np.where(np.arange(MODES) == 0, 1.0, 2.0).astype(np.float32)[:, None]
    forward = low(np.concatenate([cosine, -sine]) * lon_factor)
    inverse = low(np.concatenate([cosine * weight, -sine * weight]) * lon_factor)
    cosine, sine = table_pair(lat_count, lat_count, lat_count)
    lat_factor = np.float32(1.0 / math.sqrt(lat_count))
    same = np.eye(chunk, dtype=np.float32)
    cosine = np.kron(low(cosine * lat_factor).astype(np.float32), same)
    sine = np.kron(low(sine * lat_factor).astype(np.float32), same)
    turn_fwd = low(np.concatenate([cosine, sine], axis=1))
    turn_inv = low(np.concatenate([cosine, -sine], axis=1))
    eye, none = np.eye(block_size), np.zeros((block_size, block_size))
    swap = low(np.block([[none, -eye], [eye, none]]))
    return dict(
        fwd=forward, fwd_t=forward.T.copy(), inv=inverse, inv_t=inverse.T.copy(),
        turn_fwd=turn_fwd, turn_inv=turn_inv, swap=swap,
    )


def dot(a, b, ca, cb):
    return lax.dot_general(a, b, (((ca,), (cb,)), ((), ())), preferred_element_type=f32)


def line(ref):
    return ref[...].reshape(1, -1)


def row_mean(values):
    return jnp.sum(values, axis=-1, keepdims=True) * (1.0 / values.shape[-1])


def norm_parts(values):
    centered = values - row_mean(values)
    inv_scale = lax.rsqrt(row_mean(centered * centered) + epsilon)
    return centered * inv_scale, inv_scale


def norm_back(grad_normed, unit_values, inv_scale, gain):
    grad_unit = grad_normed * gain
    plain, cross = row_mean(grad_unit), row_mean(grad_unit * unit_values)
    return inv_scale * (grad_unit - plain - unit_values * cross)


def gelu_pair(values):
    half = 0.5 * (1.0 + lax.erf(values * inv_root_two))
    return values * half, half + values * jnp.exp(-0.5 * values * values) * inv_root_tau


def shrink_pair(values):
    inverse = lax.rsqrt(values * values + shrink_level * shrink_level)
    slope = 1.0 - shrink_level * shrink_level * shrink_level * inverse * inverse * inverse
    return values - shrink_level * values * inverse, slope


def valid_row(item, box_ref, row_ref, hole_ref, lat_rows, cells):
    crop, row = item // lat_rows, row_ref[0] + item % lat_rows
    crop_count = box_ref.shape[1]
    micro, crop = crop // crop_count, crop % crop_count
    limit = jnp.where(row < box_ref[micro, crop, 0], box_ref[micro, crop, 1], 0)
    column = lax.broadcasted_iota(jnp.int32, (1, cells), 1)
    return jnp.where((column < limit) & (hole_ref[item] > 0), 1.0, 0.0)


def as_column(row):
    cells = row.shape[1]
    down = lax.broadcasted_iota(jnp.int32, (cells, cells), 0)
    along = lax.broadcasted_iota(jnp.int32, (cells, cells), 1)
    return jnp.sum(jnp.where(down == along, row, 0.0), axis=1, keepdims=True)


def pack(both):
    half = both.shape[0] // 2
    rest = both[:, 128:]
    return both[:, :128], jnp.concatenate([rest[:half], rest[half:]], axis=1)


def unpack(packed):
    points = packed.shape[0] * 2 // 3
    rest = packed[points:]
    rest = jnp.concatenate([rest[:, :64], rest[:, 64:]], axis=0)
    return jnp.concatenate([packed[:points], rest], axis=1)


def put_modes(send_ref, item, spectrum, block_size, sub):
    spectrum = spectrum.astype(bf16)
    own = MODES // sub
    for block in range(spectrum.shape[1] // block_size):
        cut = spectrum[:, block * block_size : (block + 1) * block_size]
        both = jnp.concatenate([cut[:MODES], cut[MODES:]], axis=1)
        for j in range(sub):
            top, rest = pack(both[j * own : (j + 1) * own])
            send_ref[block * sub + j, item, :own] = top
            send_ref[block * sub + j, item, own:] = rest


def get_modes(recv_ref, item, block_size, sub):
    groups = recv_ref.shape[0]
    real, imag = [], []
    for block in range(groups // sub):
        parts = [unpack(recv_ref[block * sub + j, item]) for j in range(sub)]
        both = parts[0] if sub == 1 else jnp.concatenate(parts, axis=0)
        real.append(both[:, :block_size])
        imag.append(both[:, block_size:])
    real, imag = jnp.concatenate(real, axis=1), jnp.concatenate(imag, axis=1)
    return jnp.concatenate([real, imag], axis=0)


def unpack_all(recv_ref, points_ref):
    lat_count, crops, packed, _ = recv_ref.shape
    own = packed * 2 // 3
    for p in range(lat_count):
        for crop in range(crops):
            points_ref[p, crop * own : (crop + 1) * own] = unpack(recv_ref[p, crop])


def pack_all(points_ref, send_ref):
    lat_count, crops, packed, _ = send_ref.shape
    own = packed * 2 // 3
    for p in range(lat_count):
        for crop in range(crops):
            top, rest = pack(points_ref[p, crop * own : (crop + 1) * own])
            send_ref[p, crop, :own] = top
            send_ref[p, crop, own:] = rest


def turn_rows(src_ref, dst_ref, table, swap, chunk):
    lat_count, points, wide = src_ref.shape
    for at in range(0, points, chunk):
        piece = src_ref[:, at : at + chunk, :].reshape(lat_count * chunk, wide)
        other = dot(piece, swap, 1, 0).astype(bf16)
        out = dot(table, jnp.concatenate([piece, other], axis=0), 1, 0)
        dst_ref[:, at : at + chunk, :] = out.astype(bf16).reshape(lat_count, chunk, wide)


def pre_kernel(
    lat_rows, block_size, sub,
    box_ref, row_ref, token_ref, hole_ref, gain_ref, shift_ref, table_ref,
    send_ref,
):
    items, cells, _ = token_ref.shape
    units = [norm_parts(token_ref[item].astype(f32))[0] for item in range(items)]
    for item in range(items):
        valid = valid_row(item, box_ref, row_ref, hole_ref, lat_rows, cells)
        normed = (units[item] * line(gain_ref) + line(shift_ref)).astype(bf16)
        table = (table_ref[...].astype(f32) * valid).astype(bf16)
        put_modes(send_ref, item, dot(table, normed, 1, 0), block_size, sub)


def filter_kernel(
    chunk,
    recv_ref, inner_ref, inner_bias_ref, outer_ref, outer_bias_ref, turn_fwd_ref, turn_inv_ref, swap_ref,
    send_ref, spec, hid_out, slope_out, shrunk_out,
    hid_ref, slope_ref, shrunk_ref, filt_ref, points_ref, sems,
):
    unpack_all(recv_ref, points_ref)
    spec_ref = spec.here
    turn_rows(points_ref, spec_ref, turn_fwd_ref[...], swap_ref[...], chunk)
    spec.start()
    copies = []
    lat_count, points, wide = spec_ref.shape
    for p in range(0, lat_count, GROUP):
        rows, dims = slice(p, p + GROUP), (GROUP, points, wide)
        pre = dot(spec_ref[rows].reshape(GROUP * points, wide), inner_ref[...], 1, 0) + inner_bias_ref[...]
        hid, slope = gelu_pair(pre)
        hid = hid.astype(bf16)
        hid_ref[rows] = hid.reshape(dims)
        slope_ref[rows] = slope.reshape(dims)
        mid = dot(hid, outer_ref[...], 1, 0) + outer_bias_ref[...]
        filt, shrunk = shrink_pair(mid)
        filt_ref[rows] = filt.astype(bf16).reshape(dims)
        shrunk_ref[rows] = shrunk.reshape(dims)
        for at, (kept, out) in enumerate(((hid_ref, hid_out), (slope_ref, slope_out), (shrunk_ref, shrunk_out))):
            copies.append(pltpu.make_async_copy(kept.at[rows], out.at[rows], sems.at[p, at]))
            copies[-1].start()
    turn_rows(filt_ref, points_ref, turn_inv_ref[...], swap_ref[...], chunk)
    pack_all(points_ref, send_ref)
    for copy in copies:
        copy.wait()


def mix_kernel(
    lat_rows, block_size, sub,
    box_ref, row_ref, recv_ref, token_ref, hole_ref, gain_ref, shift_ref,
    post_gain_ref, post_shift_ref, table_ref,
    mixed, post_ref,
):
    items, cells, width = token_ref.shape
    pad = post_ref.shape[1] - cells
    backs = [get_modes(recv_ref, item, block_size, sub) for item in range(items)]
    units = [norm_parts(token_ref[item].astype(f32))[0] for item in range(items)]
    for item in range(items):
        valid = as_column(valid_row(item, box_ref, row_ref, hole_ref, lat_rows, cells))
        normed = units[item] * line(gain_ref) + line(shift_ref)
        filtered = dot(table_ref[...], backs[item], 1, 0)
        value = token_ref[item].astype(f32) + normed + valid * filtered
        mixed[item] = value
        unit, _ = norm_parts(value)
        post_ref[item, :cells] = (unit * line(post_gain_ref) + line(post_shift_ref)).astype(bf16)
        if pad:
            post_ref[item, cells:] = jnp.zeros((pad, width), bf16)


def feed_kernel(
    cuts, shares, runs, run,
    bit_ref, core_ref, post_own, post_other, cot_own, cot_other, expand_far, reduce_far, bias_ref,
    *refs,
):
    far_refs, refs = refs[:6], refs[6:]
    bias_grad, out_own, grad_own, out_other_ref, grad_other_ref, *refs = refs
    post_ref, cot_ref, expand_ref, reduce_ref, hidden_ref, grad_ref, *refs = refs
    expand_grad_ref, reduce_grad_ref, row_sems, weight_sems, far_sems = refs
    rows = post_own.shape[0]
    arrivals = []
    for at, (source, to) in enumerate(((post_own, post_ref), (post_other, post_ref), (cot_own, cot_ref), (cot_other, cot_ref))):
        here = slice(at % 2 * rows, (at % 2 + 1) * rows)
        arrivals.append(pltpu.make_async_copy(source, to.at[here], row_sems.at[at]))
    fetches = []
    for r in range(runs):
        start = pl.multiple_of((2 * r + core_ref[0]) * run, 128)
        here, there = slice(r * run, (r + 1) * run), pl.ds(start, run)
        fetches.append(pltpu.make_async_copy(expand_far.at[:, there], expand_ref.at[:, here], weight_sems.at[0, r]))
        fetches.append(pltpu.make_async_copy(reduce_far.at[there], reduce_ref.at[here], weight_sems.at[1, r]))
    waves = [arrivals[:2] + fetches[:1], arrivals[2:] + fetches[1:2]] + [fetches[2 * r : 2 * r + 2] for r in range(1, runs)]

    def turn_over(at):
        for copy in waves[at]:
            copy.wait()
        for copy in waves[at + 1] if at + 1 < len(waves) else ():
            copy.start()

    for copy in waves[0]:
        copy.start()
    turn_over(0)
    post = post_ref[...]
    for r in range(runs):
        here = slice(r * run, (r + 1) * run)
        if r:
            turn_over(r + 1)
        start = pl.multiple_of((2 * r + core_ref[0]) * run, 128)
        pre = dot(post, expand_ref[:, here], 1, 0) + bias_ref[:, pl.ds(start, run)]
        hidden, slope = gelu_pair(pre)
        hidden_ref[:, here] = hidden.astype(bf16)
        if not r:
            turn_over(1)
        cot = cot_ref[...]
        grad = (dot(cot, reduce_ref[here], 1, 1) * slope).astype(bf16)
        grad_ref[:, here] = grad
        bias_grad.here[:, here] = jnp.sum(grad.astype(f32), axis=0, keepdims=True)
    bias_grad.start()

    for r in range(runs):
        here = slice(r * run, (r + 1) * run)
        expand_grad_ref[here] = dot(grad_ref[:, here], post, 0, 0).astype(bf16)
        reduce_grad_ref[here] = dot(hidden_ref[:, here], cot, 0, 0).astype(bf16)
    copies = []
    for group, (at, outer) in enumerate(cuts):
        inner = runs * run // (2 * outer)
        own = bit_ref[at]
        to_lanes = 0
        for side, source in enumerate((expand_grad_ref, reduce_grad_ref)):
            lanes = shares[side][group]
            from_lanes = sum(shares[side][:group])
            for o in range(outer):
                for target, half in enumerate((1 - own, own)):
                    start = pl.multiple_of((2 * o + half) * inner, 16)
                    part = source.at[pl.ds(start, inner), from_lanes : from_lanes + lanes]
                    to = far_refs[2 * group + target].at[o * inner : (o + 1) * inner, to_lanes : to_lanes + lanes]
                    copies.append(pltpu.make_async_copy(part, to, far_sems.at[len(copies)]))
                    copies[-1].start()
            to_lanes += lanes

    back = dot(grad_ref[...], expand_ref[...], 1, 1)
    grad_own.here[...] = back[:rows]
    grad_own.start()
    grad_other_ref[...] = back[rows:].astype(bf16)
    out_own.here[...] = dot(hidden_ref[:rows], reduce_ref[...], 1, 0)
    out_own.start()
    out_other_ref[...] = dot(hidden_ref[rows:], reduce_ref[...], 1, 0).astype(bf16)
    for copy in copies:
        copy.wait()


def combine_kernel(places, bit_ref, *refs):
    groups = len(places)
    ins, outs = refs[: 2 * groups], refs[2 * groups :]
    for at, place in enumerate(places):
        keep, recv = ins[2 * at], ins[2 * at + 1]
        low_own = bit_ref[place] == 0
        first, second = keep[:, 0] + recv[:, 0], keep[:, 1] + recv[:, 1]
        outs[2 * at].here[...] = jnp.where(low_own, second, first)
        outs[2 * at].start()
        outs[2 * at + 1].here[...] = jnp.where(low_own, first, second)
        outs[2 * at + 1].start()


def shard_kernel(shares, *refs):
    *ins, expand_ref, reduce_ref = refs
    starts = [0, 0]
    for at in range(len(ins) // 2):
        total = ins[2 * at][...].astype(f32) + ins[2 * at + 1][...].astype(f32)
        begin = 0
        for side, ref in enumerate((expand_ref, reduce_ref)):
            lanes = shares[side][at]
            ref[:, starts[side] : starts[side] + lanes] = total[:, begin : begin + lanes]
            starts[side] += lanes
            begin += lanes


def result_kernel(mixed_ref, out_own_ref, out_other_ref, bias_ref, result_ref):
    cells, items, _ = result_ref.shape
    for item in range(items):
        out = out_own_ref[item, :cells] + out_other_ref[item, :cells].astype(f32)
        value = (mixed_ref[item] + (out + line(bias_ref))).astype(bf16)
        result_ref[:, item, :] = value


def post_kernel(
    lat_rows, block_size, sub,
    box_ref, row_ref, mixed_ref, grad_own_ref, grad_other_ref, cot_ref, hole_ref, gain_ref, table_ref,
    grad_mixed, send_ref, sum_ref, mixed_grad_ref, sems,
):
    items, cells, _ = mixed_grad_ref.shape
    sums = 0.0
    copies, rounded = [], []
    parts = [norm_parts(mixed_ref[item]) for item in range(items)]
    for item in range(items):
        unit, inv_scale = parts[item]
        grad = grad_own_ref[item, :cells] + grad_other_ref[item, :cells].astype(f32)
        cot = cot_ref[item, :cells].astype(f32)
        sums += jnp.concatenate([jnp.sum(v, axis=0, keepdims=True) for v in (grad * unit, grad, cot)], axis=0)
        value = cot + norm_back(grad, unit, inv_scale, line(gain_ref))
        mixed_grad_ref[item] = value
        copies.append(pltpu.make_async_copy(mixed_grad_ref.at[item], grad_mixed.at[item], sems.at[item]))
        copies[-1].start()
        rounded.append(value.astype(bf16))
    for item in range(items):
        valid = valid_row(item, box_ref, row_ref, hole_ref, lat_rows, cells)
        table = (table_ref[...].astype(f32) * valid).astype(bf16)
        put_modes(send_ref, item, dot(table, rounded[item], 1, 0), block_size, sub)
    sum_ref[...] = sums
    for copy in copies:
        copy.wait()


def small_kernel(layout, core_ref, post_sum_ref, expand_bias_ref, small_ref):
    per_run, runs, _ = layout
    small_ref[...] = jnp.zeros_like(small_ref)
    per_line = post_sum_ref.shape[1] // 128
    for line_at in range(3):
        for at in range(per_line):
            row = line_at * per_line + at
            small_ref[row : row + 1] = post_sum_ref[line_at : line_at + 1, at * 128 : (at + 1) * 128]
    for at in range(runs * per_run):
        row = (at // per_run * 2 + core_ref[0]) * per_run + at % per_run
        small_ref[pl.ds(3 * per_line + row, 1)] = expand_bias_ref[:, at * 128 : (at + 1) * 128]


def filter_back_kernel(
    chunk,
    recv_ref, slope_ref, shrunk_ref, inner_ref, outer_ref, turn_fwd_ref, turn_inv_ref, swap_ref,
    send_ref, grad_mid, grad_pre, bias_ref,
    turned_ref, points_ref,
):
    lat_count, points, wide = turned_ref.shape
    grad_mid_ref, grad_pre_ref = grad_mid.here, grad_pre.here
    unpack_all(recv_ref, points_ref)
    turn_rows(points_ref, turned_ref, turn_fwd_ref[...], swap_ref[...], chunk)
    inner_bias = jnp.zeros((1, wide), f32)
    outer_bias = jnp.zeros((1, wide), f32)
    for p in range(0, lat_count, GROUP):
        rows, dims, flat = slice(p, p + GROUP), (GROUP, points, wide), (GROUP * points, wide)
        mid = (turned_ref[rows].astype(f32) * shrunk_ref[rows]).astype(bf16).reshape(flat)
        grad_mid_ref[rows] = mid.reshape(dims)
        outer_bias += jnp.sum(mid.astype(f32), axis=0, keepdims=True)
        pre = (dot(mid, outer_ref[...], 1, 1) * slope_ref[rows].reshape(flat)).astype(bf16)
        grad_pre_ref[rows] = pre.reshape(dims)
        inner_bias += jnp.sum(pre.astype(f32), axis=0, keepdims=True)
        turned_ref[rows] = dot(pre, inner_ref[...], 1, 1).astype(bf16).reshape(dims)
    grad_mid.start()
    grad_pre.start()
    turn_rows(turned_ref, points_ref, turn_inv_ref[...], swap_ref[...], chunk)
    pack_all(points_ref, send_ref)
    bias_ref[0:1] = inner_bias
    bias_ref[1:2] = outer_bias


def filter_weight_kernel(
    bias_row, blocks, place_ref, spec_ref, hid_ref, grad_mid_ref, grad_pre_ref, bias_ref, small_in_ref,
    send_ref, keep_ref, small_ref,
):
    lat_count, points, wide = spec_ref.shape
    flat, half = (lat_count * points, wide), wide // 2
    own = place_ref[0]
    count = small_ref.shape[0] // 2
    base = keep_ref.shape[0] - count
    small_ref[...] = small_in_ref[...]
    for at in range(2):
        for side in range(2):
            row = bias_row + (2 * at + side) * blocks + place_ref[1]
            small_ref[pl.ds(row, 1), :half] = bias_ref[at : at + 1, side * half : (side + 1) * half]
    for at, (left, right) in enumerate(((spec_ref, grad_pre_ref), (hid_ref, grad_mid_ref))):
        grad = dot(left[...].reshape(flat), right[...].reshape(flat), 0, 0)
        first = grad[:half, :half] + grad[half:, half:]
        second = grad[:half, half:] - grad[half:, :half]
        top, rest = pack(jnp.concatenate([first, second], axis=1))
        share = small_ref[at * count : (at + 1) * count]

        @pl.when(own == at)
        def _():
            keep_ref[:half] = top
            keep_ref[half:base] = rest
            keep_ref[base:] = share

        @pl.when(own != at)
        def _():
            send_ref[:half] = top
            send_ref[half:base] = rest
            send_ref[base:] = share


def halve_kernel(base, place_ref, own_ref, recv_ref, send_ref, keep_ref):
    low_own = place_ref[2] == 0
    total = own_ref[...] + recv_ref[...]
    at = 0
    for begin, end in ((0, base), (base, total.shape[0])):
        count = (end - begin) // 2
        first, second = total[begin : begin + count], total[begin + count : end]
        send_ref[at : at + count] = jnp.where(low_own, second, first)
        keep_ref[at : at + count] = jnp.where(low_own, first, second)
        at += count


def last_sums_kernel(
    lat_rows, block_size, sub, base,
    box_ref, row_ref, recv_ref, token_ref, grad_mixed_ref, hole_ref, table_ref, own_ref, other_ref,
    tail,
):
    items, cells, width = token_ref.shape
    backs = [get_modes(recv_ref, item, block_size, sub) for item in range(items)]
    units = [norm_parts(token_ref[item].astype(f32))[0] for item in range(items)]
    sums = 0.0
    for item in range(items):
        valid = as_column(valid_row(item, box_ref, row_ref, hole_ref, lat_rows, cells))
        grad = grad_mixed_ref[item] + valid * dot(table_ref[...], backs[item], 1, 0)
        sums += jnp.concatenate([jnp.sum(v, axis=0, keepdims=True) for v in (grad * units[item], grad)], axis=0)

    rows = own_ref.shape[0] - base
    total = own_ref[...] + other_ref[...]
    value_ref = tail.here.at[0]
    value_ref[:base] = total[:base].astype(bf16)
    value_ref[base : base + rows] = total[base:].astype(bf16)
    per_line, at = width // 128, base + rows
    value_ref[at:] = jnp.zeros((value_ref.shape[0] - at, 128), bf16)
    for i in range(2):
        for j in range(per_line):
            row = at + i * per_line + j
            value_ref[row : row + 1] = sums[i : i + 1, j * 128 : (j + 1) * 128].astype(bf16)
    value = value_ref[...]
    for group in range(1, tail.shape[0]):
        tail.here[group] = value
    tail.start()


def last_kernel(
    lat_rows, block_size, sub,
    box_ref, row_ref, recv_ref, token_ref, grad_mixed_ref, hole_ref, gain_ref, table_ref,
    result, result_ref, sems,
):
    items, cells, width = token_ref.shape
    copies = []
    for item in range(items):
        back = get_modes(recv_ref, item, block_size, sub)
        unit, inv_scale = norm_parts(token_ref[item].astype(f32))
        valid = as_column(valid_row(item, box_ref, row_ref, hole_ref, lat_rows, cells))
        grad = grad_mixed_ref[item] + valid * dot(table_ref[...], back, 1, 0)
        value = grad_mixed_ref[item] + norm_back(grad, unit, inv_scale, line(gain_ref))
        result_ref[item] = value[:, None, :]
        copies.append(pltpu.make_async_copy(result_ref.at[item], result.at[item], sems.at[item]))
        copies[-1].start()
    for copy in copies:
        copy.wait()


def put_split(ref, at, value):
    high = value.astype(bf16)
    rows = value.shape[0]
    ref[at : at + rows] = high
    ref[at + rows : at + 2 * rows] = (value - high.astype(f32)).astype(bf16)


def get_split(ref, at, rows):
    return ref[at : at + rows].astype(f32) + ref[at + rows : at + 2 * rows].astype(f32)


def third_kernel(sub, base, rows, pre_rows, recv_ref, *refs):
    *other_refs, out_ref = refs
    blocks = recv_ref.shape[0] // sub
    total = 0.0
    for block in range(blocks):
        part = recv_ref[block * sub]
        out_ref[block * base : (block + 1) * base] = part[:base]
        total += part[base : base + rows].astype(f32)
    put_split(out_ref, blocks * base, total)
    total = jnp.sum(recv_ref[:, base + rows : base + rows + pre_rows].astype(f32), axis=0)
    for ref in other_refs:
        total += jnp.sum(ref[...].astype(f32), axis=0)
    put_split(out_ref, blocks * base + 2 * rows, total)


def join_kernel(*refs):
    *parts, out_ref = refs
    rows = parts[0].shape[0]
    for at, ref in enumerate(parts):
        out_ref[at * rows : (at + 1) * rows] = ref[...]


def tail_kernel(
    count, rows, pre_rows, place_ref, *refs,
):
    parts, refs = list(refs[:count]), refs[count:]
    joined = parts.pop()
    size = parts[0].shape[0]
    parts += [joined.at[at * size : (at + 1) * size] for at in range(len(parts))]
    count = len(parts)
    (
        pre_gain_ref, pre_shift_ref, inner_ref, inner_bias_ref, outer_ref, outer_bias_ref,
        post_gain_ref, post_shift_ref, expand_bias_ref, reduce_bias_ref, small_ref,
    ) = refs
    own, y_own = place_ref[0], place_ref[2]

    def in_order(values):
        if count == 4:
            pairs = [values[0:2], values[2:4]]
            sides = [
                [jnp.where(y_own == 0, a, b), jnp.where(y_own == 0, b, a)] for a, b in pairs
            ]
        else:
            sides = [values[0:1], values[1:2]]
        joined = [jnp.concatenate(side, axis=0) if len(side) > 1 else side[0] for side in sides]
        return jnp.where(own == 0, joined[0], joined[1]), jnp.where(own == 0, joined[1], joined[0])

    pre_at = parts[0].shape[0] - 2 * pre_rows
    small_at = pre_at - 2 * rows
    for at, value in enumerate(in_order([get_split(ref, small_at, rows) for ref in parts])):
        small_ref[at * value.shape[0] : (at + 1) * value.shape[0]] = value
    per_line = pre_gain_ref.shape[0] // 128
    sums = sum(get_split(ref, pre_at, pre_rows) for ref in parts)

    def put(ref, at, value):
        ref[pl.ds(at * 128, 128)] = value.reshape(128)

    for i, ref in enumerate((pre_gain_ref, pre_shift_ref)):
        for j in range(per_line):
            put(ref, j, sums[i * per_line + j : i * per_line + j + 1])

    def row(at):
        return small_ref[at : at + 1]

    at = 0
    for ref in (post_gain_ref, post_shift_ref, reduce_bias_ref, expand_bias_ref):
        for j in range(ref.shape[0] // 128):
            put(ref, j, row(at))
            at += 1
    _, blocks, size = inner_bias_ref.shape
    for ref in (inner_bias_ref, outer_bias_ref):
        for side in range(2):
            for block in range(blocks):
                ref[side, block : block + 1] = row(at)[:, :size]
                at += 1
    base = small_at // blocks
    for at in range(blocks):
        cuts = [ref[at * base : (at + 1) * base].astype(f32) for ref in parts]
        for ref, value in zip((inner_ref, outer_ref), in_order(cuts)):
            value = unpack(value)
            for side in range(2):
                ref[side, at] = value[:, side * size : (side + 1) * size]


class Far:
    def __init__(self, far_ref, here_ref, sem, incoming):
        pair = (far_ref, here_ref) if incoming else (here_ref, far_ref)
        self.here, self.copy, self.pending = here_ref, pltpu.make_async_copy(*pair, sem), False
        if incoming:
            self.start()

    def start(self):
        self.copy.start()
        self.pending = True

    def wait(self):
        if self.pending:
            self.copy.wait()
            self.pending = False

    @property
    def shape(self):
        return self.here.shape

    def __getitem__(self, index):
        self.wait()
        return self.here[index]


def call(kernel, out_shape, args, prefetch=0, scratch=(), flops=0, vmem=16, after=(), far_in=(), far_out=(), raw=(), loose=()):
    args, after = tuple(args), tuple(after)
    far_out = [len(args) + i for i in far_out]
    raw = set(i if i >= 0 else len(args) - 1 - i for i in raw)
    far = list(far_in) + far_out
    count = len(args) + len(out_shape)
    every = list(args) + list(out_shape)
    anywhere = pl.BlockSpec(memory_space=pl.ANY)

    def spec(i):
        if i in far or i in raw:
            return anywhere
        dims = every[i].shape
        rest = (0,) * len(dims)
        return pl.BlockSpec(tuple(dims), lambda *_: rest)

    def whole_kernel(*refs):
        refs = list(refs[: len(args)]) + list(refs[len(args) + len(after) :])
        sems = refs.pop() if far else None
        buffers = [refs.pop() for _ in far][::-1]
        fars = {}
        for at, i in enumerate(far):
            fars[i] = refs[i] = Far(refs[i], buffers[at], sems.at[at], i < len(args))
        kernel(*refs)
        for value in fars.values():
            value.wait()

    moved = sum(math.prod(a.shape) * np.dtype(a.dtype).itemsize for a in every)
    fixed = [pltpu.with_memory_space_constraint(a, pltpu.HBM) if i in far and i not in loose else a for i, a in enumerate(args)]
    shapes = [
        pltpu.HBM(a.shape, a.dtype) if i in far_out or i in raw else a for i, a in enumerate(out_shape, len(args))
    ]
    scratch = list(scratch) + [pltpu.VMEM(every[i].shape, every[i].dtype) for i in far]
    if far:
        scratch.append(pltpu.SemaphoreType.DMA((len(far),)))
    return pl.pallas_call(
        whole_kernel,
        out_shape=shapes,
        grid_spec=pltpu.PrefetchScalarGridSpec(
            num_scalar_prefetch=prefetch,
            grid=(1,),
            in_specs=[spec(i) for i in range(prefetch, len(args))] + [anywhere] * len(after),
            out_specs=[spec(i) for i in range(len(args), count)],
            scratch_shapes=scratch,
        ),
        compiler_params=pltpu.CompilerParams(
            dimension_semantics=("arbitrary",), vmem_limit_bytes=vmem << 20
        ),
        cost_estimate=pl.CostEstimate(flops=int(flops), bytes_accessed=int(moved), transcendentals=0),
    )(*fixed, *after)


def shape(dims, dtype):
    return jax.ShapeDtypeStruct(tuple(dims), dtype)


def stay(operand):
    return pltpu.with_memory_space_constraint(operand, pltpu.HBM)


def pair_swap(operand, axis_name, bit):
    size = lax.axis_size(axis_name)
    return lax.ppermute(operand, axis_name, [(i, i ^ bit) for i in range(size)])


def axis_bits(axis_name):
    size = lax.axis_size(axis_name)
    return [1 << i for i in range(size.bit_length() - 1)]


def body(
    tokens,
    boxes,
    patch_mask,
    pre_gain,
    pre_shift,
    filter_inner,
    filter_inner_bias,
    filter_outer,
    filter_outer_bias,
    post_gain,
    post_shift,
    expand_weight,
    expand_bias,
    reduce_weight,
    reduce_bias,
    cotangent,
):
    micro_count, crop_count, lat_rows, cells, width = tokens.shape
    groups = lax.axis_size("lat")
    lat_count = lat_rows * groups
    block_count, block_size = filter_inner.shape[1:3]
    sub = groups // block_count
    modes_own = MODES // sub
    crops = micro_count * crop_count
    items = crops * lat_rows
    points = crops * modes_own
    wide = 2 * block_size
    padded = -(-cells // 16) * 16
    rows = items * padded
    chunk = 16
    hidden_width = expand_weight.shape[1]
    dp_size = lax.axis_size("dp")
    lat_index, dp_index = lax.axis_index("lat"), lax.axis_index("dp")
    own_block = lat_index // sub
    tables = {k: jnp.asarray(v) for k, v in make_tables(cells, lat_count, block_size, chunk).items()}

    box = stay(boxes)
    own_row = (lat_index * lat_rows).astype(jnp.int32).reshape(1)
    core = dp_index % 2
    token_items = tokens.reshape(items, cells, width)
    cot_pad = jnp.pad(cotangent.reshape(items, cells, width), ((0, 0), (0, padded - cells), (0, 0)))
    holes = patch_mask.reshape(items, 1, cells)
    row_item = (items, cells, width)
    pad_item = (items, padded, width)
    packed = modes_own * 3 // 2
    mode_dims = (groups, items, packed, 128)
    names = (lat_rows, block_size, sub)
    lon_flops = 2 * items * 2 * MODES * cells * width

    def exchange(both, by_rows):
        if by_rows:
            both = both.reshape(groups, crops, lat_rows, packed, 128).swapaxes(1, 2)
            both = both.reshape(groups, items * packed, 128)
            both = lax.all_to_all(both, "lat", 0, 0, tiled=True)
            return both.reshape(lat_count, crops, packed, 128)
        both = both.reshape(groups, items * packed, 128)
        both = lax.all_to_all(both, "lat", 0, 0, tiled=True)
        both = both.reshape(groups, lat_rows, crops, packed, 128).swapaxes(1, 2)
        return both.reshape(mode_dims)

    def own_matrix(matrix):
        pair = lax.dynamic_index_in_dim(matrix, own_block, 1, keepdims=False)
        top = jnp.concatenate([pair[0], pair[1]], axis=1)
        under = jnp.concatenate([-pair[1], pair[0]], axis=1)
        return jnp.concatenate([top, under], axis=0)

    def own_bias(bias):
        return lax.dynamic_index_in_dim(bias, own_block, 1, keepdims=False).reshape(1, wide)

    args = (box, own_row, token_items, holes, pre_gain, pre_shift, tables["fwd"])
    (send,) = call(
        functools.partial(pre_kernel, *names),
        [shape(mode_dims, bf16)],
        args,
        prefetch=2,
        far_in=range(3, 7),
        flops=lon_flops,
    )
    recv = exchange(send, True)
    cot_other = pair_swap(cot_pad.reshape(rows, width), "dp", 1)

    spectrum = (lat_count, points, wide)
    grid_dims = (lat_count, crops, packed, 128)
    filter_flops = 4 * lat_count * points * wide * wide
    inner, outer = own_matrix(filter_inner), own_matrix(filter_outer)
    turns = (tables["turn_fwd"], tables["turn_inv"], tables["swap"])
    args = (recv, inner, own_bias(filter_inner_bias), outer, own_bias(filter_outer_bias), *turns)
    send, spec, hid, slope, shrunk = call(
        functools.partial(filter_kernel, chunk),
        [shape(grid_dims, bf16)] + [shape(spectrum, t) for t in (bf16, bf16, f32, f32)],
        args,
        far_in=(5, 6, 7),
        far_out=(1,),
        raw=(-3, -4, -5),
        scratch=[pltpu.VMEM(spectrum, t) for t in (bf16, f32, f32, bf16, bf16)]
        + [pltpu.SemaphoreType.DMA((lat_count, 3))],
        flops=filter_flops,
    )
    recv = exchange(send, False)

    args = (
        box, own_row, recv, token_items, holes, pre_gain, pre_shift, post_gain, post_shift, tables["inv_t"],
    )
    mixed, post = call(
        functools.partial(mix_kernel, *names),
        [shape(row_item, f32), shape(pad_item, bf16)],
        args,
        prefetch=2,
        far_in=range(4, 10),
        flops=lon_flops,
    )
    post = post.reshape(rows, width)
    post_other = pair_swap(post, "dp", 1)

    dp_bits = [("dp", b) for b in axis_bits("dp")[1:]]
    lat_bits = [("lat", b) for b in axis_bits("lat")]
    bit_names = dp_bits[::-1] + lat_bits[::-1]
    own_bits = jnp.stack([(lax.axis_index(n) // b) % 2 for n, b in bit_names]).astype(jnp.int32)
    own_rows = hidden_width // (dp_size * groups)
    half = hidden_width // 2
    run = hidden_width // dp_size
    runs = dp_size // 2
    core_bit = core.astype(jnp.int32).reshape(1)

    whole_rows = [n for n in lat_bits if own_rows * n[1] % 16 == 0]
    orders = [
        dp_bits + lat_bits,
        whole_rows[:1] + [n for n in lat_bits[:-1] if n != whole_rows[0]] + dp_bits + lat_bits[-1:],
        whole_rows[1:2] + dp_bits + [n for n in lat_bits if n != whole_rows[1]],
    ]
    lefts = [list(bit_names) for _ in orders]

    def place_of(step, left):
        return bit_names.index(step), 2 ** left.index(step)

    third = width // 3
    shares = ((third * 3 // 2, third, third // 2), (third,) * 3)
    lanes = [a + b for a, b in zip(*shares)]
    flat, double = (rows, width), (2 * rows, width)
    cuts = [place_of(order[0], left) for order, left in zip(orders, lefts)]
    copy_count = sum(4 * outer for _, outer in cuts)
    args = (
        own_bits, core_bit, post, post_other, stay(cot_pad.reshape(rows, width)), cot_other,
        stay(expand_weight), stay(reduce_weight), expand_bias.reshape(1, hidden_width),
    )
    *parts, grad_b, out_own, grad_own, out_other, grad_other = call(
        functools.partial(feed_kernel, cuts, shares, runs, run),
        [shape((half // 2, n), bf16) for n in lanes for _ in range(2)]
        + [shape((1, half), f32), shape(flat, f32), shape(flat, f32), shape(flat, bf16), shape(flat, bf16)],
        args,
        prefetch=2,
        far_in=(8,),
        far_out=(6, 7, 8),
        raw=tuple(range(2, 8)) + tuple(range(-1, -7, -1)),
        scratch=[pltpu.VMEM(double, bf16)] * 2
        + [pltpu.VMEM((width, half), bf16), pltpu.VMEM((half, width), bf16)]
        + [pltpu.VMEM((2 * rows, half), bf16)] * 2
        + [pltpu.VMEM((half, width), bf16)] * 2
        + [pltpu.SemaphoreType.DMA((4,)), pltpu.SemaphoreType.DMA((2, runs))]
        + [pltpu.SemaphoreType.DMA((copy_count,))],
        flops=6 * 2 * 2 * rows * width * half,
        vmem=52,
    )
    grad_other = pair_swap(grad_other, "dp", 1).reshape(pad_item)
    out_other = pair_swap(out_other, "dp", 1).reshape(pad_item)

    class Scatter:
        def __init__(self):
            self.at, self.sends, self.keeps = 0, list(parts[0::2]), list(parts[1::2])

        def swap(self):
            self.recvs = []
            for send, order, left in zip(self.sends, orders, lefts):
                left.remove(order[self.at])
                self.recvs.append(pair_swap(send, *order[self.at]))
            self.at += 1
            return list(self.recvs)

        def add(self, after=(), flops=0):
            cuts = [place_of(order[self.at], left) for order, left in zip(orders, lefts)]
            left_rows = self.keeps[0].shape[0]
            dims = [(outer, 2, left_rows // (2 * outer), n) for (_, outer), n in zip(cuts, lanes)]
            ins = [v.reshape(d) for keep, recv, d in zip(self.keeps, self.recvs, dims) for v in (keep, recv)]
            outs = call(
                functools.partial(combine_kernel, [place for place, _ in cuts]),
                [shape((d[0], d[2], d[3]), bf16) for d in dims for _ in range(2)],
                (own_bits, *ins),
                prefetch=1,
                far_in=range(1, 7),
                loose=(2, 4, 6),
                far_out=range(6),
                after=after,
                flops=flops,
            )
            outs = [v.reshape(left_rows // 2, v.shape[-1]) for v in outs]
            self.sends, self.keeps = outs[0::2], outs[1::2]
            return outs

    scatter = Scatter()
    scatter.swap()

    args = (
        box, own_row, mixed, grad_own.reshape(pad_item), grad_other, cot_pad, holes, post_gain, tables["inv"],
    )
    grad_mixed, send, post_sums = call(
        functools.partial(post_kernel, *names),
        [shape(row_item, f32), shape(mode_dims, bf16), shape((3, width), f32)],
        args,
        prefetch=2,
        far_in=(3, 5, 7, 8, 6),
        raw=(-1,),
        scratch=[pltpu.VMEM(row_item, f32), pltpu.SemaphoreType.DMA((items,))],
        flops=lon_flops,
    )
    (result,) = call(
        result_kernel,
        [shape((cells, items, width), bf16)],
        (mixed, out_own.reshape(pad_item), out_other, reduce_bias),
        far_in=(1, 3),
        after=(send,),
    )
    recv = exchange(send, True)

    sums = scatter.add((send,), flops=COMBINE_FLOPS)
    scatter.swap()

    bias_row = 3 * width // 128 + hidden_width // 128
    small_rows = -(-(bias_row + 4 * block_count) // 32) * 32
    small_dims = (small_rows, 128)
    (small,) = call(
        functools.partial(small_kernel, (run // 128, runs, block_count)),
        [shape(small_dims, f32)],
        (core_bit, post_sums, grad_b),
        prefetch=1,
    )
    base = block_size * 3 // 2
    y_index = (dp_index // 2) % 2
    places = jnp.stack([core, own_block, y_index]).astype(jnp.int32)
    args = (recv, slope, shrunk, inner, outer, *turns)
    send, grad_mid, grad_pre, filter_bias = call(
        functools.partial(filter_back_kernel, chunk),
        [shape(grid_dims, bf16), shape(spectrum, bf16), shape(spectrum, bf16), shape((2, wide), f32)],
        args,
        far_in=(5, 7, 2, 1, 6),
        far_out=(1, 2),
        scratch=[pltpu.VMEM(spectrum, bf16)] * 2,
        flops=2 * filter_flops,
        after=[stay(v) for v in sums[:1]],
    )
    recv = exchange(send, False)

    halves = len(dp_bits) > 0
    packed_weight = (base + small_rows // 2, 128)
    send_core, keep_core = call(
        functools.partial(filter_weight_kernel, bias_row, block_count),
        [shape(packed_weight, f32)] * 2,
        (places, spec, hid, grad_mid, grad_pre, filter_bias, small),
        prefetch=1,
        far_in=(1, 4, 2, 3),
        scratch=[pltpu.VMEM(small_dims, f32)],
        after=(scatter.recvs[2],),
    )
    weight = [keep_core, pair_swap(send_core, "dp", 1)]
    sums = scatter.add((send, keep_core), flops=COMBINE_FLOPS)
    ahead = scatter.swap()
    own_base, own_small = base, small_rows // 2
    if halves:
        own_base, own_small = base // 2, small_rows // 4
        send_y, keep_y = call(
            functools.partial(halve_kernel, base),
            [shape((own_base + own_small, 128), f32)] * 2,
            (places, *weight),
            prefetch=1,
            after=[stay(sums[0])],
        )
        weight = [keep_y, pair_swap(send_y, *dp_bits[0])]
    for step in dp_bits[1:] + [n for n in lat_bits if n[1] < sub]:
        weight = [weight[0] + weight[1]]
        weight.append(pair_swap(weight[0], *step))
    pre_rows = -(-2 * width // 2048) * 16
    tail_dims = (groups, -(-(own_base + own_small + pre_rows) // 16) * 16, 128)
    (tail_send,) = call(
        functools.partial(last_sums_kernel, *names, own_base),
        [shape(tail_dims, bf16)],
        (box, own_row, recv, token_items, grad_mixed, holes, tables["fwd_t"], *weight),
        prefetch=2,
        far_in=(6, 5, 4),
        far_out=(0,),
        flops=lon_flops,
        after=ahead,
    )
    result_dims = (items, cells, 1, width)
    (grad_tokens,) = call(
        functools.partial(last_kernel, *names),
        [shape(result_dims, f32)],
        (box, own_row, recv, token_items, grad_mixed, holes, pre_gain, tables["fwd_t"]),
        prefetch=2,
        far_in=(7, 5, 4, 6),
        raw=(-1,),
        scratch=[pltpu.VMEM(result_dims, f32), pltpu.SemaphoreType.DMA((items,))],
        flops=lon_flops,
        after=(stay(tail_send),),
    )
    tail = tail_send
    tail = lax.all_to_all(tail, "lat", 0, 0, tiled=True)

    while scatter.at < len(bit_names):
        sums = scatter.add((stay(tail_send),), flops=COMBINE_FLOPS)
        scatter.swap()
    merged = [v for pair in zip(scatter.keeps, scatter.recvs) for v in pair]
    expand_part, reduce_part = call(
        functools.partial(shard_kernel, shares),
        [shape((own_rows, width), f32)] * 2,
        merged,
        far_in=range(6),
        loose=(1, 3, 5),
                flops=COMBINE_FLOPS,
        after=(result, stay(grad_tokens), tail),
    )
    expand_part = expand_part.T
    extra = [n[1] for n in dp_bits[1:]]
    masks = [sum(b for i, b in enumerate(extra) if m >> i & 1) for m in range(1, 2 ** len(extra))]
    others = [pair_swap(tail[:, own_base + own_small : own_base + own_small + pre_rows], "dp", m) for m in masks]
    third_dims = (block_count * own_base + 2 * own_small + 2 * pre_rows, 128)
    (third,) = call(
        functools.partial(third_kernel, sub, own_base, own_small, pre_rows),
        [shape(third_dims, bf16)],
        (tail, *others),
        after=(stay(sums[0]),),
    )
    thirds = [third]
    if halves:
        thirds.append(pair_swap(third, *dp_bits[0]))
    (joined,) = call(
        join_kernel,
        [shape((len(thirds) * third_dims[0], 128), bf16)],
        thirds,
        after=(stay(reduce_part),),
    )
    thirds += [pair_swap(joined, "dp", 1)]

    args = (places, *thirds)
    line_dims = (width,)
    filter_dims, bias_dims = filter_inner.shape, filter_inner_bias.shape
    out_dims = [line_dims, line_dims, filter_dims, bias_dims, filter_dims, bias_dims]
    out_dims += [line_dims, line_dims, (hidden_width,), line_dims]
    sums = call(
        functools.partial(tail_kernel, len(thirds), own_small, pre_rows),
        [shape(d, f32) for d in out_dims],
        args,
        prefetch=1,
        scratch=[pltpu.VMEM(small_dims, f32)],
    )
    return (
        result.swapaxes(0, 1).reshape(tokens.shape),
        grad_tokens.reshape(tokens.shape),
        *sums[:8],
        expand_part,
        sums[8],
        reduce_part,
        sums[9],
    )


def solution(mesh):
    rows = P(None, "dp", "lat", None, None)
    in_specs = (rows, P(None, "dp", None), P(None, "dp", "lat", None)) + (P(),) * 12 + (rows,)
    out_specs = (
        (rows, rows)
        + (P(),) * 8
        + (P(None, ("dp", "lat")), P(), P(("dp", "lat"), None), P())
    )
    return jax.shard_map(body, mesh=mesh, in_specs=in_specs, out_specs=out_specs, check_vma=False)
```

```python
import functools
import math

import jax
import jax.numpy as jnp
import ml_dtypes
import numpy as np
from jax import lax
from jax.experimental import pallas as pl
from jax.experimental.pallas import tpu as pltpu
from jax.sharding import PartitionSpec as P

MODES = 64
GROUP = 2
COMBINE_FLOPS = 2 * 10**10
shrink_level = 0.01
epsilon = 1e-05
inv_root_two = 1.0 / math.sqrt(2.0)
inv_root_tau = 1.0 / math.sqrt(2.0 * math.pi)
f32 = jnp.float32
bf16 = jnp.bfloat16


def table_pair(out_count, in_count, length):
    phase = np.arange(out_count)[:, None] * np.arange(in_count)[None, :] % length
    angle = phase.astype(np.float32) * np.float32(2.0 * math.pi / length)
    return np.cos(angle).astype(np.float32), np.sin(angle).astype(np.float32)


def low(values):
    return values.astype(np.float32).astype(ml_dtypes.bfloat16)


def make_tables(lon_cells, lat_count, block_size, chunk):
    lon_factor = np.float32(1.0 / math.sqrt(lon_cells))
    cosine, sine = table_pair(MODES, lon_cells, lon_cells)
    weight = np.where(np.arange(MODES) == 0, 1.0, 2.0).astype(np.float32)[:, None]
    forward = low(np.concatenate([cosine, -sine]) * lon_factor)
    inverse = low(np.concatenate([cosine * weight, -sine * weight]) * lon_factor)
    cosine, sine = table_pair(lat_count, lat_count, lat_count)
    lat_factor = np.float32(1.0 / math.sqrt(lat_count))
    same = np.eye(chunk, dtype=np.float32)
    cosine = np.kron(low(cosine * lat_factor).astype(np.float32), same)
    sine = np.kron(low(sine * lat_factor).astype(np.float32), same)
    turn_fwd = low(np.concatenate([cosine, sine], axis=1))
    turn_inv = low(np.concatenate([cosine, -sine], axis=1))
    eye, none = np.eye(block_size), np.zeros((block_size, block_size))
    swap = low(np.block([[none, -eye], [eye, none]]))
    return dict(
        fwd=forward, fwd_t=forward.T.copy(), inv=inverse, inv_t=inverse.T.copy(),
        turn_fwd=turn_fwd, turn_inv=turn_inv, swap=swap,
    )


def dot(a, b, ca, cb):
    return lax.dot_general(a, b, (((ca,), (cb,)), ((), ())), preferred_element_type=f32)


def line(ref):
    return ref[...].reshape(1, -1)


def row_mean(values):
    return jnp.sum(values, axis=-1, keepdims=True) * (1.0 / values.shape[-1])


def norm_parts(values):
    centered = values - row_mean(values)
    inv_scale = lax.rsqrt(row_mean(centered * centered) + epsilon)
    return centered * inv_scale, inv_scale


def norm_back(grad_normed, unit_values, inv_scale, gain):
    grad_unit = grad_normed * gain
    plain, cross = row_mean(grad_unit), row_mean(grad_unit * unit_values)
    return inv_scale * (grad_unit - plain - unit_values * cross)


def gelu_pair(values):
    half = 0.5 * (1.0 + lax.erf(values * inv_root_two))
    return values * half, half + values * jnp.exp(-0.5 * values * values) * inv_root_tau


def shrink_pair(values):
    inverse = lax.rsqrt(values * values + shrink_level * shrink_level)
    slope = 1.0 - shrink_level * shrink_level * shrink_level * inverse * inverse * inverse
    return values - shrink_level * values * inverse, slope


def valid_row(item, box_ref, row_ref, hole_ref, lat_rows, cells):
    crop, row = item // lat_rows, row_ref[0] + item % lat_rows
    crop_count = box_ref.shape[1]
    micro, crop = crop // crop_count, crop % crop_count
    limit = jnp.where(row < box_ref[micro, crop, 0], box_ref[micro, crop, 1], 0)
    column = lax.broadcasted_iota(jnp.int32, (1, cells), 1)
    return jnp.where((column < limit) & (hole_ref[item] > 0), 1.0, 0.0)


def as_column(row):
    cells = row.shape[1]
    down = lax.broadcasted_iota(jnp.int32, (cells, cells), 0)
    along = lax.broadcasted_iota(jnp.int32, (cells, cells), 1)
    return jnp.sum(jnp.where(down == along, row, 0.0), axis=1, keepdims=True)


def pack(both):
    half = both.shape[0] // 2
    rest = both[:, 128:]
    return both[:, :128], jnp.concatenate([rest[:half], rest[half:]], axis=1)


def unpack(packed):
    points = packed.shape[0] * 2 // 3
    rest = packed[points:]
    rest = jnp.concatenate([rest[:, :64], rest[:, 64:]], axis=0)
    return jnp.concatenate([packed[:points], rest], axis=1)


def put_modes(send_ref, item, spectrum, block_size, sub):
    spectrum = spectrum.astype(bf16)
    own = MODES // sub
    for block in range(spectrum.shape[1] // block_size):
        cut = spectrum[:, block * block_size : (block + 1) * block_size]
        both = jnp.concatenate([cut[:MODES], cut[MODES:]], axis=1)
        for j in range(sub):
            top, rest = pack(both[j * own : (j + 1) * own])
            send_ref[block * sub + j, item, :own] = top
            send_ref[block * sub + j, item, own:] = rest


def get_modes(recv_ref, item, block_size, sub):
    groups = recv_ref.shape[0]
    real, imag = [], []
    for block in range(groups // sub):
        parts = [unpack(recv_ref[block * sub + j, item]) for j in range(sub)]
        both = parts[0] if sub == 1 else jnp.concatenate(parts, axis=0)
        real.append(both[:, :block_size])
        imag.append(both[:, block_size:])
    real, imag = jnp.concatenate(real, axis=1), jnp.concatenate(imag, axis=1)
    return jnp.concatenate([real, imag], axis=0)


def unpack_all(recv_ref, points_ref):
    lat_count, crops, packed, _ = recv_ref.shape
    own = packed * 2 // 3
    for p in range(lat_count):
        for crop in range(crops):
            points_ref[p, crop * own : (crop + 1) * own] = unpack(recv_ref[p, crop])


def pack_all(points_ref, send_ref):
    lat_count, crops, packed, _ = send_ref.shape
    own = packed * 2 // 3
    for p in range(lat_count):
        for crop in range(crops):
            top, rest = pack(points_ref[p, crop * own : (crop + 1) * own])
            send_ref[p, crop, :own] = top
            send_ref[p, crop, own:] = rest


def turn_rows(src_ref, dst_ref, table, swap, chunk):
    lat_count, points, wide = src_ref.shape
    for at in range(0, points, chunk):
        piece = src_ref[:, at : at + chunk, :].reshape(lat_count * chunk, wide)
        other = dot(piece, swap, 1, 0).astype(bf16)
        out = dot(table, jnp.concatenate([piece, other], axis=0), 1, 0)
        dst_ref[:, at : at + chunk, :] = out.astype(bf16).reshape(lat_count, chunk, wide)


def pre_kernel(
    lat_rows, block_size, sub,
    box_ref, row_ref, token_ref, hole_ref, gain_ref, shift_ref, table_ref,
    send_ref,
):
    items, cells, _ = token_ref.shape
    units = [norm_parts(token_ref[item].astype(f32))[0] for item in range(items)]
    for item in range(items):
        valid = valid_row(item, box_ref, row_ref, hole_ref, lat_rows, cells)
        normed = (units[item] * line(gain_ref) + line(shift_ref)).astype(bf16)
        table = (table_ref[...].astype(f32) * valid).astype(bf16)
        put_modes(send_ref, item, dot(table, normed, 1, 0), block_size, sub)


def filter_kernel(
    chunk,
    recv_ref, inner_ref, inner_bias_ref, outer_ref, outer_bias_ref, turn_fwd_ref, turn_inv_ref, swap_ref,
    send_ref, spec, hid_out, slope_out, shrunk_out,
    hid_ref, slope_ref, shrunk_ref, filt_ref, points_ref, sems,
):
    unpack_all(recv_ref, points_ref)
    spec_ref = spec.here
    turn_rows(points_ref, spec_ref, turn_fwd_ref[...], swap_ref[...], chunk)
    spec.start()
    copies = []
    lat_count, points, wide = spec_ref.shape
    for p in range(0, lat_count, GROUP):
        rows, dims = slice(p, p + GROUP), (GROUP, points, wide)
        pre = dot(spec_ref[rows].reshape(GROUP * points, wide), inner_ref[...], 1, 0) + inner_bias_ref[...]
        hid, slope = gelu_pair(pre)
        hid = hid.astype(bf16)
        hid_ref[rows] = hid.reshape(dims)
        slope_ref[rows] = slope.reshape(dims)
        mid = dot(hid, outer_ref[...], 1, 0) + outer_bias_ref[...]
        filt, shrunk = shrink_pair(mid)
        filt_ref[rows] = filt.astype(bf16).reshape(dims)
        shrunk_ref[rows] = shrunk.reshape(dims)
        for at, (kept, out) in enumerate(((hid_ref, hid_out), (slope_ref, slope_out), (shrunk_ref, shrunk_out))):
            copies.append(pltpu.make_async_copy(kept.at[rows], out.at[rows], sems.at[p, at]))
            copies[-1].start()
    turn_rows(filt_ref, points_ref, turn_inv_ref[...], swap_ref[...], chunk)
    pack_all(points_ref, send_ref)
    for copy in copies:
        copy.wait()


def mix_kernel(
    lat_rows, block_size, sub,
    box_ref, row_ref, recv_ref, token_ref, hole_ref, gain_ref, shift_ref,
    post_gain_ref, post_shift_ref, table_ref,
    mixed, post_ref,
):
    items, cells, width = token_ref.shape
    pad = post_ref.shape[1] - cells
    backs = [get_modes(recv_ref, item, block_size, sub) for item in range(items)]
    units = [norm_parts(token_ref[item].astype(f32))[0] for item in range(items)]
    for item in range(items):
        valid = as_column(valid_row(item, box_ref, row_ref, hole_ref, lat_rows, cells))
        normed = units[item] * line(gain_ref) + line(shift_ref)
        filtered = dot(table_ref[...], backs[item], 1, 0)
        value = token_ref[item].astype(f32) + normed + valid * filtered
        mixed[item] = value
        unit, _ = norm_parts(value)
        post_ref[item, :cells] = (unit * line(post_gain_ref) + line(post_shift_ref)).astype(bf16)
        if pad:
            post_ref[item, cells:] = jnp.zeros((pad, width), bf16)


def feed_kernel(
    cuts, shares, runs, run,
    bit_ref, core_ref, post_own, post_other, cot_own, cot_other, expand_far, reduce_far, bias_ref,
    *refs,
):
    far_refs, refs = refs[:6], refs[6:]
    bias_grad, out_own, grad_own, out_other_ref, grad_other_ref, *refs = refs
    post_ref, cot_ref, expand_ref, reduce_ref, hidden_ref, grad_ref, *refs = refs
    expand_grad_ref, reduce_grad_ref, row_sems, weight_sems, far_sems = refs
    rows = post_own.shape[0]
    arrivals = []
    for at, (source, to) in enumerate(((post_own, post_ref), (post_other, post_ref), (cot_own, cot_ref), (cot_other, cot_ref))):
        here = slice(at % 2 * rows, (at % 2 + 1) * rows)
        arrivals.append(pltpu.make_async_copy(source, to.at[here], row_sems.at[at]))
    fetches = []
    for r in range(runs):
        start = pl.multiple_of((2 * r + core_ref[0]) * run, 128)
        here, there = slice(r * run, (r + 1) * run), pl.ds(start, run)
        fetches.append(pltpu.make_async_copy(expand_far.at[:, there], expand_ref.at[:, here], weight_sems.at[0, r]))
        fetches.append(pltpu.make_async_copy(reduce_far.at[there], reduce_ref.at[here], weight_sems.at[1, r]))
    waves = [arrivals[:2] + fetches[:1], arrivals[2:] + fetches[1:2]] + [fetches[2 * r : 2 * r + 2] for r in range(1, runs)]

    def turn_over(at):
        for copy in waves[at]:
            copy.wait()
        for copy in waves[at + 1] if at + 1 < len(waves) else ():
            copy.start()

    for copy in waves[0]:
        copy.start()
    turn_over(0)
    post = post_ref[...]
    for r in range(runs):
        here = slice(r * run, (r + 1) * run)
        if r:
            turn_over(r + 1)
        start = pl.multiple_of((2 * r + core_ref[0]) * run, 128)
        pre = dot(post, expand_ref[:, here], 1, 0) + bias_ref[:, pl.ds(start, run)]
        hidden, slope = gelu_pair(pre)
        hidden_ref[:, here] = hidden.astype(bf16)
        if not r:
            turn_over(1)
        cot = cot_ref[...]
        grad = (dot(cot, reduce_ref[here], 1, 1) * slope).astype(bf16)
        grad_ref[:, here] = grad
        bias_grad.here[:, here] = jnp.sum(grad.astype(f32), axis=0, keepdims=True)
    bias_grad.start()

    for r in range(runs):
        here = slice(r * run, (r + 1) * run)
        expand_grad_ref[here] = dot(grad_ref[:, here], post, 0, 0).astype(bf16)
        reduce_grad_ref[here] = dot(hidden_ref[:, here], cot, 0, 0).astype(bf16)
    copies = []
    for group, (at, outer) in enumerate(cuts):
        inner = runs * run // (2 * outer)
        own = bit_ref[at]
        to_lanes = 0
        for side, source in enumerate((expand_grad_ref, reduce_grad_ref)):
            lanes = shares[side][group]
            from_lanes = sum(shares[side][:group])
            for o in range(outer):
                for target, half in enumerate((1 - own, own)):
                    start = pl.multiple_of((2 * o + half) * inner, 16)
                    part = source.at[pl.ds(start, inner), from_lanes : from_lanes + lanes]
                    to = far_refs[2 * group + target].at[o * inner : (o + 1) * inner, to_lanes : to_lanes + lanes]
                    copies.append(pltpu.make_async_copy(part, to, far_sems.at[len(copies)]))
                    copies[-1].start()
            to_lanes += lanes

    back = dot(grad_ref[...], expand_ref[...], 1, 1)
    grad_own.here[...] = back[:rows]
    grad_own.start()
    grad_other_ref[...] = back[rows:].astype(bf16)
    out_own.here[...] = dot(hidden_ref[:rows], reduce_ref[...], 1, 0)
    out_own.start()
    out_other_ref[...] = dot(hidden_ref[rows:], reduce_ref[...], 1, 0).astype(bf16)
    for copy in copies:
        copy.wait()


def combine_kernel(places, bit_ref, *refs):
    groups = len(places)
    ins, outs = refs[: 2 * groups], refs[2 * groups :]
    for at, place in enumerate(places):
        keep, recv = ins[2 * at], ins[2 * at + 1]
        low_own = bit_ref[place] == 0
        first, second = keep[:, 0] + recv[:, 0], keep[:, 1] + recv[:, 1]
        outs[2 * at].here[...] = jnp.where(low_own, second, first)
        outs[2 * at].start()
        outs[2 * at + 1].here[...] = jnp.where(low_own, first, second)
        outs[2 * at + 1].start()


def shard_kernel(shares, *refs):
    *ins, expand_ref, reduce_ref = refs
    starts = [0, 0]
    for at in range(len(ins) // 2):
        total = ins[2 * at][...].astype(f32) + ins[2 * at + 1][...].astype(f32)
        begin = 0
        for side, ref in enumerate((expand_ref, reduce_ref)):
            lanes = shares[side][at]
            ref[:, starts[side] : starts[side] + lanes] = total[:, begin : begin + lanes]
            starts[side] += lanes
            begin += lanes


def result_kernel(mixed_ref, out_own_ref, out_other_ref, bias_ref, result_ref):
    cells, items, _ = result_ref.shape
    for item in range(items):
        out = out_own_ref[item, :cells] + out_other_ref[item, :cells].astype(f32)
        value = (mixed_ref[item] + (out + line(bias_ref))).astype(bf16)
        result_ref[:, item, :] = value


def post_kernel(
    lat_rows, block_size, sub,
    box_ref, row_ref, mixed_ref, grad_own_ref, grad_other_ref, cot_ref, hole_ref, gain_ref, table_ref,
    grad_mixed, send_ref, sum_ref, mixed_grad_ref, sems,
):
    items, cells, _ = mixed_grad_ref.shape
    sums = 0.0
    copies, rounded = [], []
    parts = [norm_parts(mixed_ref[item]) for item in range(items)]
    for item in range(items):
        unit, inv_scale = parts[item]
        grad = grad_own_ref[item, :cells] + grad_other_ref[item, :cells].astype(f32)
        cot = cot_ref[item, :cells].astype(f32)
        sums += jnp.concatenate([jnp.sum(v, axis=0, keepdims=True) for v in (grad * unit, grad, cot)], axis=0)
        value = cot + norm_back(grad, unit, inv_scale, line(gain_ref))
        mixed_grad_ref[item] = value
        copies.append(pltpu.make_async_copy(mixed_grad_ref.at[item], grad_mixed.at[item], sems.at[item]))
        copies[-1].start()
        rounded.append(value.astype(bf16))
    for item in range(items):
        valid = valid_row(item, box_ref, row_ref, hole_ref, lat_rows, cells)
        table = (table_ref[...].astype(f32) * valid).astype(bf16)
        put_modes(send_ref, item, dot(table, rounded[item], 1, 0), block_size, sub)
    sum_ref[...] = sums
    for copy in copies:
        copy.wait()


def small_kernel(layout, core_ref, post_sum_ref, expand_bias_ref, small_ref):
    per_run, runs, _ = layout
    small_ref[...] = jnp.zeros_like(small_ref)
    per_line = post_sum_ref.shape[1] // 128
    for line_at in range(3):
        for at in range(per_line):
            row = line_at * per_line + at
            small_ref[row : row + 1] = post_sum_ref[line_at : line_at + 1, at * 128 : (at + 1) * 128]
    for at in range(runs * per_run):
        row = (at // per_run * 2 + core_ref[0]) * per_run + at % per_run
        small_ref[pl.ds(3 * per_line + row, 1)] = expand_bias_ref[:, at * 128 : (at + 1) * 128]


def filter_back_kernel(
    chunk,
    recv_ref, slope_ref, shrunk_ref, inner_ref, outer_ref, turn_fwd_ref, turn_inv_ref, swap_ref,
    send_ref, grad_mid, grad_pre, bias_ref,
    turned_ref, points_ref,
):
    lat_count, points, wide = turned_ref.shape
    grad_mid_ref, grad_pre_ref = grad_mid.here, grad_pre.here
    unpack_all(recv_ref, points_ref)
    turn_rows(points_ref, turned_ref, turn_fwd_ref[...], swap_ref[...], chunk)
    inner_bias = jnp.zeros((1, wide), f32)
    outer_bias = jnp.zeros((1, wide), f32)
    for p in range(0, lat_count, GROUP):
        rows, dims, flat = slice(p, p + GROUP), (GROUP, points, wide), (GROUP * points, wide)
        mid = (turned_ref[rows].astype(f32) * shrunk_ref[rows]).astype(bf16).reshape(flat)
        grad_mid_ref[rows] = mid.reshape(dims)
        outer_bias += jnp.sum(mid.astype(f32), axis=0, keepdims=True)
        pre = (dot(mid, outer_ref[...], 1, 1) * slope_ref[rows].reshape(flat)).astype(bf16)
        grad_pre_ref[rows] = pre.reshape(dims)
        inner_bias += jnp.sum(pre.astype(f32), axis=0, keepdims=True)
        turned_ref[rows] = dot(pre, inner_ref[...], 1, 1).astype(bf16).reshape(dims)
    grad_mid.start()
    grad_pre.start()
    turn_rows(turned_ref, points_ref, turn_inv_ref[...], swap_ref[...], chunk)
    pack_all(points_ref, send_ref)
    bias_ref[0:1] = inner_bias
    bias_ref[1:2] = outer_bias


def filter_weight_kernel(
    bias_row, blocks, place_ref, spec_ref, hid_ref, grad_mid_ref, grad_pre_ref, bias_ref, small_in_ref,
    send_ref, keep_ref, small_ref,
):
    lat_count, points, wide = spec_ref.shape
    flat, half = (lat_count * points, wide), wide // 2
    own = place_ref[0]
    count = small_ref.shape[0] // 2
    base = keep_ref.shape[0] - count
    small_ref[...] = small_in_ref[...]
    for at in range(2):
        for side in range(2):
            row = bias_row + (2 * at + side) * blocks + place_ref[1]
            small_ref[pl.ds(row, 1), :half] = bias_ref[at : at + 1, side * half : (side + 1) * half]
    for at, (left, right) in enumerate(((spec_ref, grad_pre_ref), (hid_ref, grad_mid_ref))):
        grad = dot(left[...].reshape(flat), right[...].reshape(flat), 0, 0)
        first = grad[:half, :half] + grad[half:, half:]
        second = grad[:half, half:] - grad[half:, :half]
        top, rest = pack(jnp.concatenate([first, second], axis=1))
        share = small_ref[at * count : (at + 1) * count]

        @pl.when(own == at)
        def _():
            keep_ref[:half] = top
            keep_ref[half:base] = rest
            keep_ref[base:] = share

        @pl.when(own != at)
        def _():
            send_ref[:half] = top
            send_ref[half:base] = rest
            send_ref[base:] = share


def halve_kernel(base, place_ref, own_ref, recv_ref, send_ref, keep_ref):
    low_own = place_ref[2] == 0
    total = own_ref[...] + recv_ref[...]
    at = 0
    for begin, end in ((0, base), (base, total.shape[0])):
        count = (end - begin) // 2
        first, second = total[begin : begin + count], total[begin + count : end]
        send_ref[at : at + count] = jnp.where(low_own, second, first)
        keep_ref[at : at + count] = jnp.where(low_own, first, second)
        at += count


def last_sums_kernel(
    lat_rows, block_size, sub, base,
    box_ref, row_ref, recv_ref, token_ref, grad_mixed_ref, hole_ref, table_ref, own_ref, other_ref,
    tail,
):
    items, cells, width = token_ref.shape
    backs = [get_modes(recv_ref, item, block_size, sub) for item in range(items)]
    units = [norm_parts(token_ref[item].astype(f32))[0] for item in range(items)]
    sums = 0.0
    for item in range(items):
        valid = as_column(valid_row(item, box_ref, row_ref, hole_ref, lat_rows, cells))
        grad = grad_mixed_ref[item] + valid * dot(table_ref[...], backs[item], 1, 0)
        sums += jnp.concatenate([jnp.sum(v, axis=0, keepdims=True) for v in (grad * units[item], grad)], axis=0)

    rows = own_ref.shape[0] - base
    total = own_ref[...] + other_ref[...]
    value_ref = tail.here.at[0]
    value_ref[:base] = total[:base].astype(bf16)
    value_ref[base : base + rows] = total[base:].astype(bf16)
    per_line, at = width // 128, base + rows
    value_ref[at:] = jnp.zeros((value_ref.shape[0] - at, 128), bf16)
    for i in range(2):
        for j in range(per_line):
            row = at + i * per_line + j
            value_ref[row : row + 1] = sums[i : i + 1, j * 128 : (j + 1) * 128].astype(bf16)
    value = value_ref[...]
    for group in range(1, tail.shape[0]):
        tail.here[group] = value
    tail.start()


def last_kernel(
    lat_rows, block_size, sub,
    box_ref, row_ref, recv_ref, token_ref, grad_mixed_ref, hole_ref, gain_ref, table_ref,
    result, result_ref, sems,
):
    items, cells, width = token_ref.shape
    copies = []
    for item in range(items):
        back = get_modes(recv_ref, item, block_size, sub)
        unit, inv_scale = norm_parts(token_ref[item].astype(f32))
        valid = as_column(valid_row(item, box_ref, row_ref, hole_ref, lat_rows, cells))
        grad = grad_mixed_ref[item] + valid * dot(table_ref[...], back, 1, 0)
        value = grad_mixed_ref[item] + norm_back(grad, unit, inv_scale, line(gain_ref))
        result_ref[item] = value[:, None, :]
        copies.append(pltpu.make_async_copy(result_ref.at[item], result.at[item], sems.at[item]))
        copies[-1].start()
    for copy in copies:
        copy.wait()


def put_split(ref, at, value):
    high = value.astype(bf16)
    rows = value.shape[0]
    ref[at : at + rows] = high
    ref[at + rows : at + 2 * rows] = (value - high.astype(f32)).astype(bf16)


def get_split(ref, at, rows):
    return ref[at : at + rows].astype(f32) + ref[at + rows : at + 2 * rows].astype(f32)


def third_kernel(sub, base, rows, pre_rows, recv_ref, *refs):
    *other_refs, out_ref = refs
    blocks = recv_ref.shape[0] // sub
    total = 0.0
    for block in range(blocks):
        part = recv_ref[block * sub]
        out_ref[block * base : (block + 1) * base] = part[:base]
        total += part[base : base + rows].astype(f32)
    put_split(out_ref, blocks * base, total)
    total = jnp.sum(recv_ref[:, base + rows : base + rows + pre_rows].astype(f32), axis=0)
    for ref in other_refs:
        total += jnp.sum(ref[...].astype(f32), axis=0)
    put_split(out_ref, blocks * base + 2 * rows, total)


def pass_kernel(in_ref, out_ref):
    out_ref[...] = in_ref[...]


def tail_kernel(
    count, rows, pre_rows, place_ref, *refs,
):
    parts, refs = refs[:count], refs[count:]
    (
        pre_gain_ref, pre_shift_ref, inner_ref, inner_bias_ref, outer_ref, outer_bias_ref,
        post_gain_ref, post_shift_ref, expand_bias_ref, reduce_bias_ref, small_ref,
    ) = refs
    own, y_own = place_ref[0], place_ref[2]

    def in_order(values):
        if count == 4:
            pairs = [values[0:2], values[2:4]]
            sides = [
                [jnp.where(y_own == 0, a, b), jnp.where(y_own == 0, b, a)] for a, b in pairs
            ]
        else:
            sides = [values[0:1], values[1:2]]
        joined = [jnp.concatenate(side, axis=0) if len(side) > 1 else side[0] for side in sides]
        return jnp.where(own == 0, joined[0], joined[1]), jnp.where(own == 0, joined[1], joined[0])

    pre_at = parts[0].shape[0] - 2 * pre_rows
    small_at = pre_at - 2 * rows
    for at, value in enumerate(in_order([get_split(ref, small_at, rows) for ref in parts])):
        small_ref[at * value.shape[0] : (at + 1) * value.shape[0]] = value
    per_line = pre_gain_ref.shape[0] // 128
    sums = sum(get_split(ref, pre_at, pre_rows) for ref in parts)

    def put(ref, at, value):
        ref[pl.ds(at * 128, 128)] = value.reshape(128)

    for i, ref in enumerate((pre_gain_ref, pre_shift_ref)):
        for j in range(per_line):
            put(ref, j, sums[i * per_line + j : i * per_line + j + 1])

    def row(at):
        return small_ref[at : at + 1]

    at = 0
    for ref in (post_gain_ref, post_shift_ref, reduce_bias_ref, expand_bias_ref):
        for j in range(ref.shape[0] // 128):
            put(ref, j, row(at))
            at += 1
    _, blocks, size = inner_bias_ref.shape
    for ref in (inner_bias_ref, outer_bias_ref):
        for side in range(2):
            for block in range(blocks):
                ref[side, block : block + 1] = row(at)[:, :size]
                at += 1
    base = small_at // blocks
    for at in range(blocks):
        cuts = [ref[at * base : (at + 1) * base].astype(f32) for ref in parts]
        for ref, value in zip((inner_ref, outer_ref), in_order(cuts)):
            value = unpack(value)
            for side in range(2):
                ref[side, at] = value[:, side * size : (side + 1) * size]


class Far:
    def __init__(self, far_ref, here_ref, sem, incoming):
        pair = (far_ref, here_ref) if incoming else (here_ref, far_ref)
        self.here, self.copy, self.pending = here_ref, pltpu.make_async_copy(*pair, sem), False
        if incoming:
            self.start()

    def start(self):
        self.copy.start()
        self.pending = True

    def wait(self):
        if self.pending:
            self.copy.wait()
            self.pending = False

    @property
    def shape(self):
        return self.here.shape

    def __getitem__(self, index):
        self.wait()
        return self.here[index]


def call(kernel, out_shape, args, prefetch=0, scratch=(), flops=0, vmem=16, after=(), far_in=(), far_out=(), raw=(), loose=()):
    args, after = tuple(args), tuple(after)
    far_out = [len(args) + i for i in far_out]
    raw = set(i if i >= 0 else len(args) - 1 - i for i in raw)
    far = list(far_in) + far_out
    count = len(args) + len(out_shape)
    every = list(args) + list(out_shape)
    anywhere = pl.BlockSpec(memory_space=pl.ANY)

    def spec(i):
        if i in far or i in raw:
            return anywhere
        dims = every[i].shape
        rest = (0,) * len(dims)
        return pl.BlockSpec(tuple(dims), lambda *_: rest)

    def whole_kernel(*refs):
        refs = list(refs[: len(args)]) + list(refs[len(args) + len(after) :])
        sems = refs.pop() if far else None
        buffers = [refs.pop() for _ in far][::-1]
        fars = {}
        for at, i in enumerate(far):
            fars[i] = refs[i] = Far(refs[i], buffers[at], sems.at[at], i < len(args))
        kernel(*refs)
        for value in fars.values():
            value.wait()

    moved = sum(math.prod(a.shape) * np.dtype(a.dtype).itemsize for a in every)
    fixed = [pltpu.with_memory_space_constraint(a, pltpu.HBM) if i in far and i not in loose else a for i, a in enumerate(args)]
    shapes = [
        pltpu.HBM(a.shape, a.dtype) if i in far_out or i in raw else a for i, a in enumerate(out_shape, len(args))
    ]
    scratch = list(scratch) + [pltpu.VMEM(every[i].shape, every[i].dtype) for i in far]
    if far:
        scratch.append(pltpu.SemaphoreType.DMA((len(far),)))
    return pl.pallas_call(
        whole_kernel,
        out_shape=shapes,
        grid_spec=pltpu.PrefetchScalarGridSpec(
            num_scalar_prefetch=prefetch,
            grid=(1,),
            in_specs=[spec(i) for i in range(prefetch, len(args))] + [anywhere] * len(after),
            out_specs=[spec(i) for i in range(len(args), count)],
            scratch_shapes=scratch,
        ),
        compiler_params=pltpu.CompilerParams(
            dimension_semantics=("arbitrary",), vmem_limit_bytes=vmem << 20
        ),
        cost_estimate=pl.CostEstimate(flops=int(flops), bytes_accessed=int(moved), transcendentals=0),
    )(*fixed, *after)


def shape(dims, dtype):
    return jax.ShapeDtypeStruct(tuple(dims), dtype)


def stay(operand):
    return pltpu.with_memory_space_constraint(operand, pltpu.HBM)


def pair_swap(operand, axis_name, bit):
    size = lax.axis_size(axis_name)
    return lax.ppermute(operand, axis_name, [(i, i ^ bit) for i in range(size)])


def axis_bits(axis_name):
    size = lax.axis_size(axis_name)
    return [1 << i for i in range(size.bit_length() - 1)]


def body(
    tokens,
    boxes,
    patch_mask,
    pre_gain,
    pre_shift,
    filter_inner,
    filter_inner_bias,
    filter_outer,
    filter_outer_bias,
    post_gain,
    post_shift,
    expand_weight,
    expand_bias,
    reduce_weight,
    reduce_bias,
    cotangent,
):
    micro_count, crop_count, lat_rows, cells, width = tokens.shape
    groups = lax.axis_size("lat")
    lat_count = lat_rows * groups
    block_count, block_size = filter_inner.shape[1:3]
    sub = groups // block_count
    modes_own = MODES // sub
    crops = micro_count * crop_count
    items = crops * lat_rows
    points = crops * modes_own
    wide = 2 * block_size
    padded = -(-cells // 16) * 16
    rows = items * padded
    chunk = 16
    hidden_width = expand_weight.shape[1]
    dp_size = lax.axis_size("dp")
    lat_index, dp_index = lax.axis_index("lat"), lax.axis_index("dp")
    own_block = lat_index // sub
    tables = {k: jnp.asarray(v) for k, v in make_tables(cells, lat_count, block_size, chunk).items()}

    box = stay(boxes)
    own_row = (lat_index * lat_rows).astype(jnp.int32).reshape(1)
    core = dp_index % 2
    token_items = tokens.reshape(items, cells, width)
    cot_pad = jnp.pad(cotangent.reshape(items, cells, width), ((0, 0), (0, padded - cells), (0, 0)))
    holes = patch_mask.reshape(items, 1, cells)
    row_item = (items, cells, width)
    pad_item = (items, padded, width)
    packed = modes_own * 3 // 2
    mode_dims = (groups, items, packed, 128)
    names = (lat_rows, block_size, sub)
    lon_flops = 2 * items * 2 * MODES * cells * width

    def exchange(both, by_rows):
        if by_rows:
            both = both.reshape(groups, crops, lat_rows, packed, 128).swapaxes(1, 2)
            both = both.reshape(groups, items * packed, 128)
            both = lax.all_to_all(both, "lat", 0, 0, tiled=True)
            return both.reshape(lat_count, crops, packed, 128)
        both = both.reshape(groups, items * packed, 128)
        both = lax.all_to_all(both, "lat", 0, 0, tiled=True)
        both = both.reshape(groups, lat_rows, crops, packed, 128).swapaxes(1, 2)
        return both.reshape(mode_dims)

    def own_matrix(matrix):
        pair = lax.dynamic_index_in_dim(matrix, own_block, 1, keepdims=False)
        top = jnp.concatenate([pair[0], pair[1]], axis=1)
        under = jnp.concatenate([-pair[1], pair[0]], axis=1)
        return jnp.concatenate([top, under], axis=0)

    def own_bias(bias):
        return lax.dynamic_index_in_dim(bias, own_block, 1, keepdims=False).reshape(1, wide)

    args = (box, own_row, token_items, holes, pre_gain, pre_shift, tables["fwd"])
    (send,) = call(
        functools.partial(pre_kernel, *names),
        [shape(mode_dims, bf16)],
        args,
        prefetch=2,
        far_in=range(3, 7),
        flops=lon_flops,
    )
    recv = exchange(send, True)
    cot_other = pair_swap(cot_pad.reshape(rows, width), "dp", 1)

    spectrum = (lat_count, points, wide)
    grid_dims = (lat_count, crops, packed, 128)
    filter_flops = 4 * lat_count * points * wide * wide
    inner, outer = own_matrix(filter_inner), own_matrix(filter_outer)
    turns = (tables["turn_fwd"], tables["turn_inv"], tables["swap"])
    args = (recv, inner, own_bias(filter_inner_bias), outer, own_bias(filter_outer_bias), *turns)
    send, spec, hid, slope, shrunk = call(
        functools.partial(filter_kernel, chunk),
        [shape(grid_dims, bf16)] + [shape(spectrum, t) for t in (bf16, bf16, f32, f32)],
        args,
        far_in=(5, 6, 7),
        far_out=(1,),
        raw=(-3, -4, -5),
        scratch=[pltpu.VMEM(spectrum, t) for t in (bf16, f32, f32, bf16, bf16)]
        + [pltpu.SemaphoreType.DMA((lat_count, 3))],
        flops=filter_flops,
    )
    recv = exchange(send, False)

    args = (
        box, own_row, recv, token_items, holes, pre_gain, pre_shift, post_gain, post_shift, tables["inv_t"],
    )
    mixed, post = call(
        functools.partial(mix_kernel, *names),
        [shape(row_item, f32), shape(pad_item, bf16)],
        args,
        prefetch=2,
        far_in=range(4, 10),
        flops=lon_flops,
    )
    post = post.reshape(rows, width)
    post_other = pair_swap(post, "dp", 1)

    dp_bits = [("dp", b) for b in axis_bits("dp")[1:]]
    lat_bits = [("lat", b) for b in axis_bits("lat")]
    bit_names = dp_bits[::-1] + lat_bits[::-1]
    own_bits = jnp.stack([(lax.axis_index(n) // b) % 2 for n, b in bit_names]).astype(jnp.int32)
    own_rows = hidden_width // (dp_size * groups)
    half = hidden_width // 2
    run = hidden_width // dp_size
    runs = dp_size // 2
    core_bit = core.astype(jnp.int32).reshape(1)

    whole_rows = [n for n in lat_bits if own_rows * n[1] % 16 == 0]
    orders = [
        dp_bits + lat_bits,
        whole_rows[:1] + [n for n in lat_bits[:-1] if n != whole_rows[0]] + dp_bits + lat_bits[-1:],
        whole_rows[1:2] + dp_bits + [n for n in lat_bits if n != whole_rows[1]],
    ]
    lefts = [list(bit_names) for _ in orders]

    def place_of(step, left):
        return bit_names.index(step), 2 ** left.index(step)

    third = width // 3
    shares = ((third * 3 // 2, third, third // 2), (third,) * 3)
    lanes = [a + b for a, b in zip(*shares)]
    flat, double = (rows, width), (2 * rows, width)
    cuts = [place_of(order[0], left) for order, left in zip(orders, lefts)]
    copy_count = sum(4 * outer for _, outer in cuts)
    args = (
        own_bits, core_bit, post, post_other, stay(cot_pad.reshape(rows, width)), cot_other,
        stay(expand_weight), stay(reduce_weight), expand_bias.reshape(1, hidden_width),
    )
    *parts, grad_b, out_own, grad_own, out_other, grad_other = call(
        functools.partial(feed_kernel, cuts, shares, runs, run),
        [shape((half // 2, n), bf16) for n in lanes for _ in range(2)]
        + [shape((1, half), f32), shape(flat, f32), shape(flat, f32), shape(flat, bf16), shape(flat, bf16)],
        args,
        prefetch=2,
        far_in=(8,),
        far_out=(6, 7, 8),
        raw=tuple(range(2, 8)) + tuple(range(-1, -7, -1)),
        scratch=[pltpu.VMEM(double, bf16)] * 2
        + [pltpu.VMEM((width, half), bf16), pltpu.VMEM((half, width), bf16)]
        + [pltpu.VMEM((2 * rows, half), bf16)] * 2
        + [pltpu.VMEM((half, width), bf16)] * 2
        + [pltpu.SemaphoreType.DMA((4,)), pltpu.SemaphoreType.DMA((2, runs))]
        + [pltpu.SemaphoreType.DMA((copy_count,))],
        flops=6 * 2 * 2 * rows * width * half,
        vmem=52,
    )
    grad_other = pair_swap(grad_other, "dp", 1).reshape(pad_item)
    out_other = pair_swap(out_other, "dp", 1).reshape(pad_item)

    class Scatter:
        def __init__(self):
            self.at, self.sends, self.keeps = 0, list(parts[0::2]), list(parts[1::2])

        def swap(self):
            self.recvs = []
            for send, order, left in zip(self.sends, orders, lefts):
                left.remove(order[self.at])
                self.recvs.append(pair_swap(send, *order[self.at]))
            self.at += 1
            return list(self.recvs)

        def add(self, after=(), flops=0):
            cuts = [place_of(order[self.at], left) for order, left in zip(orders, lefts)]
            left_rows = self.keeps[0].shape[0]
            dims = [(outer, 2, left_rows // (2 * outer), n) for (_, outer), n in zip(cuts, lanes)]
            ins = [v.reshape(d) for keep, recv, d in zip(self.keeps, self.recvs, dims) for v in (keep, recv)]
            outs = call(
                functools.partial(combine_kernel, [place for place, _ in cuts]),
                [shape((d[0], d[2], d[3]), bf16) for d in dims for _ in range(2)],
                (own_bits, *ins),
                prefetch=1,
                far_in=range(1, 7),
                loose=(2, 4, 6),
                far_out=range(6),
                after=after,
                flops=flops,
            )
            outs = [v.reshape(left_rows // 2, v.shape[-1]) for v in outs]
            self.sends, self.keeps = outs[0::2], outs[1::2]
            return outs

    scatter = Scatter()
    scatter.swap()

    args = (
        box, own_row, mixed, grad_own.reshape(pad_item), grad_other, cot_pad, holes, post_gain, tables["inv"],
    )
    grad_mixed, send, post_sums = call(
        functools.partial(post_kernel, *names),
        [shape(row_item, f32), shape(mode_dims, bf16), shape((3, width), f32)],
        args,
        prefetch=2,
        far_in=(3, 5, 7, 8, 6),
        raw=(-1,),
        scratch=[pltpu.VMEM(row_item, f32), pltpu.SemaphoreType.DMA((items,))],
        flops=lon_flops,
    )
    (result,) = call(
        result_kernel,
        [shape((cells, items, width), bf16)],
        (mixed, out_own.reshape(pad_item), out_other, reduce_bias),
        far_in=(1, 3),
        after=(send,),
    )
    recv = exchange(send, True)

    sums = scatter.add((send,), flops=COMBINE_FLOPS)
    scatter.swap()

    bias_row = 3 * width // 128 + hidden_width // 128
    small_rows = -(-(bias_row + 4 * block_count) // 32) * 32
    small_dims = (small_rows, 128)
    (small,) = call(
        functools.partial(small_kernel, (run // 128, runs, block_count)),
        [shape(small_dims, f32)],
        (core_bit, post_sums, grad_b),
        prefetch=1,
    )
    base = block_size * 3 // 2
    y_index = (dp_index // 2) % 2
    places = jnp.stack([core, own_block, y_index]).astype(jnp.int32)
    args = (recv, slope, shrunk, inner, outer, *turns)
    send, grad_mid, grad_pre, filter_bias = call(
        functools.partial(filter_back_kernel, chunk),
        [shape(grid_dims, bf16), shape(spectrum, bf16), shape(spectrum, bf16), shape((2, wide), f32)],
        args,
        far_in=(5, 7, 2, 1, 6),
        far_out=(1, 2),
        scratch=[pltpu.VMEM(spectrum, bf16)] * 2,
        flops=2 * filter_flops,
        after=[stay(v) for v in sums[:1]],
    )
    recv = exchange(send, False)

    halves = len(dp_bits) > 0
    packed_weight = (base + small_rows // 2, 128)
    send_core, keep_core = call(
        functools.partial(filter_weight_kernel, bias_row, block_count),
        [shape(packed_weight, f32)] * 2,
        (places, spec, hid, grad_mid, grad_pre, filter_bias, small),
        prefetch=1,
        far_in=(1, 4, 2, 3),
        scratch=[pltpu.VMEM(small_dims, f32)],
        after=(scatter.recvs[2],),
    )
    weight = [keep_core, pair_swap(send_core, "dp", 1)]
    sums = scatter.add((send, keep_core), flops=COMBINE_FLOPS)
    ahead = scatter.swap()
    own_base, own_small = base, small_rows // 2
    if halves:
        own_base, own_small = base // 2, small_rows // 4
        send_y, keep_y = call(
            functools.partial(halve_kernel, base),
            [shape((own_base + own_small, 128), f32)] * 2,
            (places, *weight),
            prefetch=1,
            after=[stay(sums[0])],
        )
        weight = [keep_y, pair_swap(send_y, *dp_bits[0])]
    for step in dp_bits[1:] + [n for n in lat_bits if n[1] < sub]:
        weight = [weight[0] + weight[1]]
        weight.append(pair_swap(weight[0], *step))
    pre_rows = -(-2 * width // 2048) * 16
    tail_dims = (groups, -(-(own_base + own_small + pre_rows) // 16) * 16, 128)
    (tail_send,) = call(
        functools.partial(last_sums_kernel, *names, own_base),
        [shape(tail_dims, bf16)],
        (box, own_row, recv, token_items, grad_mixed, holes, tables["fwd_t"], *weight),
        prefetch=2,
        far_in=(6, 5, 4),
        far_out=(0,),
        flops=lon_flops,
    )
    result_dims = (items, cells, 1, width)
    (grad_tokens,) = call(
        functools.partial(last_kernel, *names),
        [shape(result_dims, f32)],
        (box, own_row, recv, token_items, grad_mixed, holes, pre_gain, tables["fwd_t"]),
        prefetch=2,
        far_in=(7, 5, 4, 6),
        raw=(-1,),
        scratch=[pltpu.VMEM(result_dims, f32), pltpu.SemaphoreType.DMA((items,))],
        flops=lon_flops,
        after=(stay(tail_send),),
    )
    tail = tail_send
    tail = lax.all_to_all(tail, "lat", 0, 0, tiled=True)

    while scatter.at < len(bit_names):
        sums = scatter.add((stay(tail_send),), flops=COMBINE_FLOPS)
        scatter.swap()
    merged = [v for pair in zip(scatter.keeps, scatter.recvs) for v in pair]
    expand_part, reduce_part = call(
        functools.partial(shard_kernel, shares),
        [shape((own_rows, width), f32)] * 2,
        merged,
        far_in=range(6),
        loose=(1, 3, 5),
                flops=COMBINE_FLOPS,
        after=(result, stay(grad_tokens), tail),
    )
    expand_part = expand_part.T
    extra = [n[1] for n in dp_bits[1:]]
    masks = [sum(b for i, b in enumerate(extra) if m >> i & 1) for m in range(1, 2 ** len(extra))]
    others = [pair_swap(tail[:, own_base + own_small : own_base + own_small + pre_rows], "dp", m) for m in masks]
    third_dims = (block_count * own_base + 2 * own_small + 2 * pre_rows, 128)
    (third,) = call(
        functools.partial(third_kernel, sub, own_base, own_small, pre_rows),
        [shape(third_dims, bf16)],
        (tail, *others),
        after=(stay(sums[0]),),
    )
    thirds = [third]
    if halves:
        thirds.append(pair_swap(third, *dp_bits[0]))
    (last,) = call(
        pass_kernel,
        [shape(third_dims, bf16)],
        thirds[-1:],
        after=(stay(reduce_part),),
    )
    thirds += [pair_swap(v, "dp", 1) for v in thirds[:-1] + [last]]

    args = (places, *thirds)
    line_dims = (width,)
    filter_dims, bias_dims = filter_inner.shape, filter_inner_bias.shape
    out_dims = [line_dims, line_dims, filter_dims, bias_dims, filter_dims, bias_dims]
    out_dims += [line_dims, line_dims, (hidden_width,), line_dims]
    sums = call(
        functools.partial(tail_kernel, len(thirds), own_small, pre_rows),
        [shape(d, f32) for d in out_dims],
        args,
        prefetch=1,
        scratch=[pltpu.VMEM(small_dims, f32)],
    )
    return (
        result.swapaxes(0, 1).reshape(tokens.shape),
        grad_tokens.reshape(tokens.shape),
        *sums[:8],
        expand_part,
        sums[8],
        reduce_part,
        sums[9],
    )


def solution(mesh):
    rows = P(None, "dp", "lat", None, None)
    in_specs = (rows, P(None, "dp", None), P(None, "dp", "lat", None)) + (P(),) * 12 + (rows,)
    out_specs = (
        (rows, rows)
        + (P(),) * 8
        + (P(None, ("dp", "lat")), P(), P(("dp", "lat"), None), P())
    )
    return jax.shard_map(body, mesh=mesh, in_specs=in_specs, out_specs=out_specs, check_vma=False)
```

```python
import functools
import math

import jax
import jax.numpy as jnp
import ml_dtypes
import numpy as np
from jax import lax
from jax.experimental import pallas as pl
from jax.experimental.pallas import tpu as pltpu
from jax.sharding import PartitionSpec as P

MODES = 64
GROUP = 4
COMBINE_FLOPS = 2 * 10**10
shrink_level = 0.01
epsilon = 1e-05
inv_root_two = 1.0 / math.sqrt(2.0)
inv_root_tau = 1.0 / math.sqrt(2.0 * math.pi)
f32 = jnp.float32
bf16 = jnp.bfloat16


def table_pair(out_count, in_count, length):
    phase = np.arange(out_count)[:, None] * np.arange(in_count)[None, :] % length
    angle = phase.astype(np.float32) * np.float32(2.0 * math.pi / length)
    return np.cos(angle).astype(np.float32), np.sin(angle).astype(np.float32)


def low(values):
    return values.astype(np.float32).astype(ml_dtypes.bfloat16)


def make_tables(lon_cells, lat_count, block_size, chunk):
    lon_factor = np.float32(1.0 / math.sqrt(lon_cells))
    cosine, sine = table_pair(MODES, lon_cells, lon_cells)
    weight = np.where(np.arange(MODES) == 0, 1.0, 2.0).astype(np.float32)[:, None]
    forward = low(np.concatenate([cosine, -sine]) * lon_factor)
    inverse = low(np.concatenate([cosine * weight, -sine * weight]) * lon_factor)
    cosine, sine = table_pair(lat_count, lat_count, lat_count)
    lat_factor = np.float32(1.0 / math.sqrt(lat_count))
    same = np.eye(chunk, dtype=np.float32)
    cosine = np.kron(low(cosine * lat_factor).astype(np.float32), same)
    sine = np.kron(low(sine * lat_factor).astype(np.float32), same)
    turn_fwd = low(np.concatenate([cosine, sine], axis=1))
    turn_inv = low(np.concatenate([cosine, -sine], axis=1))
    eye, none = np.eye(block_size), np.zeros((block_size, block_size))
    swap = low(np.block([[none, -eye], [eye, none]]))
    return dict(
        fwd=forward, fwd_t=forward.T.copy(), inv=inverse, inv_t=inverse.T.copy(),
        turn_fwd=turn_fwd, turn_inv=turn_inv, swap=swap,
    )


def dot(a, b, ca, cb):
    return lax.dot_general(a, b, (((ca,), (cb,)), ((), ())), preferred_element_type=f32)


def line(ref):
    return ref[...].reshape(1, -1)


def row_mean(values):
    return jnp.sum(values, axis=-1, keepdims=True) * (1.0 / values.shape[-1])


def norm_parts(values):
    centered = values - row_mean(values)
    inv_scale = lax.rsqrt(row_mean(centered * centered) + epsilon)
    return centered * inv_scale, inv_scale


def norm_back(grad_normed, unit_values, inv_scale, gain):
    grad_unit = grad_normed * gain
    plain, cross = row_mean(grad_unit), row_mean(grad_unit * unit_values)
    return inv_scale * (grad_unit - plain - unit_values * cross)


def gelu_pair(values):
    half = 0.5 * (1.0 + lax.erf(values * inv_root_two))
    return values * half, half + values * jnp.exp(-0.5 * values * values) * inv_root_tau


def shrink_pair(values):
    inverse = lax.rsqrt(values * values + shrink_level * shrink_level)
    slope = 1.0 - shrink_level * shrink_level * shrink_level * inverse * inverse * inverse
    return values - shrink_level * values * inverse, slope


def valid_row(item, box_ref, row_ref, hole_ref, lat_rows, cells):
    crop, row = item // lat_rows, row_ref[0] + item % lat_rows
    crop_count = box_ref.shape[1]
    micro, crop = crop // crop_count, crop % crop_count
    limit = jnp.where(row < box_ref[micro, crop, 0], box_ref[micro, crop, 1], 0)
    column = lax.broadcasted_iota(jnp.int32, (1, cells), 1)
    return jnp.where((column < limit) & (hole_ref[item] > 0), 1.0, 0.0)


def as_column(row):
    cells = row.shape[1]
    down = lax.broadcasted_iota(jnp.int32, (cells, cells), 0)
    along = lax.broadcasted_iota(jnp.int32, (cells, cells), 1)
    return jnp.sum(jnp.where(down == along, row, 0.0), axis=1, keepdims=True)


def pack(both):
    half = both.shape[0] // 2
    rest = both[:, 128:]
    return both[:, :128], jnp.concatenate([rest[:half], rest[half:]], axis=1)


def unpack(packed):
    points = packed.shape[0] * 2 // 3
    rest = packed[points:]
    rest = jnp.concatenate([rest[:, :64], rest[:, 64:]], axis=0)
    return jnp.concatenate([packed[:points], rest], axis=1)


def put_modes(send_ref, item, spectrum, block_size, sub):
    spectrum = spectrum.astype(bf16)
    own = MODES // sub
    for block in range(spectrum.shape[1] // block_size):
        cut = spectrum[:, block * block_size : (block + 1) * block_size]
        both = jnp.concatenate([cut[:MODES], cut[MODES:]], axis=1)
        for j in range(sub):
            top, rest = pack(both[j * own : (j + 1) * own])
            send_ref[block * sub + j, item, :own] = top
            send_ref[block * sub + j, item, own:] = rest


def get_modes(recv_ref, item, block_size, sub):
    groups = recv_ref.shape[0]
    real, imag = [], []
    for block in range(groups // sub):
        parts = [unpack(recv_ref[block * sub + j, item]) for j in range(sub)]
        both = parts[0] if sub == 1 else jnp.concatenate(parts, axis=0)
        real.append(both[:, :block_size])
        imag.append(both[:, block_size:])
    real, imag = jnp.concatenate(real, axis=1), jnp.concatenate(imag, axis=1)
    return jnp.concatenate([real, imag], axis=0)


def unpack_all(recv_ref, points_ref):
    lat_count, crops, packed, _ = recv_ref.shape
    own = packed * 2 // 3
    for p in range(lat_count):
        for crop in range(crops):
            points_ref[p, crop * own : (crop + 1) * own] = unpack(recv_ref[p, crop])


def pack_all(points_ref, send_ref):
    lat_count, crops, packed, _ = send_ref.shape
    own = packed * 2 // 3
    for p in range(lat_count):
        for crop in range(crops):
            top, rest = pack(points_ref[p, crop * own : (crop + 1) * own])
            send_ref[p, crop, :own] = top
            send_ref[p, crop, own:] = rest


def turn_rows(src_ref, dst_ref, table, swap, chunk):
    lat_count, points, wide = src_ref.shape
    for at in range(0, points, chunk):
        piece = src_ref[:, at : at + chunk, :].reshape(lat_count * chunk, wide)
        other = dot(piece, swap, 1, 0).astype(bf16)
        out = dot(table, jnp.concatenate([piece, other], axis=0), 1, 0)
        dst_ref[:, at : at + chunk, :] = out.astype(bf16).reshape(lat_count, chunk, wide)


def pre_kernel(
    lat_rows, block_size, sub,
    box_ref, row_ref, token_ref, hole_ref, gain_ref, shift_ref, table_ref,
    send_ref,
):
    items, cells, _ = token_ref.shape
    units = [norm_parts(token_ref[item].astype(f32))[0] for item in range(items)]
    for item in range(items):
        valid = valid_row(item, box_ref, row_ref, hole_ref, lat_rows, cells)
        normed = (units[item] * line(gain_ref) + line(shift_ref)).astype(bf16)
        table = (table_ref[...].astype(f32) * valid).astype(bf16)
        put_modes(send_ref, item, dot(table, normed, 1, 0), block_size, sub)


def filter_kernel(
    chunk,
    recv_ref, inner_ref, inner_bias_ref, outer_ref, outer_bias_ref, turn_fwd_ref, turn_inv_ref, swap_ref,
    send_ref, spec, hid_out, slope_out, shrunk_out,
    hid_ref, slope_ref, shrunk_ref, filt_ref, points_ref, sems,
):
    unpack_all(recv_ref, points_ref)
    spec_ref = spec.here
    turn_rows(points_ref, spec_ref, turn_fwd_ref[...], swap_ref[...], chunk)
    spec.start()
    copies = []
    lat_count, points, wide = spec_ref.shape
    for p in range(0, lat_count, GROUP):
        rows, dims = slice(p, p + GROUP), (GROUP, points, wide)
        pre = dot(spec_ref[rows].reshape(GROUP * points, wide), inner_ref[...], 1, 0) + inner_bias_ref[...]
        hid, slope = gelu_pair(pre)
        hid = hid.astype(bf16)
        hid_ref[rows] = hid.reshape(dims)
        slope_ref[rows] = slope.reshape(dims)
        mid = dot(hid, outer_ref[...], 1, 0) + outer_bias_ref[...]
        filt, shrunk = shrink_pair(mid)
        filt_ref[rows] = filt.astype(bf16).reshape(dims)
        shrunk_ref[rows] = shrunk.reshape(dims)
        for at, (kept, out) in enumerate(((hid_ref, hid_out), (slope_ref, slope_out), (shrunk_ref, shrunk_out))):
            copies.append(pltpu.make_async_copy(kept.at[rows], out.at[rows], sems.at[p, at]))
            copies[-1].start()
    turn_rows(filt_ref, points_ref, turn_inv_ref[...], swap_ref[...], chunk)
    pack_all(points_ref, send_ref)
    for copy in copies:
        copy.wait()


def mix_kernel(
    lat_rows, block_size, sub,
    box_ref, row_ref, recv_ref, token_ref, hole_ref, gain_ref, shift_ref,
    post_gain_ref, post_shift_ref, table_ref,
    mixed, post_ref,
):
    items, cells, width = token_ref.shape
    pad = post_ref.shape[1] - cells
    backs = [get_modes(recv_ref, item, block_size, sub) for item in range(items)]
    units = [norm_parts(token_ref[item].astype(f32))[0] for item in range(items)]
    for item in range(items):
        valid = as_column(valid_row(item, box_ref, row_ref, hole_ref, lat_rows, cells))
        normed = units[item] * line(gain_ref) + line(shift_ref)
        filtered = dot(table_ref[...], backs[item], 1, 0)
        value = token_ref[item].astype(f32) + normed + valid * filtered
        mixed[item] = value
        unit, _ = norm_parts(value)
        post_ref[item, :cells] = (unit * line(post_gain_ref) + line(post_shift_ref)).astype(bf16)
        if pad:
            post_ref[item, cells:] = jnp.zeros((pad, width), bf16)


def feed_kernel(
    cuts, shares, runs, run,
    bit_ref, core_ref, post_own, post_other, cot_own, cot_other, expand_far, reduce_far, bias_ref,
    *refs,
):
    far_refs, refs = refs[:6], refs[6:]
    bias_grad, out_own, grad_own, out_other_ref, grad_other_ref, *refs = refs
    post_ref, cot_ref, expand_ref, reduce_ref, hidden_ref, grad_ref, *refs = refs
    expand_grad_ref, reduce_grad_ref, row_sems, weight_sems, far_sems = refs
    rows = post_own.shape[0]
    arrivals = []
    for at, (source, to) in enumerate(((post_own, post_ref), (post_other, post_ref), (cot_own, cot_ref), (cot_other, cot_ref))):
        here = slice(at % 2 * rows, (at % 2 + 1) * rows)
        arrivals.append(pltpu.make_async_copy(source, to.at[here], row_sems.at[at]))
    fetches = []
    for r in range(runs):
        start = pl.multiple_of((2 * r + core_ref[0]) * run, 128)
        here, there = slice(r * run, (r + 1) * run), pl.ds(start, run)
        fetches.append(pltpu.make_async_copy(expand_far.at[:, there], expand_ref.at[:, here], weight_sems.at[0, r]))
        fetches.append(pltpu.make_async_copy(reduce_far.at[there], reduce_ref.at[here], weight_sems.at[1, r]))
    waves = [arrivals[:2] + fetches[:1], arrivals[2:] + fetches[1:2]] + [fetches[2 * r : 2 * r + 2] for r in range(1, runs)]

    def turn_over(at):
        for copy in waves[at]:
            copy.wait()
        for copy in waves[at + 1] if at + 1 < len(waves) else ():
            copy.start()

    for copy in waves[0]:
        copy.start()
    turn_over(0)
    post = post_ref[...]
    for r in range(runs):
        here = slice(r * run, (r + 1) * run)
        if r:
            turn_over(r + 1)
        start = pl.multiple_of((2 * r + core_ref[0]) * run, 128)
        pre = dot(post, expand_ref[:, here], 1, 0) + bias_ref[:, pl.ds(start, run)]
        hidden, slope = gelu_pair(pre)
        hidden_ref[:, here] = hidden.astype(bf16)
        if not r:
            turn_over(1)
        cot = cot_ref[...]
        grad = (dot(cot, reduce_ref[here], 1, 1) * slope).astype(bf16)
        grad_ref[:, here] = grad
        bias_grad.here[:, here] = jnp.sum(grad.astype(f32), axis=0, keepdims=True)
    bias_grad.start()

    for r in range(runs):
        here = slice(r * run, (r + 1) * run)
        expand_grad_ref[here] = dot(grad_ref[:, here], post, 0, 0).astype(bf16)
        reduce_grad_ref[here] = dot(hidden_ref[:, here], cot, 0, 0).astype(bf16)
    copies = []
    for group, (at, outer) in enumerate(cuts):
        inner = runs * run // (2 * outer)
        own = bit_ref[at]
        to_lanes = 0
        for side, source in enumerate((expand_grad_ref, reduce_grad_ref)):
            lanes = shares[side][group]
            from_lanes = sum(shares[side][:group])
            for o in range(outer):
                for target, half in enumerate((1 - own, own)):
                    start = pl.multiple_of((2 * o + half) * inner, 16)
                    part = source.at[pl.ds(start, inner), from_lanes : from_lanes + lanes]
                    to = far_refs[2 * group + target].at[o * inner : (o + 1) * inner, to_lanes : to_lanes + lanes]
                    copies.append(pltpu.make_async_copy(part, to, far_sems.at[len(copies)]))
                    copies[-1].start()
            to_lanes += lanes

    back = dot(grad_ref[...], expand_ref[...], 1, 1)
    grad_own.here[...] = back[:rows]
    grad_own.start()
    grad_other_ref[...] = back[rows:].astype(bf16)
    out_own.here[...] = dot(hidden_ref[:rows], reduce_ref[...], 1, 0)
    out_own.start()
    out_other_ref[...] = dot(hidden_ref[rows:], reduce_ref[...], 1, 0).astype(bf16)
    for copy in copies:
        copy.wait()


def combine_kernel(places, bit_ref, *refs):
    groups = len(places)
    ins, outs = refs[: 2 * groups], refs[2 * groups :]
    for at, place in enumerate(places):
        keep, recv = ins[2 * at], ins[2 * at + 1]
        low_own = bit_ref[place] == 0
        first, second = keep[:, 0] + recv[:, 0], keep[:, 1] + recv[:, 1]
        outs[2 * at].here[...] = jnp.where(low_own, second, first)
        outs[2 * at].start()
        outs[2 * at + 1].here[...] = jnp.where(low_own, first, second)
        outs[2 * at + 1].start()


def shard_kernel(shares, *refs):
    *ins, expand_ref, reduce_ref = refs
    starts = [0, 0]
    for at in range(len(ins) // 2):
        total = ins[2 * at][...].astype(f32) + ins[2 * at + 1][...].astype(f32)
        begin = 0
        for side, ref in enumerate((expand_ref, reduce_ref)):
            lanes = shares[side][at]
            ref[:, starts[side] : starts[side] + lanes] = total[:, begin : begin + lanes]
            starts[side] += lanes
            begin += lanes


def result_kernel(mixed_ref, out_own_ref, out_other_ref, bias_ref, result_ref):
    cells, items, _ = result_ref.shape
    for item in range(items):
        out = out_own_ref[item, :cells] + out_other_ref[item, :cells].astype(f32)
        value = (mixed_ref[item] + (out + line(bias_ref))).astype(bf16)
        result_ref[:, item, :] = value


def post_kernel(
    lat_rows, block_size, sub,
    box_ref, row_ref, mixed_ref, grad_own_ref, grad_other_ref, cot_ref, hole_ref, gain_ref, table_ref,
    grad_mixed, send_ref, sum_ref, mixed_grad_ref, sems,
):
    items, cells, _ = mixed_grad_ref.shape
    sums = 0.0
    copies, rounded = [], []
    parts = [norm_parts(mixed_ref[item]) for item in range(items)]
    for item in range(items):
        unit, inv_scale = parts[item]
        grad = grad_own_ref[item, :cells] + grad_other_ref[item, :cells].astype(f32)
        cot = cot_ref[item, :cells].astype(f32)
        sums += jnp.concatenate([jnp.sum(v, axis=0, keepdims=True) for v in (grad * unit, grad, cot)], axis=0)
        value = cot + norm_back(grad, unit, inv_scale, line(gain_ref))
        mixed_grad_ref[item] = value
        copies.append(pltpu.make_async_copy(mixed_grad_ref.at[item], grad_mixed.at[item], sems.at[item]))
        copies[-1].start()
        rounded.append(value.astype(bf16))
    for item in range(items):
        valid = valid_row(item, box_ref, row_ref, hole_ref, lat_rows, cells)
        table = (table_ref[...].astype(f32) * valid).astype(bf16)
        put_modes(send_ref, item, dot(table, rounded[item], 1, 0), block_size, sub)
    sum_ref[...] = sums
    for copy in copies:
        copy.wait()


def small_kernel(layout, core_ref, post_sum_ref, expand_bias_ref, small_ref):
    per_run, runs, _ = layout
    small_ref[...] = jnp.zeros_like(small_ref)
    per_line = post_sum_ref.shape[1] // 128
    for line_at in range(3):
        for at in range(per_line):
            row = line_at * per_line + at
            small_ref[row : row + 1] = post_sum_ref[line_at : line_at + 1, at * 128 : (at + 1) * 128]
    for at in range(runs * per_run):
        row = (at // per_run * 2 + core_ref[0]) * per_run + at % per_run
        small_ref[pl.ds(3 * per_line + row, 1)] = expand_bias_ref[:, at * 128 : (at + 1) * 128]


def filter_back_kernel(
    chunk,
    recv_ref, slope_ref, shrunk_ref, inner_ref, outer_ref, turn_fwd_ref, turn_inv_ref, swap_ref,
    send_ref, grad_mid, grad_pre, bias_ref,
    turned_ref, points_ref,
):
    lat_count, points, wide = turned_ref.shape
    grad_mid_ref, grad_pre_ref = grad_mid.here, grad_pre.here
    unpack_all(recv_ref, points_ref)
    turn_rows(points_ref, turned_ref, turn_fwd_ref[...], swap_ref[...], chunk)
    inner_bias = jnp.zeros((1, wide), f32)
    outer_bias = jnp.zeros((1, wide), f32)
    for p in range(0, lat_count, GROUP):
        rows, dims, flat = slice(p, p + GROUP), (GROUP, points, wide), (GROUP * points, wide)
        mid = (turned_ref[rows].astype(f32) * shrunk_ref[rows]).astype(bf16).reshape(flat)
        grad_mid_ref[rows] = mid.reshape(dims)
        outer_bias += jnp.sum(mid.astype(f32), axis=0, keepdims=True)
        pre = (dot(mid, outer_ref[...], 1, 1) * slope_ref[rows].reshape(flat)).astype(bf16)
        grad_pre_ref[rows] = pre.reshape(dims)
        inner_bias += jnp.sum(pre.astype(f32), axis=0, keepdims=True)
        turned_ref[rows] = dot(pre, inner_ref[...], 1, 1).astype(bf16).reshape(dims)
    grad_mid.start()
    grad_pre.start()
    turn_rows(turned_ref, points_ref, turn_inv_ref[...], swap_ref[...], chunk)
    pack_all(points_ref, send_ref)
    bias_ref[0:1] = inner_bias
    bias_ref[1:2] = outer_bias


def filter_weight_kernel(
    bias_row, blocks, place_ref, spec_ref, hid_ref, grad_mid_ref, grad_pre_ref, bias_ref, small_in_ref,
    send_ref, keep_ref, small_ref,
):
    lat_count, points, wide = spec_ref.shape
    flat, half = (lat_count * points, wide), wide // 2
    own = place_ref[0]
    count = small_ref.shape[0] // 2
    base = keep_ref.shape[0] - count
    small_ref[...] = small_in_ref[...]
    for at in range(2):
        for side in range(2):
            row = bias_row + (2 * at + side) * blocks + place_ref[1]
            small_ref[pl.ds(row, 1), :half] = bias_ref[at : at + 1, side * half : (side + 1) * half]
    for at, (left, right) in enumerate(((spec_ref, grad_pre_ref), (hid_ref, grad_mid_ref))):
        grad = dot(left[...].reshape(flat), right[...].reshape(flat), 0, 0)
        first = grad[:half, :half] + grad[half:, half:]
        second = grad[:half, half:] - grad[half:, :half]
        top, rest = pack(jnp.concatenate([first, second], axis=1))
        share = small_ref[at * count : (at + 1) * count]

        @pl.when(own == at)
        def _():
            keep_ref[:half] = top
            keep_ref[half:base] = rest
            keep_ref[base:] = share

        @pl.when(own != at)
        def _():
            send_ref[:half] = top
            send_ref[half:base] = rest
            send_ref[base:] = share


def halve_kernel(base, place_ref, own_ref, recv_ref, send_ref, keep_ref):
    low_own = place_ref[2] == 0
    total = own_ref[...] + recv_ref[...]
    at = 0
    for begin, end in ((0, base), (base, total.shape[0])):
        count = (end - begin) // 2
        first, second = total[begin : begin + count], total[begin + count : end]
        send_ref[at : at + count] = jnp.where(low_own, second, first)
        keep_ref[at : at + count] = jnp.where(low_own, first, second)
        at += count


def last_sums_kernel(
    lat_rows, block_size, sub, base,
    box_ref, row_ref, recv_ref, token_ref, grad_mixed_ref, hole_ref, table_ref, own_ref, other_ref,
    tail,
):
    items, cells, width = token_ref.shape
    backs = [get_modes(recv_ref, item, block_size, sub) for item in range(items)]
    units = [norm_parts(token_ref[item].astype(f32))[0] for item in range(items)]
    sums = 0.0
    for item in range(items):
        valid = as_column(valid_row(item, box_ref, row_ref, hole_ref, lat_rows, cells))
        grad = grad_mixed_ref[item] + valid * dot(table_ref[...], backs[item], 1, 0)
        sums += jnp.concatenate([jnp.sum(v, axis=0, keepdims=True) for v in (grad * units[item], grad)], axis=0)

    rows = own_ref.shape[0] - base
    total = own_ref[...] + other_ref[...]
    value_ref = tail.here.at[0]
    value_ref[:base] = total[:base].astype(bf16)
    value_ref[base : base + rows] = total[base:].astype(bf16)
    per_line, at = width // 128, base + rows
    value_ref[at:] = jnp.zeros((value_ref.shape[0] - at, 128), bf16)
    for i in range(2):
        for j in range(per_line):
            row = at + i * per_line + j
            value_ref[row : row + 1] = sums[i : i + 1, j * 128 : (j + 1) * 128].astype(bf16)
    value = value_ref[...]
    for group in range(1, tail.shape[0]):
        tail.here[group] = value
    tail.start()


def last_kernel(
    lat_rows, block_size, sub,
    box_ref, row_ref, recv_ref, token_ref, grad_mixed_ref, hole_ref, gain_ref, table_ref,
    result, result_ref, sems,
):
    items, cells, width = token_ref.shape
    copies = []
    for item in range(items):
        back = get_modes(recv_ref, item, block_size, sub)
        unit, inv_scale = norm_parts(token_ref[item].astype(f32))
        valid = as_column(valid_row(item, box_ref, row_ref, hole_ref, lat_rows, cells))
        grad = grad_mixed_ref[item] + valid * dot(table_ref[...], back, 1, 0)
        value = grad_mixed_ref[item] + norm_back(grad, unit, inv_scale, line(gain_ref))
        result_ref[item] = value[:, None, :]
        copies.append(pltpu.make_async_copy(result_ref.at[item], result.at[item], sems.at[item]))
        copies[-1].start()
    for copy in copies:
        copy.wait()


def put_split(ref, at, value):
    high = value.astype(bf16)
    rows = value.shape[0]
    ref[at : at + rows] = high
    ref[at + rows : at + 2 * rows] = (value - high.astype(f32)).astype(bf16)


def get_split(ref, at, rows):
    return ref[at : at + rows].astype(f32) + ref[at + rows : at + 2 * rows].astype(f32)


def third_kernel(sub, base, rows, pre_rows, recv_ref, *refs):
    *other_refs, out_ref = refs
    blocks = recv_ref.shape[0] // sub
    total = 0.0
    for block in range(blocks):
        part = recv_ref[block * sub]
        out_ref[block * base : (block + 1) * base] = part[:base]
        total += part[base : base + rows].astype(f32)
    put_split(out_ref, blocks * base, total)
    total = jnp.sum(recv_ref[:, base + rows : base + rows + pre_rows].astype(f32), axis=0)
    for ref in other_refs:
        total += jnp.sum(ref[...].astype(f32), axis=0)
    put_split(out_ref, blocks * base + 2 * rows, total)


def gate_kernel(place_ref, out_ref):
    out_ref[...] = jnp.zeros_like(out_ref)


def pass_kernel(in_ref, out_ref):
    out_ref[...] = in_ref[...]


def tail_kernel(
    count, rows, pre_rows, place_ref, *refs,
):
    parts, refs = refs[:count], refs[count:]
    (
        pre_gain_ref, pre_shift_ref, inner_ref, inner_bias_ref, outer_ref, outer_bias_ref,
        post_gain_ref, post_shift_ref, expand_bias_ref, reduce_bias_ref, small_ref,
    ) = refs
    own, y_own = place_ref[0], place_ref[2]

    def in_order(values):
        if count == 4:
            pairs = [values[0:2], values[2:4]]
            sides = [
                [jnp.where(y_own == 0, a, b), jnp.where(y_own == 0, b, a)] for a, b in pairs
            ]
        else:
            sides = [values[0:1], values[1:2]]
        joined = [jnp.concatenate(side, axis=0) if len(side) > 1 else side[0] for side in sides]
        return jnp.where(own == 0, joined[0], joined[1]), jnp.where(own == 0, joined[1], joined[0])

    pre_at = parts[0].shape[0] - 2 * pre_rows
    small_at = pre_at - 2 * rows
    for at, value in enumerate(in_order([get_split(ref, small_at, rows) for ref in parts])):
        small_ref[at * value.shape[0] : (at + 1) * value.shape[0]] = value
    per_line = pre_gain_ref.shape[0] // 128
    sums = sum(get_split(ref, pre_at, pre_rows) for ref in parts)

    def put(ref, at, value):
        ref[pl.ds(at * 128, 128)] = value.reshape(128)

    for i, ref in enumerate((pre_gain_ref, pre_shift_ref)):
        for j in range(per_line):
            put(ref, j, sums[i * per_line + j : i * per_line + j + 1])

    def row(at):
        return small_ref[at : at + 1]

    at = 0
    for ref in (post_gain_ref, post_shift_ref, reduce_bias_ref, expand_bias_ref):
        for j in range(ref.shape[0] // 128):
            put(ref, j, row(at))
            at += 1
    _, blocks, size = inner_bias_ref.shape
    for ref in (inner_bias_ref, outer_bias_ref):
        for side in range(2):
            for block in range(blocks):
                ref[side, block : block + 1] = row(at)[:, :size]
                at += 1
    base = small_at // blocks
    for at in range(blocks):
        cuts = [ref[at * base : (at + 1) * base].astype(f32) for ref in parts]
        for ref, value in zip((inner_ref, outer_ref), in_order(cuts)):
            value = unpack(value)
            for side in range(2):
                ref[side, at] = value[:, side * size : (side + 1) * size]


class Far:
    def __init__(self, far_ref, here_ref, sem, incoming):
        pair = (far_ref, here_ref) if incoming else (here_ref, far_ref)
        self.here, self.copy, self.pending = here_ref, pltpu.make_async_copy(*pair, sem), False
        if incoming:
            self.start()

    def start(self):
        self.copy.start()
        self.pending = True

    def wait(self):
        if self.pending:
            self.copy.wait()
            self.pending = False

    @property
    def shape(self):
        return self.here.shape

    def __getitem__(self, index):
        self.wait()
        return self.here[index]


def call(kernel, out_shape, args, prefetch=0, scratch=(), flops=0, vmem=16, after=(), far_in=(), far_out=(), raw=(), loose=()):
    args, after = tuple(args), tuple(after)
    far_out = [len(args) + i for i in far_out]
    raw = set(i if i >= 0 else len(args) - 1 - i for i in raw)
    far = list(far_in) + far_out
    count = len(args) + len(out_shape)
    every = list(args) + list(out_shape)
    anywhere = pl.BlockSpec(memory_space=pl.ANY)

    def spec(i):
        if i in far or i in raw:
            return anywhere
        dims = every[i].shape
        rest = (0,) * len(dims)
        return pl.BlockSpec(tuple(dims), lambda *_: rest)

    def whole_kernel(*refs):
        refs = list(refs[: len(args)]) + list(refs[len(args) + len(after) :])
        sems = refs.pop() if far else None
        buffers = [refs.pop() for _ in far][::-1]
        fars = {}
        for at, i in enumerate(far):
            fars[i] = refs[i] = Far(refs[i], buffers[at], sems.at[at], i < len(args))
        kernel(*refs)
        for value in fars.values():
            value.wait()

    moved = sum(math.prod(a.shape) * np.dtype(a.dtype).itemsize for a in every)
    fixed = [pltpu.with_memory_space_constraint(a, pltpu.HBM) if i in far and i not in loose else a for i, a in enumerate(args)]
    shapes = [
        pltpu.HBM(a.shape, a.dtype) if i in far_out or i in raw else a for i, a in enumerate(out_shape, len(args))
    ]
    scratch = list(scratch) + [pltpu.VMEM(every[i].shape, every[i].dtype) for i in far]
    if far:
        scratch.append(pltpu.SemaphoreType.DMA((len(far),)))
    return pl.pallas_call(
        whole_kernel,
        out_shape=shapes,
        grid_spec=pltpu.PrefetchScalarGridSpec(
            num_scalar_prefetch=prefetch,
            grid=(1,),
            in_specs=[spec(i) for i in range(prefetch, len(args))] + [anywhere] * len(after),
            out_specs=[spec(i) for i in range(len(args), count)],
            scratch_shapes=scratch,
        ),
        compiler_params=pltpu.CompilerParams(
            dimension_semantics=("arbitrary",), vmem_limit_bytes=vmem << 20
        ),
        cost_estimate=pl.CostEstimate(flops=int(flops), bytes_accessed=int(moved), transcendentals=0),
    )(*fixed, *after)


def shape(dims, dtype):
    return jax.ShapeDtypeStruct(tuple(dims), dtype)


def stay(operand):
    return pltpu.with_memory_space_constraint(operand, pltpu.HBM)


def pair_swap(operand, axis_name, bit):
    size = lax.axis_size(axis_name)
    return lax.ppermute(operand, axis_name, [(i, i ^ bit) for i in range(size)])


def axis_bits(axis_name):
    size = lax.axis_size(axis_name)
    return [1 << i for i in range(size.bit_length() - 1)]


def body(
    tokens,
    boxes,
    patch_mask,
    pre_gain,
    pre_shift,
    filter_inner,
    filter_inner_bias,
    filter_outer,
    filter_outer_bias,
    post_gain,
    post_shift,
    expand_weight,
    expand_bias,
    reduce_weight,
    reduce_bias,
    cotangent,
):
    micro_count, crop_count, lat_rows, cells, width = tokens.shape
    groups = lax.axis_size("lat")
    lat_count = lat_rows * groups
    block_count, block_size = filter_inner.shape[1:3]
    sub = groups // block_count
    modes_own = MODES // sub
    crops = micro_count * crop_count
    items = crops * lat_rows
    points = crops * modes_own
    wide = 2 * block_size
    padded = -(-cells // 16) * 16
    rows = items * padded
    chunk = 16
    hidden_width = expand_weight.shape[1]
    dp_size = lax.axis_size("dp")
    lat_index, dp_index = lax.axis_index("lat"), lax.axis_index("dp")
    own_block = lat_index // sub
    tables = {k: jnp.asarray(v) for k, v in make_tables(cells, lat_count, block_size, chunk).items()}

    box = stay(boxes)
    own_row = (lat_index * lat_rows).astype(jnp.int32).reshape(1)
    core = dp_index % 2
    token_items = tokens.reshape(items, cells, width)
    cot_pad = jnp.pad(cotangent.reshape(items, cells, width), ((0, 0), (0, padded - cells), (0, 0)))
    holes = patch_mask.reshape(items, 1, cells)
    row_item = (items, cells, width)
    pad_item = (items, padded, width)
    packed = modes_own * 3 // 2
    mode_dims = (groups, items, packed, 128)
    names = (lat_rows, block_size, sub)
    lon_flops = 2 * items * 2 * MODES * cells * width

    def exchange(both, by_rows):
        if by_rows:
            both = both.reshape(groups, crops, lat_rows, packed, 128).swapaxes(1, 2)
            both = both.reshape(groups, items * packed, 128)
            both = lax.all_to_all(both, "lat", 0, 0, tiled=True)
            return both.reshape(lat_count, crops, packed, 128)
        both = both.reshape(groups, items * packed, 128)
        both = lax.all_to_all(both, "lat", 0, 0, tiled=True)
        both = both.reshape(groups, lat_rows, crops, packed, 128).swapaxes(1, 2)
        return both.reshape(mode_dims)

    def own_matrix(matrix):
        pair = lax.dynamic_index_in_dim(matrix, own_block, 1, keepdims=False)
        top = jnp.concatenate([pair[0], pair[1]], axis=1)
        under = jnp.concatenate([-pair[1], pair[0]], axis=1)
        return jnp.concatenate([top, under], axis=0)

    def own_bias(bias):
        return lax.dynamic_index_in_dim(bias, own_block, 1, keepdims=False).reshape(1, wide)

    args = (box, own_row, token_items, holes, pre_gain, pre_shift, tables["fwd"])
    (send,) = call(
        functools.partial(pre_kernel, *names),
        [shape(mode_dims, bf16)],
        args,
        prefetch=2,
        far_in=range(3, 7),
        flops=lon_flops,
    )
    recv = exchange(send, True)
    cot_other = pair_swap(cot_pad.reshape(rows, width), "dp", 1)

    spectrum = (lat_count, points, wide)
    grid_dims = (lat_count, crops, packed, 128)
    filter_flops = 4 * lat_count * points * wide * wide
    inner, outer = own_matrix(filter_inner), own_matrix(filter_outer)
    turns = (tables["turn_fwd"], tables["turn_inv"], tables["swap"])
    args = (recv, inner, own_bias(filter_inner_bias), outer, own_bias(filter_outer_bias), *turns)
    send, spec, hid, slope, shrunk = call(
        functools.partial(filter_kernel, chunk),
        [shape(grid_dims, bf16)] + [shape(spectrum, t) for t in (bf16, bf16, f32, f32)],
        args,
        far_in=(5, 6, 7),
        far_out=(1,),
        raw=(-3, -4, -5),
        scratch=[pltpu.VMEM(spectrum, t) for t in (bf16, f32, f32, bf16, bf16)]
        + [pltpu.SemaphoreType.DMA((lat_count, 3))],
        flops=filter_flops,
    )
    recv = exchange(send, False)

    args = (
        box, own_row, recv, token_items, holes, pre_gain, pre_shift, post_gain, post_shift, tables["inv_t"],
    )
    mixed, post = call(
        functools.partial(mix_kernel, *names),
        [shape(row_item, f32), shape(pad_item, bf16)],
        args,
        prefetch=2,
        far_in=range(4, 10),
        flops=lon_flops,
    )
    post = post.reshape(rows, width)
    post_other = pair_swap(post, "dp", 1)

    dp_bits = [("dp", b) for b in axis_bits("dp")[1:]]
    lat_bits = [("lat", b) for b in axis_bits("lat")]
    bit_names = dp_bits[::-1] + lat_bits[::-1]
    own_bits = jnp.stack([(lax.axis_index(n) // b) % 2 for n, b in bit_names]).astype(jnp.int32)
    own_rows = hidden_width // (dp_size * groups)
    half = hidden_width // 2
    run = hidden_width // dp_size
    runs = dp_size // 2
    core_bit = core.astype(jnp.int32).reshape(1)

    whole_rows = [n for n in lat_bits if own_rows * n[1] % 16 == 0]
    orders = [
        dp_bits + lat_bits,
        whole_rows[:1] + [n for n in lat_bits[:-1] if n != whole_rows[0]] + dp_bits + lat_bits[-1:],
        whole_rows[1:2] + dp_bits + [n for n in lat_bits if n != whole_rows[1]],
    ]
    lefts = [list(bit_names) for _ in orders]

    def place_of(step, left):
        return bit_names.index(step), 2 ** left.index(step)

    third = width // 3
    shares = ((third * 3 // 2, third, third // 2), (third,) * 3)
    lanes = [a + b for a, b in zip(*shares)]
    flat, double = (rows, width), (2 * rows, width)
    cuts = [place_of(order[0], left) for order, left in zip(orders, lefts)]
    copy_count = sum(4 * outer for _, outer in cuts)
    args = (
        own_bits, core_bit, post, post_other, stay(cot_pad.reshape(rows, width)), cot_other,
        stay(expand_weight), stay(reduce_weight), expand_bias.reshape(1, hidden_width),
    )
    *parts, grad_b, out_own, grad_own, out_other, grad_other = call(
        functools.partial(feed_kernel, cuts, shares, runs, run),
        [shape((half // 2, n), bf16) for n in lanes for _ in range(2)]
        + [shape((1, half), f32), shape(flat, f32), shape(flat, f32), shape(flat, bf16), shape(flat, bf16)],
        args,
        prefetch=2,
        far_in=(8,),
        far_out=(6, 7, 8),
        raw=tuple(range(2, 8)) + tuple(range(-1, -7, -1)),
        scratch=[pltpu.VMEM(double, bf16)] * 2
        + [pltpu.VMEM((width, half), bf16), pltpu.VMEM((half, width), bf16)]
        + [pltpu.VMEM((2 * rows, half), bf16)] * 2
        + [pltpu.VMEM((half, width), bf16)] * 2
        + [pltpu.SemaphoreType.DMA((4,)), pltpu.SemaphoreType.DMA((2, runs))]
        + [pltpu.SemaphoreType.DMA((copy_count,))],
        flops=6 * 2 * 2 * rows * width * half,
        vmem=52,
    )
    grad_other = pair_swap(grad_other, "dp", 1).reshape(pad_item)
    out_other = pair_swap(out_other, "dp", 1).reshape(pad_item)

    class Scatter:
        def __init__(self):
            self.at, self.sends, self.keeps = 0, list(parts[0::2]), list(parts[1::2])

        def swap(self):
            self.recvs = []
            for send, order, left in zip(self.sends, orders, lefts):
                left.remove(order[self.at])
                self.recvs.append(pair_swap(send, *order[self.at]))
            self.at += 1
            return list(self.recvs)

        def add(self, after=(), flops=0):
            cuts = [place_of(order[self.at], left) for order, left in zip(orders, lefts)]
            left_rows = self.keeps[0].shape[0]
            dims = [(outer, 2, left_rows // (2 * outer), n) for (_, outer), n in zip(cuts, lanes)]
            ins = [v.reshape(d) for keep, recv, d in zip(self.keeps, self.recvs, dims) for v in (keep, recv)]
            outs = call(
                functools.partial(combine_kernel, [place for place, _ in cuts]),
                [shape((d[0], d[2], d[3]), bf16) for d in dims for _ in range(2)],
                (own_bits, *ins),
                prefetch=1,
                far_in=range(1, 7),
                loose=(2, 4, 6),
                far_out=range(6),
                after=after,
                flops=flops,
            )
            outs = [v.reshape(left_rows // 2, v.shape[-1]) for v in outs]
            self.sends, self.keeps = outs[0::2], outs[1::2]
            return outs

    scatter = Scatter()
    scatter.swap()

    args = (
        box, own_row, mixed, grad_own.reshape(pad_item), grad_other, cot_pad, holes, post_gain, tables["inv"],
    )
    grad_mixed, send, post_sums = call(
        functools.partial(post_kernel, *names),
        [shape(row_item, f32), shape(mode_dims, bf16), shape((3, width), f32)],
        args,
        prefetch=2,
        far_in=(3, 5, 7, 8, 6),
        raw=(-1,),
        scratch=[pltpu.VMEM(row_item, f32), pltpu.SemaphoreType.DMA((items,))],
        flops=lon_flops,
    )
    (result,) = call(
        result_kernel,
        [shape((cells, items, width), bf16)],
        (mixed, out_own.reshape(pad_item), out_other, reduce_bias),
        far_in=(1, 3),
        after=(send,),
    )
    recv = exchange(send, True)

    sums = scatter.add((send,), flops=COMBINE_FLOPS)
    scatter.swap()

    bias_row = 3 * width // 128 + hidden_width // 128
    small_rows = -(-(bias_row + 4 * block_count) // 32) * 32
    small_dims = (small_rows, 128)
    (small,) = call(
        functools.partial(small_kernel, (run // 128, runs, block_count)),
        [shape(small_dims, f32)],
        (core_bit, post_sums, grad_b),
        prefetch=1,
    )
    base = block_size * 3 // 2
    y_index = (dp_index // 2) % 2
    places = jnp.stack([core, own_block, y_index]).astype(jnp.int32)
    args = (recv, slope, shrunk, inner, outer, *turns)
    send, grad_mid, grad_pre, filter_bias = call(
        functools.partial(filter_back_kernel, chunk),
        [shape(grid_dims, bf16), shape(spectrum, bf16), shape(spectrum, bf16), shape((2, wide), f32)],
        args,
        far_in=(5, 7, 2, 1, 6),
        far_out=(1, 2),
        scratch=[pltpu.VMEM(spectrum, bf16)] * 2,
        flops=2 * filter_flops,
        after=[stay(v) for v in sums[:1]],
    )
    recv = exchange(send, False)

    halves = len(dp_bits) > 0
    packed_weight = (base + small_rows // 2, 128)
    send_core, keep_core = call(
        functools.partial(filter_weight_kernel, bias_row, block_count),
        [shape(packed_weight, f32)] * 2,
        (places, spec, hid, grad_mid, grad_pre, filter_bias, small),
        prefetch=1,
        far_in=(1, 4, 2, 3),
        scratch=[pltpu.VMEM(small_dims, f32)],
        after=(scatter.recvs[2],),
    )
    weight = [keep_core, pair_swap(send_core, "dp", 1)]
    sums = scatter.add((send, keep_core), flops=COMBINE_FLOPS)
    ahead = scatter.swap()
    own_base, own_small = base, small_rows // 2
    if halves:
        own_base, own_small = base // 2, small_rows // 4
        send_y, keep_y = call(
            functools.partial(halve_kernel, base),
            [shape((own_base + own_small, 128), f32)] * 2,
            (places, *weight),
            prefetch=1,
            after=[stay(sums[0])],
        )
        weight = [keep_y, pair_swap(send_y, *dp_bits[0])]
    for step in dp_bits[1:] + [n for n in lat_bits if n[1] < sub]:
        weight = [weight[0] + weight[1]]
        weight.append(pair_swap(weight[0], *step))
    pre_rows = -(-2 * width // 2048) * 16
    tail_dims = (groups, -(-(own_base + own_small + pre_rows) // 16) * 16, 128)
    (tail_send,) = call(
        functools.partial(last_sums_kernel, *names, own_base),
        [shape(tail_dims, bf16)],
        (box, own_row, recv, token_items, grad_mixed, holes, tables["fwd_t"], *weight),
        prefetch=2,
        far_in=(6, 5, 4),
        far_out=(0,),
        flops=lon_flops,
    )
    result_dims = (items, cells, 1, width)
    (grad_tokens,) = call(
        functools.partial(last_kernel, *names),
        [shape(result_dims, f32)],
        (box, own_row, recv, token_items, grad_mixed, holes, pre_gain, tables["fwd_t"]),
        prefetch=2,
        far_in=(7, 5, 4, 6),
        raw=(-1,),
        scratch=[pltpu.VMEM(result_dims, f32), pltpu.SemaphoreType.DMA((items,))],
        flops=lon_flops,
        after=(stay(tail_send),),
    )
    tail = tail_send
    tail = lax.all_to_all(tail, "lat", 0, 0, tiled=True)

    while scatter.at < len(bit_names):
        sums = scatter.add((stay(tail_send),), flops=COMBINE_FLOPS)
        scatter.swap()
    merged = [v for pair in zip(scatter.keeps, scatter.recvs) for v in pair]
    expand_part, reduce_part = call(
        functools.partial(shard_kernel, shares),
        [shape((own_rows, width), f32)] * 2,
        merged,
        far_in=range(6),
        loose=(1, 3, 5),
                flops=COMBINE_FLOPS,
        after=(result, stay(grad_tokens), tail),
    )
    expand_part = expand_part.T
    extra = [n[1] for n in dp_bits[1:]]
    masks = [sum(b for i, b in enumerate(extra) if m >> i & 1) for m in range(1, 2 ** len(extra))]
    others = [pair_swap(tail[:, own_base + own_small : own_base + own_small + pre_rows], "dp", m) for m in masks]
    third_dims = (block_count * own_base + 2 * own_small + 2 * pre_rows, 128)
    (third,) = call(
        functools.partial(third_kernel, sub, own_base, own_small, pre_rows),
        [shape(third_dims, bf16)],
        (tail, *others),
        after=(stay(sums[0]),),
    )
    thirds = [third]
    if halves:
        thirds.append(pair_swap(third, *dp_bits[0]))
    (gate,) = call(
        gate_kernel,
        [shape((8, 128), f32)],
        (places,),
        prefetch=1,
        flops=COMBINE_FLOPS,
        after=scatter.recvs,
    )
    (last,) = call(
        pass_kernel,
        [shape(third_dims, bf16)],
        thirds[-1:],
        after=(gate,),
    )
    thirds += [pair_swap(v, "dp", 1) for v in thirds[:-1] + [last]]

    args = (places, *thirds)
    line_dims = (width,)
    filter_dims, bias_dims = filter_inner.shape, filter_inner_bias.shape
    out_dims = [line_dims, line_dims, filter_dims, bias_dims, filter_dims, bias_dims]
    out_dims += [line_dims, line_dims, (hidden_width,), line_dims]
    sums = call(
        functools.partial(tail_kernel, len(thirds), own_small, pre_rows),
        [shape(d, f32) for d in out_dims],
        args,
        prefetch=1,
        scratch=[pltpu.VMEM(small_dims, f32)],
    )
    return (
        result.swapaxes(0, 1).reshape(tokens.shape),
        grad_tokens.reshape(tokens.shape),
        *sums[:8],
        expand_part,
        sums[8],
        reduce_part,
        sums[9],
    )


def solution(mesh):
    rows = P(None, "dp", "lat", None, None)
    in_specs = (rows, P(None, "dp", None), P(None, "dp", "lat", None)) + (P(),) * 12 + (rows,)
    out_specs = (
        (rows, rows)
        + (P(),) * 8
        + (P(None, ("dp", "lat")), P(), P(("dp", "lat"), None), P())
    )
    return jax.shard_map(body, mesh=mesh, in_specs=in_specs, out_specs=out_specs, check_vma=False)
```
